32 devices in a mesh: sx: 8 (over z, core), sy: 4 (over y, x).
Axes of the slice: x: 2, y: 2, z: 4, core: 2. Of those that a mesh axis runs over, the one named last changes fastest.
Arguments:
- weights: float32 [8, 16, 32, 16, 128], P(None, None, 'sx', 'sy'), may hold values from -0.6 to 0.6
Outputs:
- outgoing: float32 [2, 64, 2, 128, 2, 1, 128], P(None, 'sx', None, 'sy')
The draws below stay inside these ranges and needn't reach their ends.
All inputs are finite; a program needn't handle non-finite values.
Results may differ from the reference program's by a relative error of at most 0.0075.
Values sent between devices are 32-bit elements; how exact they have to be, the bound alone decides.
No kernel may reach another device: no remote copies, remote signals or barrier semaphores. Data moves between devices by JAX's collectives and lax.ppermute only.
A program may use at most 64 MiB of HBM per device.

```python
import math
import jax
import jax.numpy as jnp
from jax import lax

RANK = 64
GRID = 4096
BOXES = 64
T0X = 8
T0Y = 16
N_SX = 8
N_SY = 4


def block_scale(key, dims, split, least, high):
    def one(dim, shards_of):
        heights = jax.random.uniform(jax.random.fold_in(jax.random.fold_in(key, 6), dim), (shards_of,), jnp.float32, least / len(split), high / len(split))
        return jnp.repeat(jnp.exp(heights), dims[dim] // shards_of).reshape((-1,) + (1,) * (len(dims) - dim - 1))

    gain = one(*split[0])
    for cut in split[1:]:
        gain = gain * one(*cut)
    return gain


def bell_draw(rng, extent, scale, limit, shards=(), kind=jnp.bfloat16):
    values = jax.random.normal(rng, extent, jnp.float32) * scale
    if len(shards) > 0:
        values = block_scale(rng, extent, shards, -0.22, 0.18) * values
    return jnp.clip(values, min=-limit, max=limit).astype(kind)


def setup_inputs(seed: int = 0) -> dict:
    key_list = jax.random.split(jax.random.key(seed), 2)
    weights = bell_draw(key_list[0], (T0X, T0Y, 4 * N_SX, 4 * N_SY, 2 * RANK), 0.1, 0.6, ((2, 8), (3, 4)), jnp.float32)
    return {"weights": weights}


two_pi = 2.0 * math.pi

def chebyshev_nodes():
    counter = jnp.arange(8, dtype=jnp.float32)
    return 0.5 - 0.5 * jnp.cos(math.pi * (2.0 * counter + 1.0) / 16.0)

def lagrange_child(points, child_side):
    shifted = (child_side + points) / 2.0
    numerator = shifted[None, :, None] - points[None, None, :]
    denominator = points[:, None] - points[None, :]
    diagonal_mask = jnp.eye(8, dtype=bool)
    numerator = jnp.where(diagonal_mask[:, None, :], 1.0, numerator)
    denominator = jnp.where(diagonal_mask, 1.0, denominator)
    return jnp.prod(numerator / denominator[:, None, :], axis=2)

def child_blocks():
    points = chebyshev_nodes()
    stacked = []
    for side_x in range(2):
        for side_y in range(2):
            kernel = jnp.kron(lagrange_child(points, side_x), lagrange_child(points, side_y))
            transposed = kernel.T
            zero_block = jnp.zeros((64, 64), jnp.float32)
            stacked.append(jnp.block([[transposed, zero_block], [zero_block, transposed]]))
    return jnp.concatenate(stacked, axis=0)

def centers(first_box, how_many, boxes_all):
    return ((first_box + jnp.arange(how_many, dtype=jnp.int32)).astype(jnp.float32) + 0.5) / boxes_all

def box_points(first_box, how_many, boxes_all, points):
    anchor = (first_box + jnp.arange(how_many, dtype=jnp.int32)).astype(jnp.float32)
    return (anchor[:, None] + points[None, :]) / boxes_all

def phase_of(x_centers, y_centers, points_x, points_y):
    coord_x = x_centers[:, None, None, None, None, None]
    coord_y = y_centers[None, :, None, None, None, None]
    freq_x = points_x[None, None, :, None, :, None]
    freq_y = points_y[None, None, None, :, None, :]
    speed_map = (2.0 + jnp.sin(two_pi * coord_x) * jnp.sin(two_pi * coord_y)) / 3.0
    cycles = GRID * (coord_x * freq_x + coord_y * freq_y + speed_map * jnp.sqrt(freq_x * freq_x + freq_y * freq_y))
    angles = two_pi * (cycles - jnp.floor(cycles))
    return angles.reshape(x_centers.shape[0], y_centers.shape[0], points_x.shape[0], points_y.shape[0], 64)

def rotate(values, angles):
    cosine = jnp.cos(angles)
    sine_part = jnp.sin(angles)
    real_part = values[..., :64]
    imag_part = values[..., 64:]
    return jnp.concatenate([cosine * real_part - sine_part * imag_part, sine_part * real_part + cosine * imag_part], axis=-1)

def advance(widened, x_centers, y_centers, child_px, child_py, parent_px, parent_py, child_mix):
    turned = rotate(widened, -phase_of(x_centers, y_centers, child_px, child_py))
    dims_now = turned.shape
    boxes_x = dims_now[2] // 2
    boxes_y = dims_now[3] // 2
    grouped = turned.reshape(dims_now[0], dims_now[1], boxes_x, 2, boxes_y, 2, 128)
    grouped = grouped.transpose(0, 1, 2, 4, 3, 5, 6).reshape(dims_now[0], dims_now[1], boxes_x, boxes_y, 512)
    combined = jnp.dot(grouped, child_mix, precision=lax.Precision.HIGHEST, preferred_element_type=jnp.float32)
    return rotate(combined, phase_of(x_centers, y_centers, parent_px, parent_py))

def level_step(parent, child_mix, points, level_index):
    rows_new = 2 * parent.shape[0]
    cols_new = 2 * parent.shape[1]
    boxes_x = parent.shape[2]
    boxes_y = parent.shape[3]
    target_all = GRID // BOXES * 2 ** (level_index + 1)
    child_all = BOXES // 2 ** level_index
    parent_all = child_all // 2
    y_centers = centers(0, cols_new, target_all)
    child_px = box_points(0, boxes_x, child_all, points)
    child_py = box_points(0, boxes_y, child_all, points)
    parent_px = box_points(0, boxes_x // 2, parent_all, points)
    parent_py = box_points(0, boxes_y // 2, parent_all, points)

    def one_row(row_index):
        x_center = ((row_index.astype(jnp.float32) + 0.5) / target_all).reshape(1)
        parent_row = lax.dynamic_index_in_dim(parent, row_index // 2, 0, keepdims=False)
        widened = jnp.repeat(parent_row, 2, axis=0)[None]
        return advance(widened, x_center, y_centers, child_px, child_py, parent_px, parent_py, child_mix)[0]
    return lax.map(one_row, jnp.arange(rows_new, dtype=jnp.int32))

def reference(weights):
    child_mix = child_blocks()
    points = chebyshev_nodes()
    current = weights
    for level_index in range(4):
        current = level_step(current, child_mix, points, level_index)
    rows_all = current.shape[0]
    cols_all = current.shape[1]
    return current.reshape(2, rows_all // 2, 2, cols_all // 2, current.shape[2], current.shape[3], 128)
```

```python
import functools

import jax
import jax.numpy as jnp
import ml_dtypes
import numpy as np
from jax import lax
from jax.experimental import pallas as pl
from jax.experimental.pallas import tpu as pltpu
from jax.sharding import PartitionSpec as P

GRID = 4096
BOXES = 64

COS = (0.9999991998413439, -19.738978175861412, 64.92858783993668,
       -85.27084362693975, 58.78694076314819, -21.065429407708887)
SIN = (6.283184911827355, -41.3415883021802, 81.59991361943699,
       -76.61414030097438, 41.34136538557779, -12.468818618521846)

NODES = 0.5 - 0.5 * np.cos(np.pi * (2.0 * np.arange(8) + 1.0) / 16.0)


def mixing():
    def side(c):
        shifted = (c + NODES) / 2.0
        out = np.ones((8, 8))
        for i in range(8):
            for k in range(8):
                if k != i:
                    out[i] *= (shifted - NODES[k]) / (NODES[i] - NODES[k])
        return out

    rows = []
    for cx in range(2):
        for cy in range(2):
            rows.append(np.kron(np.eye(2), np.kron(side(cx), side(cy)).T))
    full = np.concatenate(rows, axis=0)
    high = full.astype(ml_dtypes.bfloat16)
    low = (full - high.astype(np.float64)).astype(ml_dtypes.bfloat16)
    return np.concatenate([high, low], axis=1)


def horner(coefs, z):
    total = coefs[-1] * z + coefs[-2]
    for c in coefs[-3::-1]:
        total = total * z + c
    return total


def sincos(cycles):
    f = cycles - jnp.round(cycles)
    z = f * f
    return f * horner(SIN, z), horner(COS, z)


def sine(cycles):
    f = cycles - jnp.round(cycles)
    return f * horner(SIN, f * f)


def iotas():
    lane = lax.broadcasted_iota(jnp.int32, (8, 128), 1)
    row = lax.broadcasted_iota(jnp.int32, (8, 128), 0)
    return lane, row


def lane_nodes(lane):
    j1 = (lane >> 3) & 7
    j2 = lane & 7
    z1 = jnp.zeros((8, 128), jnp.float32)
    z2 = jnp.zeros((8, 128), jnp.float32)
    for j in range(8):
        z1 = jnp.where(j1 == j, float(NODES[j]), z1)
        z2 = jnp.where(j2 == j, float(NODES[j]), z2)
    return z1, z2


def doubled(value, low_half):
    other = pltpu.roll(value, 64, 1)
    return jnp.where(low_half, value, other), jnp.where(low_half, other, value)


def halves(real, imag):
    both = jnp.concatenate([real, imag], axis=0)
    high = both.astype(jnp.bfloat16)
    return high, (both - high.astype(jnp.float32)).astype(jnp.bfloat16)


def contract(high_ref, low_ref, mix):
    first = jnp.dot(high_ref[...], mix, preferred_element_type=jnp.float32)
    second = jnp.dot(low_ref[...], mix[:, :128], preferred_element_type=jnp.float32)
    return first[:, :128] + first[:, 128:] + second


def turn_back(real, imag, cycles):
    s, c = sincos(cycles)
    return real * c + imag * s, imag * c - real * s


def source_kernel(w_ref, mix_ref, out_ref, amp0, amp1, q_tab, sh, sl, z1_ref):
    a_mid = pl.program_id(0)
    lane, row = iotas()
    low_half = lane < 64
    upper = (lane >> 6) & 1
    pos_x = lax.axis_index("sx")
    pos_y = lax.axis_index("sy")

    @pl.when(a_mid == 0)
    def _():
        z1, z2 = lane_nodes(lane)
        for m in range(4):
            q_tab[m] = (4 * pos_x + m).astype(jnp.float32) + z1
            q_tab[4 + m] = (4 * pos_y + m).astype(jnp.float32) + z2
        for m in range(4):
            for n in range(4):
                amp0[4 * m + n] = 64.0 * jnp.sqrt(q_tab[m] * q_tab[m] + q_tab[4 + n] * q_tab[4 + n])
        sign = jnp.where(low_half, -0.25, 0.25)
        for m in range(2):
            qx = (2 * pos_x + m).astype(jnp.float32) + z1
            q_tab[8 + m] = 0.25 * qx
            for n in range(2):
                qy = (2 * pos_y + n).astype(jnp.float32) + z2
                q_tab[10 + n] = sign * qy
                amp1[2 * m + n] = 128.0 * jnp.sqrt(qx * qx + qy * qy)

    hx = row >> 2
    hy = (row >> 1) & 1
    third = row & 1
    rows0 = hx * 4 + a_mid
    w = w_ref.reshape(8 * 4 * 16, 128)

    def base_column(jb):
        return hy * 8 + jb * 2 + third

    def center(index, total):
        return (index.astype(jnp.float32) + 0.5) * (1.0 / total)

    def level_one(jb, carry):
        columns = base_column(jb) * 2 + upper
        s_y = sine(center(columns, 128))
        shift_y = []
        for n in range(4):
            v = (columns.astype(jnp.float32) + 0.5) * 0.5 * q_tab[4 + n]
            shift_y.append(v - jnp.round(v))
        for s1 in range(2):
            rows = rows0 * 2 + s1
            s_x = sine(center(rows, 128))
            speed = (2.0 + s_x * s_y) * (1.0 / 3.0)
            shift_x = []
            for m in range(4):
                v = (rows.astype(jnp.float32) + 0.5) * 0.5 * q_tab[m]
                shift_x.append(v - jnp.round(v))
            for m in range(4):
                for n in range(4):
                    value = w_ref_load(w, jb, 4 * m + n)
                    other = pltpu.roll(value, 64, 1)
                    real = jnp.where(low_half, value, other)
                    imag = jnp.where(low_half, other, value)
                    cycles = speed * amp0[4 * m + n] + (shift_x[m] + shift_y[n])
                    ure, uim = turn_back(real, imag, cycles)
                    high, low = halves(ure, uim)
                    tile = (s1 * 2 + m // 2) * 2 + n // 2
                    start = pl.multiple_of(jb * 128 + tile * 16, 16)
                    col = (2 * (m % 2) + n % 2) * 128
                    sh[pl.ds(start, 16), col:col + 128] = high
                    sl[pl.ds(start, 16), col:col + 128] = low
        return carry

    def w_ref_load(flat, jb, box):
        parts = [
            flat[pl.ds(((g * 4 + jb) * 2) * 16 + box, 2, stride=16), :] for g in range(4)
        ]
        return jnp.concatenate(parts, axis=0)

    lax.fori_loop(0, 4, level_one, 0)
    z1_ref[...] = contract(sh, sl, mix_ref[...])

    def level_two(jb, carry):
        columns = base_column(jb) * 2
        for s1 in range(2):
            rows = rows0 * 2 + s1
            s_x = sine(center(rows, 128))
            child_x = [sine(center(rows * 2 + t1, 256)) for t1 in range(2)]
            for s2 in range(2):
                s_y = sine(center(columns + s2, 128))
                child_y = sine(center((columns + s2) * 2 + upper, 256))
                for t1 in range(2):
                    change = (child_x[t1] * child_y - s_x * s_y) * (1.0 / 3.0)
                    tile = ((s1 * 4 + jb) * 2 + t1) * 2 + s2
                    start = pl.multiple_of(tile * 16, 16)
                    for c in range(4):
                        source = pl.multiple_of(jb * 128 + (s1 * 4 + c) * 16, 16)
                        real = doubled(z1_ref[pl.ds(source, 8), :], low_half)[s2]
                        imag = doubled(z1_ref[pl.ds(source + 8, 8), :], low_half)[s2]
                        linear = q_tab[10 + c % 2] + (2 * t1 - 1) * q_tab[8 + c // 2]
                        cycles = change * amp1[c] + linear
                        ure, uim = turn_back(real, imag, cycles)
                        high, low = halves(ure, uim)
                        sh[pl.ds(start, 16), c * 128:(c + 1) * 128] = high
                        sl[pl.ds(start, 16), c * 128:(c + 1) * 128] = low
        return carry

    lax.fori_loop(0, 4, level_two, 0)
    out_ref[...] = contract(sh, sl, mix_ref[...])


def source_side(weights, mix):
    pieces = weights.reshape(2, 4, 2, 4, 2, 16, 128)
    return pl.pallas_call(
        source_kernel,
        grid=(4,),
        in_specs=[
            pl.BlockSpec((2, None, 2, 4, 2, 16, 128), lambda a: (0, a, 0, 0, 0, 0, 0)),
            pl.BlockSpec((512, 256), lambda a: (0, 0)),
        ],
        out_specs=pl.BlockSpec((512, 128), lambda a: (a, 0)),
        out_shape=jax.ShapeDtypeStruct((2048, 128), jnp.float32),
        scratch_shapes=[
            pltpu.VMEM((16, 8, 128), jnp.float32),
            pltpu.VMEM((4, 8, 128), jnp.float32),
            pltpu.VMEM((12, 8, 128), jnp.float32),
            pltpu.VMEM((512, 512), jnp.bfloat16),
            pltpu.VMEM((512, 512), jnp.bfloat16),
            pltpu.VMEM((512, 128), jnp.float32),
        ],
        name="source_levels",
        cost_estimate=pl.CostEstimate(flops=2 * 10**9, bytes_accessed=2 * 2**20, transcendentals=0),
    )(pieces, mix)


def target_kernel(nx, ny, piece_x, piece_y, w_ref, mix_ref, out_ref,
                  amp2, lin2, amp3, lin3, amp4, change4, speed4, sh, sl, z3_ref):
    step = pl.program_id(0)
    gx = step // (piece_y // 4)
    gy = step % (piece_y // 4)
    px, py = nx // 2, ny // 2
    fx, fy = nx // 4, ny // 4
    parents = px * py
    lane, row = iotas()
    low_half = lane < 64
    upper = (lane >> 6) & 1
    pos_x = lax.axis_index("sx")
    pos_y = lax.axis_index("sy")
    sign = jnp.where(low_half, -0.25, 0.25)

    @pl.when(step == 0)
    def _():
        z1, z2 = lane_nodes(lane)

        def tables(count_y, scale, amp, lin):
            def one(box, carry):
                qx = (box // count_y).astype(jnp.float32) + z1
                qy = (box % count_y).astype(jnp.float32) + z2
                amp[box] = scale * jnp.sqrt(qx * qx + qy * qy)
                if lin is not None:
                    lin[2 * box] = sign * qy - 0.25 * qx
                    lin[2 * box + 1] = sign * qy + 0.25 * qx
                return carry

            return one

        lax.fori_loop(0, nx * ny, tables(ny, 256.0, amp2, lin2), 0)
        lax.fori_loop(0, px * py, tables(py, 512.0, amp3, lin3), 0)
        lax.fori_loop(0, fx * fy, tables(fy, 1024.0, amp4, None), 0)

    hx = row >> 2
    hy = (row >> 1) & 1
    third = row & 1
    rows2 = hx * 16 + pos_x * piece_x + gx
    cols2 = hy * 32 + pos_y * piece_y + third * (piece_y // 2) + gy * 2

    def center(index, total):
        return (index.astype(jnp.float32) + 0.5) * (1.0 / total)

    change3 = [None] * 4
    s_x2 = sine(center(rows2, 256))
    x3 = [sine(center(2 * rows2 + a1, 512)) for a1 in range(2)]
    x4 = [[sine(center(4 * rows2 + 2 * a1 + b1, 1024)) for b1 in range(2)] for a1 in range(2)]
    for t2 in range(2):
        s_y2 = sine(center(cols2 + t2, 256))
        y3 = sine(center(2 * (cols2 + t2) + upper, 512))
        for a1 in range(2):
            change3[2 * t2 + a1] = (x3[a1] * y3 - s_x2 * s_y2) * (1.0 / 3.0)
            for a2 in range(2):
                y3_own = sine(center(2 * (cols2 + t2) + a2, 512))
                y4 = sine(center(4 * (cols2 + t2) + 2 * a2 + upper, 1024))
                for b1 in range(2):
                    k = ((t2 * 2 + a1) * 2 + a2) * 2 + b1
                    change4[k] = (x4[a1][b1] * y4 - x3[a1] * y3_own) * (1.0 / 3.0)
                    speed4[k] = (2.0 + x4[a1][b1] * y4) * (1.0 / 3.0)

    def level_three(parent, carry):
        m3 = parent // py
        n3 = parent % py
        for c in range(4):
            box = (2 * m3 + c // 2) * ny + 2 * n3 + c % 2
            reals = doubled(w_ref[box, 0:8, :], low_half)
            imags = doubled(w_ref[box, 8:16, :], low_half)
            amp = amp2[box]
            for a1 in range(2):
                lin = lin2[2 * box + a1]
                for t2 in range(2):
                    cycles = change3[2 * t2 + a1] * amp + lin
                    ure, uim = turn_back(reals[t2], imags[t2], cycles)
                    high, low = halves(ure, uim)
                    start = pl.multiple_of(((2 * t2 + a1) * parents + parent) * 16, 16)
                    sh[pl.ds(start, 16), c * 128:(c + 1) * 128] = high
                    sl[pl.ds(start, 16), c * 128:(c + 1) * 128] = low
        return carry

    lax.fori_loop(0, parents, level_three, 0)
    z3_ref[...] = contract(sh, sl, mix_ref[...])

    def level_four(index, carry):
        last = index % (fx * fy)
        ta = index // (fx * fy)
        m4 = last // fy
        n4 = last % fy
        for c in range(4):
            box = (2 * m4 + c // 2) * py + 2 * n4 + c % 2
            source = pl.multiple_of((ta * parents + box) * 16, 16)
            reals = doubled(z3_ref[pl.ds(source, 8), :], low_half)
            imags = doubled(z3_ref[pl.ds(source + 8, 8), :], low_half)
            amp = amp3[box]
            for b1 in range(2):
                lin = lin3[2 * box + b1]
                for a2 in range(2):
                    cycles = change4[ta * 4 + a2 * 2 + b1] * amp + lin
                    ure, uim = turn_back(reals[a2], imags[a2], cycles)
                    high, low = halves(ure, uim)
                    tile = (ta * 4 + a2 * 2 + b1) * (fx * fy) + last
                    start = pl.multiple_of(tile * 16, 16)
                    sh[pl.ds(start, 16), c * 128:(c + 1) * 128] = high
                    sl[pl.ds(start, 16), c * 128:(c + 1) * 128] = low
        return carry

    lax.fori_loop(0, 4 * fx * fy, level_four, 0)
    z3_ref[...] = contract(sh, sl, mix_ref[...])

    boxes = fx * fy
    out = out_ref.reshape(2 * 4 * 4 * 8 * boxes, 128)
    z1, z2 = lane_nodes(lane)

    def finish(index, carry):
        last = index % boxes
        ta = index // boxes
        t2 = ta // 2
        a1 = ta % 2
        p1 = (last // fy).astype(jnp.float32) + z1
        p2 = (last % fy).astype(jnp.float32) + z2
        amp = amp4[last]
        for a2 in range(2):
            col = (4 * (cols2 + t2) + 2 * a2 + upper).astype(jnp.float32) + 0.5
            for b1 in range(2):
                k = ta * 4 + a2 * 2 + b1
                source = pl.multiple_of((k * boxes + last) * 16, 16)
                real = z3_ref[pl.ds(source, 8), :]
                imag = z3_ref[pl.ds(source + 8, 8), :]
                r4 = (4 * rows2 + 2 * a1 + b1).astype(jnp.float32) + 0.5
                cycles = speed4[k] * amp + (r4 * p1 + col * p2)
                s, c = sincos(cycles)
                ore = real * c - imag * s
                oim = real * s + imag * c
                first = jnp.where(low_half, ore, pltpu.roll(oim, 64, 1))
                second = jnp.where(low_half, pltpu.roll(ore, 64, 1), oim)
                for b2, value in enumerate((first, second)):
                    for h in range(2):
                        at = ((h * 4 + 2 * a1 + b1) * 4 * 8 + (4 * t2 + 2 * a2 + b2)) * boxes + last
                        out[pl.ds(at, 4, stride=8 * boxes), :] = value[4 * h:4 * h + 4]
        return carry

    lax.fori_loop(0, 4 * boxes, finish, 0)


def target_side(arrived, mix, nx, ny, piece_x, piece_y):
    fx, fy = nx // 4, ny // 4
    quarter = piece_y // 4
    steps = piece_x * quarter
    rows = 4 * (nx // 2) * (ny // 2) * 16
    return pl.pallas_call(
        functools.partial(target_kernel, nx, ny, piece_x, piece_y),
        grid=(steps,),
        in_specs=[
            pl.BlockSpec((nx * ny, 16, 128), lambda g: (0, g, 0)),
            pl.BlockSpec((512, 256), lambda g: (0, 0)),
        ],
        out_specs=pl.BlockSpec(
            (2, None, 4, 2, 2, None, 8 * fx * fy, 128),
            lambda g: (0, g // quarter, 0, 0, 0, g % quarter, 0, 0),
        ),
        out_shape=jax.ShapeDtypeStruct(
            (2, piece_x, 4, 2, 2, quarter, 8 * fx * fy, 128), jnp.float32
        ),
        scratch_shapes=[
            pltpu.VMEM((nx * ny, 8, 128), jnp.float32),
            pltpu.VMEM((2 * nx * ny, 8, 128), jnp.float32),
            pltpu.VMEM((nx * ny // 4, 8, 128), jnp.float32),
            pltpu.VMEM((nx * ny // 2, 8, 128), jnp.float32),
            pltpu.VMEM((fx * fy, 8, 128), jnp.float32),
            pltpu.VMEM((16, 8, 128), jnp.float32),
            pltpu.VMEM((16, 8, 128), jnp.float32),
            pltpu.VMEM((rows, 512), jnp.bfloat16),
            pltpu.VMEM((rows, 512), jnp.bfloat16),
            pltpu.VMEM((rows, 128), jnp.float32),
        ],
        name="target_levels",
        cost_estimate=pl.CostEstimate(flops=2 * 10**9, bytes_accessed=2 * 2**20, transcendentals=0),
    )(arrived, mix)


def on_device(weights):
    nx = lax.axis_size("sx")
    ny = lax.axis_size("sy")
    piece_x = 2 * weights.shape[0] // nx
    piece_y = 2 * weights.shape[1] // ny
    mix = jnp.asarray(mixing())
    made = source_side(weights, mix)
    if (piece_x, piece_y) != (2, 8):
        made = made.reshape(8, 4, 2, 2, 2, 4, 2, 128)
        lead = [0] + ([2] if piece_x == 1 else []) + [1] + ([6] if piece_y == 4 else [])
        rest = ([2] if piece_x == 2 else []) + ([3] if piece_y == 8 else []) + [4, 5]
        rest += [6] if piece_y == 8 else [3]
        made = made.transpose(lead + rest + [7])
    made = made.reshape(nx * ny, -1, 128)
    arrived = lax.all_to_all(made, ("sx", "sy"), split_axis=0, concat_axis=0, tiled=True)
    out = target_side(arrived, mix, nx, ny, piece_x, piece_y)
    return out.reshape(2, 4 * piece_x, 2, 4 * piece_y, nx // 4, ny // 4, 128)


def solution(mesh):
    return jax.shard_map(
        on_device,
        mesh=mesh,
        in_specs=(P(None, None, "sx", "sy", None),),
        out_specs=P(None, "sx", None, "sy", None, None, None),
        check_vma=False,
    )
```

```python
import functools

import jax
import jax.numpy as jnp
import ml_dtypes
import numpy as np
from jax import lax
from jax.experimental import pallas as pl
from jax.experimental.pallas import tpu as pltpu
from jax.sharding import PartitionSpec as P

GRID = 4096
BOXES = 64

HALF_SIN = (4.442879586469155, -7.3078180482250685, 3.597788731355218, -0.7912382117199773)
HALF_COS = (1.4142134965649689, -6.978850988233124, 5.739461170564865,
            -1.883562986553834, 0.3106981903146949)

UNROLL = 8

LOW = (True, True, True, True)

NODES = 0.5 - 0.5 * np.cos(np.pi * (2.0 * np.arange(8) + 1.0) / 16.0)


def mixing():
    def side(c):
        shifted = (c + NODES) / 2.0
        out = np.ones((8, 8))
        for i in range(8):
            for k in range(8):
                if k != i:
                    out[i] *= (shifted - NODES[k]) / (NODES[i] - NODES[k])
        return out

    rows = []
    for cx in range(2):
        for cy in range(2):
            rows.append(np.kron(np.eye(2), np.kron(side(cx), side(cy)).T))
    full = np.concatenate(rows, axis=0)
    high = full.astype(ml_dtypes.bfloat16)
    low = (full - high.astype(np.float64)).astype(ml_dtypes.bfloat16)
    return np.concatenate([high, low], axis=1)


def horner(coefs, z):
    total = coefs[-1] * z + coefs[-2]
    for c in coefs[-3::-1]:
        total = total * z + c
    return total


def sincos(cycles):
    f = cycles - jnp.round(cycles)
    z = f * f
    half_sin = f * horner(HALF_SIN, z)
    half_cos = horner(HALF_COS, z)
    return half_sin * half_cos, 1.0 - half_sin * half_sin


def sine(cycles):
    return sincos(cycles)[0]


def iotas():
    lane = lax.broadcasted_iota(jnp.int32, (8, 128), 1)
    row = lax.broadcasted_iota(jnp.int32, (8, 128), 0)
    return lane, row


def lane_nodes(lane):
    j1 = (lane >> 3) & 7
    j2 = lane & 7
    z1 = jnp.zeros((8, 128), jnp.float32)
    z2 = jnp.zeros((8, 128), jnp.float32)
    for j in range(8):
        z1 = jnp.where(j1 == j, float(NODES[j]), z1)
        z2 = jnp.where(j2 == j, float(NODES[j]), z2)
    return z1, z2


def center(index, total):
    return (index.astype(jnp.float32) + 0.5) * (1.0 / total)


def doubled(value, low_half):
    other = pltpu.roll(value, 64, 1)
    return jnp.where(low_half, value, other), jnp.where(low_half, other, value)


def turn_back(real, imag, cycles, buffer, tile, col, low):
    s, c = sincos(cycles)
    both = jnp.concatenate([real * c + imag * s, imag * c - real * s], axis=0)
    high = both.astype(jnp.bfloat16)
    buffer[tile:tile + 16, col:col + 128] = high
    if low:
        rest = both - high.astype(jnp.float32)
        buffer[64 + tile:80 + tile, col:col + 128] = rest.astype(jnp.bfloat16)


def log2(n):
    return n.bit_length() - 1


def staged(count, produce, consume, buffers, mix_ref, low):
    def contracted(buffer):
        rows = buffer[...] if low else buffer[:64, :]
        y = jnp.dot(rows, mix_ref[...], preferred_element_type=jnp.float32)
        total = y[:64, :128] + y[:64, 128:]
        return total + y[64:, :128] if low else total

    produce(jnp.int32(0), buffers[0])

    def body(k, carry):
        for j in range(UNROLL):
            i = k * UNROLL + j
            y = contracted(buffers[j % 2])
            produce(jnp.minimum(i + 1, count - 1), buffers[(j + 1) % 2])
            consume(i, y)
        return carry

    lax.fori_loop(0, count // UNROLL, body, 0)


def source_kernel(w_ref, mix_ref, out_ref, amp0, amp1, q_tab, speed, shift_x, shift_y, change,
                  first, second, z1_ref):
    lane, row = iotas()
    low_half = lane < 64
    upper = (lane >> 6) & 1
    pos_x = lax.axis_index("sx")
    pos_y = lax.axis_index("sy")
    third = 1.0 / 3.0

    z1, z2 = lane_nodes(lane)
    qx0 = [(4 * pos_x + m).astype(jnp.float32) + z1 for m in range(4)]
    qy0 = [(4 * pos_y + n).astype(jnp.float32) + z2 for n in range(4)]
    for m in range(4):
        for n in range(4):
            amp0[4 * m + n] = 64.0 * jnp.sqrt(qx0[m] * qx0[m] + qy0[n] * qy0[n])
    sign = jnp.where(low_half, -0.25, 0.25)
    for m in range(2):
        qx = (2 * pos_x + m).astype(jnp.float32) + z1
        for n in range(2):
            qy = (2 * pos_y + n).astype(jnp.float32) + z2
            amp1[2 * m + n] = 128.0 * jnp.sqrt(qx * qx + qy * qy)
            for t1 in range(2):
                q_tab[2 * (2 * m + n) + t1] = sign * qy + (0.25 * (2 * t1 - 1)) * qx

    hx = row >> 2
    hy = (row >> 1) & 1
    b_low = row & 1
    y_tabs = []
    for jb in range(4):
        column = hy * 8 + jb * 2 + b_low
        both = column * 2 + upper
        for n in range(4):
            v = (both.astype(jnp.float32) + 0.5) * 0.5 * qy0[n]
            shift_y[jb * 4 + n] = v - jnp.round(v)
        own = [sine(center(column * 2 + s2, 128)) for s2 in range(2)]
        child = [sine(center((column * 2 + s2) * 2 + upper, 256)) for s2 in range(2)]
        y_tabs.append((jnp.where(low_half, own[0], own[1]), own, child))

    def tables(i, carry):
        a_mid = i >> 1
        s1 = i & 1
        rows = (hx * 4 + a_mid) * 2 + s1
        s_x = sine(center(rows, 128))
        child_x = [sine(center(rows * 2 + t1, 256)) for t1 in range(2)]
        for m in range(4):
            v = (rows.astype(jnp.float32) + 0.5) * 0.5 * qx0[m]
            shift_x[i * 4 + m] = v - jnp.round(v)
        for jb in range(4):
            both, own, child = y_tabs[jb]
            at = (a_mid * 4 + jb) * 2 + s1
            speed[at] = (2.0 + s_x * both) * third
            for t1 in range(2):
                for s2 in range(2):
                    change[at * 4 + t1 * 2 + s2] = (child_x[t1] * child[s2] - s_x * own[s2]) * third
        return carry

    lax.fori_loop(0, 8, tables, 0)

    def produce_one(i, buffer):
        ajb = i >> 1
        m_half = i & 1
        a_mid = ajb >> 2
        jb = ajb & 3
        for n_half in range(2):
            for cx in range(2):
                m = 2 * m_half + cx
                for cy in range(2):
                    n = 2 * n_half + cy
                    box = 4 * m + n
                    parts = [
                        w_ref[h >> 1, a_mid, h & 1, jb, :, pl.ds(box, 1), :].reshape(2, 128)
                        for h in range(4)
                    ]
                    value = jnp.concatenate(parts, axis=0)
                    other = pltpu.roll(value, 64, 1)
                    real = jnp.where(low_half, value, other)
                    imag = jnp.where(low_half, other, value)
                    amp = amp0[box]
                    for s1 in range(2):
                        shift = shift_x[(a_mid * 2 + s1) * 4 + m] + shift_y[jb * 4 + n]
                        cycles = speed[ajb * 2 + s1] * amp + shift
                        tile = (n_half * 2 + s1) * 16
                        col = (2 * cx + cy) * 128
                        turn_back(real, imag, cycles, buffer, tile, col, LOW[0])

    def consume_one(i, y):
        z1_ref[pl.ds(pl.multiple_of(i * 64, 64), 64), :] = y

    staged(32, produce_one, consume_one, (first, second), mix_ref, LOW[0])

    def produce_two(i, buffer):
        s1 = i & 1
        ajb = i >> 1
        for c in range(4):
            source = pl.multiple_of(((ajb * 4 + c) * 2 + s1) * 16, 16)
            reals = doubled(z1_ref[pl.ds(source, 8), :], low_half)
            imags = doubled(z1_ref[pl.ds(source + 8, 8), :], low_half)
            amp = amp1[c]
            for t1 in range(2):
                lin = q_tab[2 * c + t1]
                for s2 in range(2):
                    cycles = change[i * 4 + t1 * 2 + s2] * amp + lin
                    tile = (t1 * 2 + s2) * 16
                    turn_back(reals[s2], imags[s2], cycles, buffer, tile, c * 128, LOW[1])

    def consume_two(i, y):
        s1 = i & 1
        ajb = i >> 1
        base = pl.multiple_of((((ajb >> 2) * 2 + s1) * 4 + (ajb & 3)) * 64, 64)
        for t1 in range(2):
            for s2 in range(2):
                tile = (t1 * 2 + s2) * 16
                for part in range(2):
                    at = base + (t1 * 32 + part * 16 + s2)
                    out_ref[pl.ds(at, 8, stride=2), :] = y[tile + 8 * part:tile + 8 * part + 8]

    staged(32, produce_two, consume_two, (first, second), mix_ref, LOW[1])


def tab(n):
    return pltpu.VMEM((n, 8, 128), jnp.float32)


def source_side(weights, mix):
    pieces = weights.reshape(2, 4, 2, 4, 2, 16, 128)
    return pl.pallas_call(
        source_kernel,
        in_specs=[pl.BlockSpec(memory_space=pltpu.VMEM)] * 2,
        out_specs=pl.BlockSpec(memory_space=pltpu.VMEM),
        out_shape=jax.ShapeDtypeStruct((2048, 128), jnp.float32),
        scratch_shapes=[
            tab(16), tab(4), tab(8), tab(32), tab(32), tab(16), tab(128),
            pltpu.VMEM((128, 512), jnp.bfloat16),
            pltpu.VMEM((128, 512), jnp.bfloat16),
            pltpu.VMEM((2048, 128), jnp.float32),
        ],
        name="source_levels",
        cost_estimate=pl.CostEstimate(flops=2 * 10**9, bytes_accessed=2 * 2**20, transcendentals=0),
    )(pieces, mix)


def target_kernel(nx, ny, piece_x, piece_y, w_ref, mix_ref, out_ref,
                  amp2, lin2, amp3, lin3, amp4, change3, change4, speed4, first, second, z3_ref):
    px, py = nx // 2, ny // 2
    fx, fy = nx // 4, ny // 4
    parents, boxes = px * py, fx * fy
    wide = piece_y == 8
    groups = piece_x * (2 if wide else 1)
    lane, row = iotas()
    low_half = lane < 64
    upper = (lane >> 6) & 1
    pos_x = lax.axis_index("sx")
    pos_y = lax.axis_index("sy")
    sign = jnp.where(low_half, -0.25, 0.25)
    third = 1.0 / 3.0
    z1, z2 = lane_nodes(lane)

    def box_tables(count_x, count_y, scale, amp, lin):
        qys = [float(n) + z2 for n in range(count_y)]

        def one(m, carry):
            qx = m.astype(jnp.float32) + z1
            for n, qy in enumerate(qys):
                box = m * count_y + n
                amp[box] = scale * jnp.sqrt(qx * qx + qy * qy)
                if lin is not None:
                    lin[2 * box] = sign * qy - 0.25 * qx
                    lin[2 * box + 1] = sign * qy + 0.25 * qx
            return carry

        lax.fori_loop(0, count_x, one, 0)

    box_tables(nx, ny, 256.0, amp2, lin2)
    box_tables(px, py, 512.0, amp3, lin3)
    box_tables(fx, fy, 1024.0, amp4, None)

    if wide:
        hy = row >> 2
        k = row & 3
    else:
        hy = (row >> 1) & 1
        k = row & 1
    cols2 = hy * 32 + pos_y * piece_y + 2 * k

    def rows2(g):
        if wide:
            return jnp.full((8, 128), (g & 1) * 16 + pos_x * piece_x + (g >> 1), jnp.int32)
        return (row >> 2) * 16 + pos_x * piece_x + g

    y_tabs = []
    for t2 in range(2):
        s_y2 = sine(center(cols2 + t2, 256))
        own = [sine(center(2 * (cols2 + t2) + a2, 512)) for a2 in range(2)]
        last = [sine(center(4 * (cols2 + t2) + 2 * a2 + upper, 1024)) for a2 in range(2)]
        y_tabs.append((s_y2, jnp.where(low_half, own[0], own[1]), own, last))

    def target_tables(g, carry):
        rows = rows2(g)
        s_x2 = sine(center(rows, 256))
        for a1 in range(2):
            x3 = sine(center(2 * rows + a1, 512))
            x4 = [sine(center(4 * rows + 2 * a1 + b1, 1024)) for b1 in range(2)]
            for t2 in range(2):
                s_y2, y3, own, last = y_tabs[t2]
                ta = 2 * t2 + a1
                change3[g * 4 + ta] = (x3 * y3 - s_x2 * s_y2) * third
                for a2 in range(2):
                    for b1 in range(2):
                        at = (g * 4 + ta) * 4 + a2 * 2 + b1
                        product = x4[b1] * last[a2]
                        change4[at] = (product - x3 * own[a2]) * third
                        speed4[at] = (2.0 + product) * third
        return carry

    lax.fori_loop(0, groups, target_tables, 0)

    def arrived(box, g, part):
        if wide:
            at = (((g >> 1) * 2 + part) * 2 + (g & 1)) * 8
        else:
            at = (g * 2 + part) * 8
        return w_ref[box, pl.ds(pl.multiple_of(at, 8), 8), :]

    def produce_three(i, buffer):
        g = i >> log2(parents)
        parent = i & (parents - 1)
        m3 = parent >> log2(py)
        n3 = parent & (py - 1)
        for c in range(4):
            box = (2 * m3 + c // 2) * ny + 2 * n3 + c % 2
            reals = doubled(arrived(box, g, 0), low_half)
            imags = doubled(arrived(box, g, 1), low_half)
            amp = amp2[box]
            for a1 in range(2):
                lin = lin2[2 * box + a1]
                for t2 in range(2):
                    ta = 2 * t2 + a1
                    cycles = change3[g * 4 + ta] * amp + lin
                    turn_back(reals[t2], imags[t2], cycles, buffer, ta * 16, c * 128, LOW[2])

    def consume_three(i, y):
        z3_ref[pl.ds(pl.multiple_of(i * 64, 64), 64), :] = y

    staged(groups * parents, produce_three, consume_three, (first, second), mix_ref, LOW[2])

    def decode(i):
        last = i & (boxes - 1)
        gta = i >> log2(boxes)
        return gta >> 2, gta & 3, last

    def produce_four(i, buffer):
        g, ta, last = decode(i)
        m4 = last >> log2(fy)
        n4 = last & (fy - 1)
        for c in range(4):
            box = (2 * m4 + c // 2) * py + 2 * n4 + c % 2
            source = pl.multiple_of(((g * parents + box) * 4 + ta) * 16, 16)
            reals = doubled(z3_ref[pl.ds(source, 8), :], low_half)
            imags = doubled(z3_ref[pl.ds(source + 8, 8), :], low_half)
            amp = amp3[box]
            for b1 in range(2):
                lin = lin3[2 * box + b1]
                for a2 in range(2):
                    tile = a2 * 2 + b1
                    cycles = change4[(g * 4 + ta) * 4 + tile] * amp + lin
                    turn_back(reals[a2], imags[a2], cycles, buffer, tile * 16, c * 128, LOW[3])

    def consume_four(i, y):
        g, ta, last = decode(i)
        t2 = ta >> 1
        a1 = ta & 1
        p1 = (last >> log2(fy)).astype(jnp.float32) + z1
        p2 = (last & (fy - 1)).astype(jnp.float32) + z2
        amp = amp4[last]
        rows = rows2(g) * 4 + 2 * a1
        gx = g >> 1 if wide else g
        for a2 in range(2):
            col = (4 * (cols2 + t2) + 2 * a2 + upper).astype(jnp.float32) + 0.5
            for b1 in range(2):
                tile = a2 * 2 + b1
                real = y[tile * 16:tile * 16 + 8]
                imag = y[tile * 16 + 8:tile * 16 + 16]
                r4 = (rows + b1).astype(jnp.float32) + 0.5
                cycles = speed4[(g * 4 + ta) * 4 + tile] * amp + (r4 * p1 + col * p2)
                s, c = sincos(cycles)
                ore = real * c - imag * s
                oim = real * s + imag * c
                pair = (
                    jnp.where(low_half, ore, pltpu.roll(oim, 64, 1)),
                    jnp.where(low_half, pltpu.roll(ore, 64, 1), oim),
                )
                for b2, value in enumerate(pair):
                    inner = (4 * t2 + 2 * a2 + b2) * boxes + last

                    def at(h):
                        line = (h * piece_x + gx) * 4 + 2 * a1 + b1
                        return line * (piece_y * 8 * boxes) + inner

                    if wide:
                        out_ref[pl.ds(at(g & 1), 8, stride=8 * boxes), :] = value
                    else:
                        for h in range(2):
                            out_ref[pl.ds(at(h), 4, stride=8 * boxes), :] = value[4 * h:4 * h + 4]

    staged(groups * 4 * boxes, produce_four, consume_four, (first, second), mix_ref, LOW[3])


def target_side(arrived, mix, nx, ny, piece_x, piece_y):
    parents, boxes = (nx // 2) * (ny // 2), (nx // 4) * (ny // 4)
    groups = piece_x * (2 if piece_y == 8 else 1)
    return pl.pallas_call(
        functools.partial(target_kernel, nx, ny, piece_x, piece_y),
        in_specs=[pl.BlockSpec(memory_space=pltpu.VMEM)] * 2,
        out_specs=pl.BlockSpec(memory_space=pltpu.VMEM),
        out_shape=jax.ShapeDtypeStruct((2 * 4 * piece_x * 2 * 4 * piece_y * boxes, 128), jnp.float32),
        scratch_shapes=[
            tab(nx * ny), tab(2 * nx * ny), tab(parents), tab(2 * parents), tab(boxes),
            tab(groups * 4), tab(groups * 16), tab(groups * 16),
            pltpu.VMEM((128, 512), jnp.bfloat16),
            pltpu.VMEM((128, 512), jnp.bfloat16),
            pltpu.VMEM((groups * parents * 64, 128), jnp.float32),
        ],
        name="target_levels",
        cost_estimate=pl.CostEstimate(flops=2 * 10**9, bytes_accessed=2 * 2**20, transcendentals=0),
    )(arrived, mix)


def to_targets(made, nx, ny, piece_x, piece_y):
    if (piece_x, piece_y) != (2, 8):
        made = made.reshape(4, 2, 4, 2, 2, 4, 2, 2, 128)
        lead = [0, 1] + ([3] if piece_x == 1 else []) + [2] + ([6] if piece_y == 4 else [])
        rest = ([3] if piece_x == 2 else []) + [4, 5] + ([6] if piece_y == 8 else []) + [7]
        made = made.transpose(lead + rest + [8])
    return made.reshape(nx * ny, -1, 128)


def on_device(weights):
    nx = lax.axis_size("sx")
    ny = lax.axis_size("sy")
    piece_x = 2 * weights.shape[0] // nx
    piece_y = 2 * weights.shape[1] // ny
    mix = jnp.asarray(mixing())
    made = to_targets(source_side(weights, mix), nx, ny, piece_x, piece_y)
    arrived = lax.all_to_all(made, ("sx", "sy"), split_axis=0, concat_axis=0, tiled=True)
    out = target_side(arrived, mix, nx, ny, piece_x, piece_y)
    return out.reshape(2, 4 * piece_x, 2, 4 * piece_y, nx // 4, ny // 4, 128)


def solution(mesh):
    return jax.shard_map(
        on_device,
        mesh=mesh,
        in_specs=(P(None, None, "sx", "sy", None),),
        out_specs=P(None, "sx", None, "sy", None, None, None),
        check_vma=False,
    )
```

```python
import functools

import jax
import jax.numpy as jnp
import ml_dtypes
import numpy as np
from jax import lax
from jax.experimental import pallas as pl
from jax.experimental.pallas import tpu as pltpu
from jax.sharding import PartitionSpec as P

GRID = 4096
BOXES = 64

HALF_SIN = (4.442867279052734, -7.30741548538208, 3.5945212841033936, -0.7836661338806152)

UNROLL = 8

LOW = (True, True, True, True)

NODES = 0.5 - 0.5 * np.cos(np.pi * (2.0 * np.arange(8) + 1.0) / 16.0)


def mixing():
    def side(c):
        shifted = (c + NODES) / 2.0
        out = np.ones((8, 8))
        for i in range(8):
            for k in range(8):
                if k != i:
                    out[i] *= (shifted - NODES[k]) / (NODES[i] - NODES[k])
        return out

    rows = []
    for cx in range(2):
        for cy in range(2):
            rows.append(np.kron(np.eye(2), np.kron(side(cx), side(cy)).T))
    full = np.concatenate(rows, axis=0)
    high = full.astype(ml_dtypes.bfloat16)
    low = (full - high.astype(np.float64)).astype(ml_dtypes.bfloat16)
    return np.concatenate([high, low], axis=1)


def horner(coefs, z):
    total = coefs[-1] * z + coefs[-2]
    for c in coefs[-3::-1]:
        total = total * z + c
    return total


def sincos(cycles):
    f = cycles - jnp.round(cycles)
    h = f * horner(HALF_SIN, f * f)
    w = h * h
    d = 2.0 - w
    return h * d * lax.rsqrt(d), 1.0 - w


def sine(cycles):
    return sincos(cycles)[0]


def iotas():
    lane = lax.broadcasted_iota(jnp.int32, (8, 128), 1)
    row = lax.broadcasted_iota(jnp.int32, (8, 128), 0)
    return lane, row


def lane_nodes(lane):
    j1 = (lane >> 3) & 7
    j2 = lane & 7
    z1 = jnp.zeros((8, 128), jnp.float32)
    z2 = jnp.zeros((8, 128), jnp.float32)
    for j in range(8):
        z1 = jnp.where(j1 == j, float(NODES[j]), z1)
        z2 = jnp.where(j2 == j, float(NODES[j]), z2)
    return z1, z2


def center(index, total):
    return (index.astype(jnp.float32) + 0.5) * (1.0 / total)


def doubled(value, low_half):
    other = pltpu.roll(value, 64, 1)
    return jnp.where(low_half, value, other), jnp.where(low_half, other, value)


def turn_back(real, imag, cycles, tiles, tile, child, low):
    s, c = sincos(cycles)
    both = jnp.concatenate([real * c + imag * s, imag * c - real * s], axis=0)
    high = both.astype(jnp.bfloat16)
    tiles[tile][child] = high
    if low:
        tiles[4 + tile][child] = (both - high.astype(jnp.float32)).astype(jnp.bfloat16)


def fresh(low):
    return [[None] * 4 for _ in range(8 if low else 4)]


def laid(tiles):
    return jnp.concatenate([jnp.concatenate(row, axis=1) for row in tiles], axis=0)


def log2(n):
    return n.bit_length() - 1


def staged(count, produce, consume, mix_ref, low, after=None):
    def contracted(rows):
        y = jnp.dot(rows, mix_ref[...], preferred_element_type=jnp.float32)
        total = y[:64, :128] + y[:64, 128:]
        return total + y[64:, :128] if low else total

    def body(k, rows):
        for j in range(UNROLL):
            i = k * UNROLL + j
            y = contracted(rows)
            rows = produce(jnp.minimum(i + 1, count - 1))
            consume(i, y)
        if after is not None:
            after(k)
        return rows

    lax.fori_loop(0, count // UNROLL, body, produce(jnp.int32(0)))


def source_kernel(w_hbm, mix_hbm, out_hbm, amp0, amp1, q_tab, speed, shift_x, shift_y, change,
                  z1_ref, w_ref, mix_ref, out_ref, in_sem, mix_sem, out_sem):
    fetches = [
        pltpu.make_async_copy(w_hbm.at[:, a, :, b], w_ref.at[4 * a + b], in_sem.at[4 * a + b])
        for a in range(4)
        for b in range(4)
    ]
    fetches.append(pltpu.make_async_copy(mix_hbm, mix_ref, mix_sem))
    for fetch in fetches:
        fetch.start()
    lane, row = iotas()
    low_half = lane < 64
    upper = (lane >> 6) & 1
    pos_x = lax.axis_index("sx")
    pos_y = lax.axis_index("sy")
    third = 1.0 / 3.0

    z1, z2 = lane_nodes(lane)
    qx0 = [(4 * pos_x + m).astype(jnp.float32) + z1 for m in range(4)]
    qy0 = [(4 * pos_y + n).astype(jnp.float32) + z2 for n in range(4)]
    for m in range(4):
        for n in range(4):
            amp0[4 * m + n] = 64.0 * jnp.sqrt(qx0[m] * qx0[m] + qy0[n] * qy0[n])
    sign = jnp.where(low_half, -0.25, 0.25)
    for m in range(2):
        qx = (2 * pos_x + m).astype(jnp.float32) + z1
        for n in range(2):
            qy = (2 * pos_y + n).astype(jnp.float32) + z2
            amp1[2 * m + n] = 128.0 * jnp.sqrt(qx * qx + qy * qy)
            for t1 in range(2):
                q_tab[2 * (2 * m + n) + t1] = sign * qy + (0.25 * (2 * t1 - 1)) * qx

    hx = row >> 2
    hy = (row >> 1) & 1
    b_low = row & 1
    y_tabs = []
    for jb in range(4):
        column = hy * 8 + jb * 2 + b_low
        both = column * 2 + upper
        for n in range(4):
            v = (both.astype(jnp.float32) + 0.5) * 0.5 * qy0[n]
            shift_y[jb * 4 + n] = v - jnp.round(v)
        own = [sine(center(column * 2 + s2, 128)) for s2 in range(2)]
        child = [sine(center((column * 2 + s2) * 2 + upper, 256)) for s2 in range(2)]
        y_tabs.append((jnp.where(low_half, own[0], own[1]), own, child))

    def tables(i, carry):
        a_mid = i >> 1
        s1 = i & 1
        rows = (hx * 4 + a_mid) * 2 + s1
        s_x = sine(center(rows, 128))
        child_x = [sine(center(rows * 2 + t1, 256)) for t1 in range(2)]
        for m in range(4):
            v = (rows.astype(jnp.float32) + 0.5) * 0.5 * qx0[m]
            shift_x[i * 4 + m] = v - jnp.round(v)
        for jb in range(4):
            both, own, child = y_tabs[jb]
            at = (a_mid * 4 + jb) * 2 + s1
            speed[at] = (2.0 + s_x * both) * third
            for t1 in range(2):
                for s2 in range(2):
                    change[at * 4 + t1 * 2 + s2] = (child_x[t1] * child[s2] - s_x * own[s2]) * third
        return carry

    lax.fori_loop(0, 8, tables, 0)
    for fetch in fetches:
        fetch.wait()
    w_rows = w_ref.reshape(16 * 128, 128)

    def produce_one(i):
        tiles = fresh(LOW[0])
        ajb = i >> 1
        m_half = i & 1
        a_mid = ajb >> 2
        jb = ajb & 3
        for n_half in range(2):
            for cx in range(2):
                m = 2 * m_half + cx
                for cy in range(2):
                    n = 2 * n_half + cy
                    box = 4 * m + n
                    value = w_rows[pl.ds(ajb * 128 + box, 8, stride=16), :]
                    other = pltpu.roll(value, 64, 1)
                    real = jnp.where(low_half, value, other)
                    imag = jnp.where(low_half, other, value)
                    amp = amp0[box]
                    for s1 in range(2):
                        shift = shift_x[(a_mid * 2 + s1) * 4 + m] + shift_y[jb * 4 + n]
                        cycles = speed[ajb * 2 + s1] * amp + shift
                        turn_back(real, imag, cycles, tiles, n_half * 2 + s1, 2 * cx + cy, LOW[0])
        return laid(tiles)

    def consume_one(i, y):
        z1_ref[pl.ds(pl.multiple_of(i * 64, 64), 64), :] = y

    staged(32, produce_one, consume_one, mix_ref, LOW[0])

    def produce_two(i):
        tiles = fresh(LOW[1])
        s1 = i & 1
        ajb = i >> 1
        for c in range(4):
            source = pl.multiple_of(((ajb * 4 + c) * 2 + s1) * 16, 16)
            reals = doubled(z1_ref[pl.ds(source, 8), :], low_half)
            imags = doubled(z1_ref[pl.ds(source + 8, 8), :], low_half)
            amp = amp1[c]
            for t1 in range(2):
                lin = q_tab[2 * c + t1]
                for s2 in range(2):
                    cycles = change[i * 4 + t1 * 2 + s2] * amp + lin
                    turn_back(reals[s2], imags[s2], cycles, tiles, t1 * 2 + s2, c, LOW[1])
        return laid(tiles)

    def consume_two(i, y):
        s1 = i & 1
        ajb = i >> 1
        base = pl.multiple_of((((ajb >> 2) * 2 + s1) * 4 + (ajb & 3)) * 64, 64)
        for t1 in range(2):
            for s2 in range(2):
                tile = (t1 * 2 + s2) * 16
                for part in range(2):
                    at = base + (t1 * 32 + part * 16 + s2)
                    out_ref[pl.ds(at, 8, stride=2), :] = y[tile + 8 * part:tile + 8 * part + 8]

    def leaving(k):
        rows = pl.ds(pl.multiple_of(k * 512, 512), 512)
        return pltpu.make_async_copy(out_ref.at[rows], out_hbm.at[rows], out_sem.at[k])

    staged(32, produce_two, consume_two, mix_ref, LOW[1],
           lambda k: leaving(k).start())
    for k in range(4):
        leaving(k).wait()


def tab(n):
    return pltpu.VMEM((n, 8, 128), jnp.float32)


def source_side(weights, mix):
    pieces = weights.reshape(2, 4, 2, 4, 2, 16, 128)
    return pl.pallas_call(
        source_kernel,
        in_specs=[pl.BlockSpec(memory_space=pl.ANY)] * 2,
        out_specs=pl.BlockSpec(memory_space=pl.ANY),
        out_shape=jax.ShapeDtypeStruct((2048, 128), jnp.float32),
        scratch_shapes=[
            tab(16), tab(4), tab(8), tab(32), tab(32), tab(16), tab(128),
            pltpu.VMEM((2048, 128), jnp.float32),
            pltpu.VMEM((16, 2, 2, 2, 16, 128), jnp.float32),
            pltpu.VMEM((512, 256), jnp.bfloat16),
            pltpu.VMEM((2048, 128), jnp.float32),
            pltpu.SemaphoreType.DMA((16,)),
            pltpu.SemaphoreType.DMA,
            pltpu.SemaphoreType.DMA((4,)),
        ],
        name="source_levels",
        cost_estimate=pl.CostEstimate(flops=2 * 10**9, bytes_accessed=2 * 2**20, transcendentals=0),
    )(pieces, mix)


def target_kernel(nx, ny, piece_x, piece_y, w_hbm, mix_hbm, out_hbm,
                  amp2, lin2, amp3, lin3, amp4, change3, change4, speed4, z3_ref,
                  w_ref, mix_ref, out_ref, in_sem, mix_sem, out_sem):
    fetches = [
        pltpu.make_async_copy(w_hbm, w_ref, in_sem),
        pltpu.make_async_copy(mix_hbm, mix_ref, mix_sem),
    ]
    for fetch in fetches:
        fetch.start()
    px, py = nx // 2, ny // 2
    fx, fy = nx // 4, ny // 4
    parents, boxes = px * py, fx * fy
    wide = piece_y == 8
    groups = piece_x * (2 if wide else 1)
    lane, row = iotas()
    low_half = lane < 64
    upper = (lane >> 6) & 1
    pos_x = lax.axis_index("sx")
    pos_y = lax.axis_index("sy")
    sign = jnp.where(low_half, -0.25, 0.25)
    third = 1.0 / 3.0
    z1, z2 = lane_nodes(lane)

    def box_tables(count_x, count_y, scale, amp, lin):
        qys = [float(n) + z2 for n in range(count_y)]

        def one(m, carry):
            qx = m.astype(jnp.float32) + z1
            for n, qy in enumerate(qys):
                box = m * count_y + n
                amp[box] = scale * jnp.sqrt(qx * qx + qy * qy)
                if lin is not None:
                    lin[2 * box] = sign * qy - 0.25 * qx
                    lin[2 * box + 1] = sign * qy + 0.25 * qx
            return carry

        lax.fori_loop(0, count_x, one, 0)

    box_tables(nx, ny, 256.0, amp2, lin2)
    box_tables(px, py, 512.0, amp3, lin3)
    box_tables(fx, fy, 1024.0, amp4, None)

    if wide:
        hy = row >> 2
        k = row & 3
    else:
        hy = (row >> 1) & 1
        k = row & 1
    cols2 = hy * 32 + pos_y * piece_y + 2 * k

    def rows2(g):
        if wide:
            return jnp.full((8, 128), (g & 1) * 16 + pos_x * piece_x + (g >> 1), jnp.int32)
        return (row >> 2) * 16 + pos_x * piece_x + g

    y_tabs = []
    for t2 in range(2):
        s_y2 = sine(center(cols2 + t2, 256))
        own = [sine(center(2 * (cols2 + t2) + a2, 512)) for a2 in range(2)]
        last = [sine(center(4 * (cols2 + t2) + 2 * a2 + upper, 1024)) for a2 in range(2)]
        y_tabs.append((s_y2, jnp.where(low_half, own[0], own[1]), own, last))

    def target_tables(g, carry):
        rows = rows2(g)
        s_x2 = sine(center(rows, 256))
        for a1 in range(2):
            x3 = sine(center(2 * rows + a1, 512))
            x4 = [sine(center(4 * rows + 2 * a1 + b1, 1024)) for b1 in range(2)]
            for t2 in range(2):
                s_y2, y3, own, last = y_tabs[t2]
                ta = 2 * t2 + a1
                change3[g * 4 + ta] = (x3 * y3 - s_x2 * s_y2) * third
                for a2 in range(2):
                    for b1 in range(2):
                        at = (g * 4 + ta) * 4 + a2 * 2 + b1
                        product = x4[b1] * last[a2]
                        change4[at] = (product - x3 * own[a2]) * third
                        speed4[at] = (2.0 + product) * third
        return carry

    lax.fori_loop(0, groups, target_tables, 0)
    for fetch in fetches:
        fetch.wait()

    def arrived(box, g, part):
        if wide:
            at = (((g >> 1) * 2 + part) * 2 + (g & 1)) * 8
        else:
            at = (g * 2 + part) * 8
        return w_ref[box, pl.ds(pl.multiple_of(at, 8), 8), :]

    def produce_three(i):
        tiles = fresh(LOW[2])
        g = i >> log2(parents)
        parent = i & (parents - 1)
        m3 = parent >> log2(py)
        n3 = parent & (py - 1)
        for c in range(4):
            box = (2 * m3 + c // 2) * ny + 2 * n3 + c % 2
            reals = doubled(arrived(box, g, 0), low_half)
            imags = doubled(arrived(box, g, 1), low_half)
            amp = amp2[box]
            for a1 in range(2):
                lin = lin2[2 * box + a1]
                for t2 in range(2):
                    ta = 2 * t2 + a1
                    cycles = change3[g * 4 + ta] * amp + lin
                    turn_back(reals[t2], imags[t2], cycles, tiles, ta, c, LOW[2])
        return laid(tiles)

    def consume_three(i, y):
        z3_ref[pl.ds(pl.multiple_of(i * 64, 64), 64), :] = y

    staged(groups * parents, produce_three, consume_three, mix_ref, LOW[2])

    def decode(i):
        last = i & (boxes - 1)
        gta = i >> log2(boxes)
        return gta >> 2, gta & 3, last

    def produce_four(i):
        tiles = fresh(LOW[3])
        g, ta, last = decode(i)
        m4 = last >> log2(fy)
        n4 = last & (fy - 1)
        for c in range(4):
            box = (2 * m4 + c // 2) * py + 2 * n4 + c % 2
            source = pl.multiple_of(((g * parents + box) * 4 + ta) * 16, 16)
            reals = doubled(z3_ref[pl.ds(source, 8), :], low_half)
            imags = doubled(z3_ref[pl.ds(source + 8, 8), :], low_half)
            amp = amp3[box]
            for b1 in range(2):
                lin = lin3[2 * box + b1]
                for a2 in range(2):
                    tile = a2 * 2 + b1
                    cycles = change4[(g * 4 + ta) * 4 + tile] * amp + lin
                    turn_back(reals[a2], imags[a2], cycles, tiles, tile, c, LOW[3])
        return laid(tiles)

    def consume_four(i, y):
        g, ta, last = decode(i)
        t2 = ta >> 1
        a1 = ta & 1
        p1 = (last >> log2(fy)).astype(jnp.float32) + z1
        p2 = (last & (fy - 1)).astype(jnp.float32) + z2
        amp = amp4[last]
        rows = rows2(g) * 4 + 2 * a1
        gx = g >> 1 if wide else g
        for a2 in range(2):
            col = (4 * (cols2 + t2) + 2 * a2 + upper).astype(jnp.float32) + 0.5
            for b1 in range(2):
                tile = a2 * 2 + b1
                real = y[tile * 16:tile * 16 + 8]
                imag = y[tile * 16 + 8:tile * 16 + 16]
                r4 = (rows + b1).astype(jnp.float32) + 0.5
                cycles = speed4[(g * 4 + ta) * 4 + tile] * amp + (r4 * p1 + col * p2)
                s, c = sincos(cycles)
                ore = real * c - imag * s
                oim = real * s + imag * c
                pair = (
                    jnp.where(low_half, ore, pltpu.roll(oim, 64, 1)),
                    jnp.where(low_half, pltpu.roll(ore, 64, 1), oim),
                )
                for b2, value in enumerate(pair):
                    inner = (4 * t2 + 2 * a2 + b2) * boxes + last

                    def at(h):
                        line = (h * piece_x + gx) * 4 + 2 * a1 + b1
                        return line * (piece_y * 8 * boxes) + inner

                    if wide:
                        out_ref[pl.ds(at(g & 1), 8, stride=8 * boxes), :] = value
                    else:
                        for h in range(2):
                            out_ref[pl.ds(at(h), 4, stride=8 * boxes), :] = value[4 * h:4 * h + 4]

    early = wide and 4 * boxes == UNROLL
    size = 4 * piece_y * 8 * boxes if early else out_hbm.shape[0]

    def leaving(k):
        if early:
            k = (k & 1) * piece_x + (k >> 1)
        rows = pl.ds(pl.multiple_of(k * size, size), size)
        return pltpu.make_async_copy(out_ref.at[rows], out_hbm.at[rows], out_sem.at[k])

    staged(groups * 4 * boxes, produce_four, consume_four, mix_ref, LOW[3],
           (lambda k: leaving(k).start()) if early else None)
    if not early:
        leaving(0).start()
    for k in range(groups if early else 1):
        leaving(k).wait()


def target_side(arrived, mix, nx, ny, piece_x, piece_y):
    parents, boxes = (nx // 2) * (ny // 2), (nx // 4) * (ny // 4)
    groups = piece_x * (2 if piece_y == 8 else 1)
    return pl.pallas_call(
        functools.partial(target_kernel, nx, ny, piece_x, piece_y),
        in_specs=[pl.BlockSpec(memory_space=pl.ANY)] * 2,
        out_specs=pl.BlockSpec(memory_space=pl.ANY),
        out_shape=jax.ShapeDtypeStruct((2 * 4 * piece_x * 2 * 4 * piece_y * boxes, 128), jnp.float32),
        scratch_shapes=[
            tab(nx * ny), tab(2 * nx * ny), tab(parents), tab(2 * parents), tab(boxes),
            tab(groups * 4), tab(groups * 16), tab(groups * 16),
            pltpu.VMEM((groups * parents * 64, 128), jnp.float32),
            pltpu.VMEM(arrived.shape, jnp.float32),
            pltpu.VMEM((512, 256), jnp.bfloat16),
            pltpu.VMEM((2 * 4 * piece_x * 2 * 4 * piece_y * boxes, 128), jnp.float32),
            pltpu.SemaphoreType.DMA,
            pltpu.SemaphoreType.DMA,
            pltpu.SemaphoreType.DMA((groups,)),
        ],
        name="target_levels",
        cost_estimate=pl.CostEstimate(flops=2 * 10**9, bytes_accessed=2 * 2**20, transcendentals=0),
    )(arrived, mix)


def to_targets(made, nx, ny, piece_x, piece_y):
    if (piece_x, piece_y) != (2, 8):
        made = made.reshape(4, 2, 4, 2, 2, 4, 2, 2, 128)
        lead = [0, 1] + ([3] if piece_x == 1 else []) + [2] + ([6] if piece_y == 4 else [])
        rest = ([3] if piece_x == 2 else []) + [4, 5] + ([6] if piece_y == 8 else []) + [7]
        made = made.transpose(lead + rest + [8])
    return made.reshape(nx * ny, -1, 128)


def on_device(weights):
    nx = lax.axis_size("sx")
    ny = lax.axis_size("sy")
    piece_x = 2 * weights.shape[0] // nx
    piece_y = 2 * weights.shape[1] // ny
    mix = jnp.asarray(mixing())
    made = to_targets(source_side(weights, mix), nx, ny, piece_x, piece_y)
    arrived = lax.all_to_all(made, ("sx", "sy"), split_axis=0, concat_axis=0, tiled=True)
    out = target_side(arrived, mix, nx, ny, piece_x, piece_y)
    return out.reshape(2, 4 * piece_x, 2, 4 * piece_y, nx // 4, ny // 4, 128)


def solution(mesh):
    return jax.shard_map(
        on_device,
        mesh=mesh,
        in_specs=(P(None, None, "sx", "sy", None),),
        out_specs=P(None, "sx", None, "sy", None, None, None),
        check_vma=False,
    )
```

```python
import functools

import jax
import jax.numpy as jnp
import ml_dtypes
import numpy as np
from jax import lax
from jax.experimental import pallas as pl
from jax.experimental.pallas import tpu as pltpu
from jax.sharding import PartitionSpec as P

GRID = 4096
BOXES = 64

HALF_SIN = (4.442867279052734, -7.30741548538208, 3.5945212841033936, -0.7836661338806152)

UNROLL = 8

LOW = (True, True, True, True)

NODES = 0.5 - 0.5 * np.cos(np.pi * (2.0 * np.arange(8) + 1.0) / 16.0)


def mixing():
    def side(c):
        shifted = (c + NODES) / 2.0
        out = np.ones((8, 8))
        for i in range(8):
            for k in range(8):
                if k != i:
                    out[i] *= (shifted - NODES[k]) / (NODES[i] - NODES[k])
        return out

    rows = []
    for cx in range(2):
        for cy in range(2):
            rows.append(np.kron(np.eye(2), np.kron(side(cx), side(cy)).T))
    full = np.concatenate(rows, axis=0)
    high = full.astype(ml_dtypes.bfloat16)
    low = (full - high.astype(np.float64)).astype(ml_dtypes.bfloat16)
    return np.concatenate([high, low], axis=1)


def horner(coefs, z):
    total = coefs[-1] * z + coefs[-2]
    for c in coefs[-3::-1]:
        total = total * z + c
    return total


def sincos(cycles):
    f = cycles - jnp.round(cycles)
    h = f * horner(HALF_SIN, f * f)
    w = h * h
    d = 2.0 - w
    return h * d * lax.rsqrt(d), 1.0 - w


def sine(cycles):
    return sincos(cycles)[0]


def iotas():
    lane = lax.broadcasted_iota(jnp.int32, (8, 128), 1)
    row = lax.broadcasted_iota(jnp.int32, (8, 128), 0)
    return lane, row


def lane_nodes(lane):
    j1 = (lane >> 3) & 7
    j2 = lane & 7
    z1 = jnp.zeros((8, 128), jnp.float32)
    z2 = jnp.zeros((8, 128), jnp.float32)
    for j in range(8):
        z1 = jnp.where(j1 == j, float(NODES[j]), z1)
        z2 = jnp.where(j2 == j, float(NODES[j]), z2)
    return z1, z2


def center(index, total):
    return (index.astype(jnp.float32) + 0.5) * (1.0 / total)


def doubled(value, low_half):
    other = pltpu.roll(value, 64, 1)
    return jnp.where(low_half, value, other), jnp.where(low_half, other, value)


def turn_back(real, imag, c, s, tiles, tile, child, low):
    both = jnp.concatenate([real * c + imag * s, imag * c - real * s], axis=0)
    high = both.astype(jnp.bfloat16)
    tiles[tile][child] = high
    if low:
        tiles[4 + tile][child] = (both - high.astype(jnp.float32)).astype(jnp.bfloat16)


def fresh(low):
    return [[None] * 4 for _ in range(8 if low else 4)]


def laid(tiles):
    return jnp.concatenate([jnp.concatenate(row, axis=1) for row in tiles], axis=0)


def log2(n):
    return n.bit_length() - 1


def staged(count, produce, consume, mix_ref, low, before=None, after=None):
    def contracted(rows):
        y = jnp.dot(rows, mix_ref[...], preferred_element_type=jnp.float32)
        total = y[:64, :128] + y[:64, 128:]
        return total + y[64:, :128] if low else total

    def body(k, rows):
        if before is not None:
            before(k)
        for j in range(UNROLL):
            i = k * UNROLL + j
            y = contracted(rows)
            rows = produce(jnp.minimum(i + 1, count - 1))
            consume(i, y)
        if after is not None:
            after(k)
        return rows

    lax.fori_loop(0, count // UNROLL, body, produce(jnp.int32(0)))


def source_kernel(w_hbm, mix_hbm, out_hbm, amp0, amp1, q_tab, speed, shift_x, shift_y, change,
                  z1_ref, w_ref, mix_ref, out_ref, in_sem, mix_sem, out_sem):
    fetches = [
        pltpu.make_async_copy(w_hbm.at[:, a, :, b], w_ref.at[4 * a + b], in_sem.at[4 * a + b])
        for a in range(4)
        for b in range(4)
    ]
    fetches.append(pltpu.make_async_copy(mix_hbm, mix_ref, mix_sem))
    for fetch in fetches:
        fetch.start()
    lane, row = iotas()
    low_half = lane < 64
    upper = (lane >> 6) & 1
    pos_x = lax.axis_index("sx")
    pos_y = lax.axis_index("sy")
    third = 1.0 / 3.0

    z1, z2 = lane_nodes(lane)
    qx0 = [(4 * pos_x + m).astype(jnp.float32) + z1 for m in range(4)]
    qy0 = [(4 * pos_y + n).astype(jnp.float32) + z2 for n in range(4)]
    for m in range(4):
        for n in range(4):
            amp0[4 * m + n] = 64.0 * jnp.sqrt(qx0[m] * qx0[m] + qy0[n] * qy0[n])
    sign = jnp.where(low_half, -0.25, 0.25)
    for m in range(2):
        qx = (2 * pos_x + m).astype(jnp.float32) + z1
        for n in range(2):
            qy = (2 * pos_y + n).astype(jnp.float32) + z2
            amp1[2 * m + n] = 128.0 * jnp.sqrt(qx * qx + qy * qy)
            for t1 in range(2):
                q_tab[2 * (2 * m + n) + t1] = sign * qy + (0.25 * (2 * t1 - 1)) * qx

    hx = row >> 2
    hy = (row >> 1) & 1
    b_low = row & 1
    y_tabs = []
    for jb in range(4):
        column = hy * 8 + jb * 2 + b_low
        both = column * 2 + upper
        for n in range(4):
            v = (both.astype(jnp.float32) + 0.5) * 0.5 * qy0[n]
            shift_y[jb * 4 + n] = v - jnp.round(v)
        own = [sine(center(column * 2 + s2, 128)) for s2 in range(2)]
        child = [sine(center((column * 2 + s2) * 2 + upper, 256)) for s2 in range(2)]
        y_tabs.append((jnp.where(low_half, own[0], own[1]), own, child))

    def tables(i, carry):
        a_mid = i >> 1
        s1 = i & 1
        rows = (hx * 4 + a_mid) * 2 + s1
        s_x = sine(center(rows, 128))
        child_x = [sine(center(rows * 2 + t1, 256)) for t1 in range(2)]
        for m in range(4):
            v = (rows.astype(jnp.float32) + 0.5) * 0.5 * qx0[m]
            shift_x[i * 4 + m] = v - jnp.round(v)
        for jb in range(4):
            both, own, child = y_tabs[jb]
            at = (a_mid * 4 + jb) * 2 + s1
            speed[at] = (2.0 + s_x * both) * third
            for t1 in range(2):
                for s2 in range(2):
                    change[at * 4 + t1 * 2 + s2] = (child_x[t1] * child[s2] - s_x * own[s2]) * third
        return carry

    lax.fori_loop(0, 8, tables, 0)
    for fetch in fetches:
        fetch.wait()
    w_rows = w_ref.reshape(16 * 128, 128)

    def produce_one(i):
        tiles = fresh(LOW[0])
        ajb = i >> 1
        m_half = i & 1
        a_mid = ajb >> 2
        jb = ajb & 3
        for n_half in range(2):
            for cx in range(2):
                m = 2 * m_half + cx
                for cy in range(2):
                    n = 2 * n_half + cy
                    box = 4 * m + n
                    value = w_rows[pl.ds(ajb * 128 + box, 8, stride=16), :]
                    other = pltpu.roll(value, 64, 1)
                    real = jnp.where(low_half, value, other)
                    imag = jnp.where(low_half, other, value)
                    amp = amp0[box]
                    for s1 in range(2):
                        shift = shift_x[(a_mid * 2 + s1) * 4 + m] + shift_y[jb * 4 + n]
                        cycles = speed[ajb * 2 + s1] * amp + shift
                        s, c = sincos(cycles)
                        turn_back(real, imag, c, s, tiles, n_half * 2 + s1, 2 * cx + cy, LOW[0])
        return laid(tiles)

    def consume_one(i, y):
        z1_ref[pl.ds(pl.multiple_of(i * 64, 64), 64), :] = y

    staged(32, produce_one, consume_one, mix_ref, LOW[0])

    def produce_two(i):
        tiles = fresh(LOW[1])
        s1 = i & 1
        ajb = i >> 1
        for c in range(4):
            source = pl.multiple_of(((ajb * 4 + c) * 2 + s1) * 16, 16)
            reals = doubled(z1_ref[pl.ds(source, 8), :], low_half)
            imags = doubled(z1_ref[pl.ds(source + 8, 8), :], low_half)
            amp = amp1[c]
            for t1 in range(2):
                lin = q_tab[2 * c + t1]
                for s2 in range(2):
                    cycles = change[i * 4 + t1 * 2 + s2] * amp + lin
                    sin, cos = sincos(cycles)
                    turn_back(reals[s2], imags[s2], cos, sin, tiles, t1 * 2 + s2, c, LOW[1])
        return laid(tiles)

    def consume_two(i, y):
        s1 = i & 1
        ajb = i >> 1
        base = pl.multiple_of((((ajb >> 2) * 2 + s1) * 4 + (ajb & 3)) * 64, 64)
        for t1 in range(2):
            for s2 in range(2):
                tile = (t1 * 2 + s2) * 16
                for part in range(2):
                    at = base + (t1 * 32 + part * 16 + s2)
                    out_ref[pl.ds(at, 8, stride=2), :] = y[tile + 8 * part:tile + 8 * part + 8]

    def leaving(k):
        rows = pl.ds(pl.multiple_of(k * 512, 512), 512)
        return pltpu.make_async_copy(out_ref.at[rows], out_hbm.at[rows], out_sem.at[k])

    staged(32, produce_two, consume_two, mix_ref, LOW[1],
           after=lambda k: leaving(k).start())
    for k in range(4):
        leaving(k).wait()


def tab(n):
    return pltpu.VMEM((n, 8, 128), jnp.float32)


def source_side(weights, mix):
    pieces = weights.reshape(2, 4, 2, 4, 2, 16, 128)
    return pl.pallas_call(
        source_kernel,
        in_specs=[pl.BlockSpec(memory_space=pl.ANY)] * 2,
        out_specs=pl.BlockSpec(memory_space=pl.ANY),
        out_shape=jax.ShapeDtypeStruct((2048, 128), jnp.float32),
        scratch_shapes=[
            tab(16), tab(4), tab(8), tab(32), tab(32), tab(16), tab(128),
            pltpu.VMEM((2048, 128), jnp.float32),
            pltpu.VMEM((16, 2, 2, 2, 16, 128), jnp.float32),
            pltpu.VMEM((512, 256), jnp.bfloat16),
            pltpu.VMEM((2048, 128), jnp.float32),
            pltpu.SemaphoreType.DMA((16,)),
            pltpu.SemaphoreType.DMA,
            pltpu.SemaphoreType.DMA((4,)),
        ],
        name="source_levels",
        cost_estimate=pl.CostEstimate(flops=2 * 10**9, bytes_accessed=2 * 2**20, transcendentals=0),
    )(pieces, mix)


def group_bits(nx, ny, piece_x, piece_y):
    return nx // 2, ny // 2, nx // 4, ny // 4, piece_y == 8, piece_x * (2 if piece_y == 8 else 1)


def phase_kernel(nx, ny, piece_x, piece_y, cs3, cs4, cs5,
                 amp2, lin2, amp3, lin3, amp4, change3, change4, speed4):
    px, py, fx, fy, wide, groups = group_bits(nx, ny, piece_x, piece_y)
    parents, boxes = px * py, fx * fy
    lane, row = iotas()
    low_half = lane < 64
    upper = (lane >> 6) & 1
    pos_x = lax.axis_index("sx")
    pos_y = lax.axis_index("sy")
    sign = jnp.where(low_half, -0.25, 0.25)
    third = 1.0 / 3.0
    z1, z2 = lane_nodes(lane)

    def box_tables(count_x, count_y, scale, amp, lin):
        qys = [float(n) + z2 for n in range(count_y)]

        def one(m, carry):
            qx = m.astype(jnp.float32) + z1
            for n, qy in enumerate(qys):
                box = m * count_y + n
                amp[box] = scale * jnp.sqrt(qx * qx + qy * qy)
                if lin is not None:
                    lin[2 * box] = sign * qy - 0.25 * qx
                    lin[2 * box + 1] = sign * qy + 0.25 * qx
            return carry

        lax.fori_loop(0, count_x, one, 0)

    box_tables(nx, ny, 256.0, amp2, lin2)
    box_tables(px, py, 512.0, amp3, lin3)
    box_tables(fx, fy, 1024.0, amp4, None)

    if wide:
        hy = row >> 2
        k = row & 3
    else:
        hy = (row >> 1) & 1
        k = row & 1
    cols2 = hy * 32 + pos_y * piece_y + 2 * k

    def rows2(g):
        if wide:
            return jnp.full((8, 128), (g & 1) * 16 + pos_x * piece_x + (g >> 1), jnp.int32)
        return (row >> 2) * 16 + pos_x * piece_x + g

    y_tabs = []
    for t2 in range(2):
        s_y2 = sine(center(cols2 + t2, 256))
        own = [sine(center(2 * (cols2 + t2) + a2, 512)) for a2 in range(2)]
        last = [sine(center(4 * (cols2 + t2) + 2 * a2 + upper, 1024)) for a2 in range(2)]
        y_tabs.append((s_y2, jnp.where(low_half, own[0], own[1]), own, last))

    def target_tables(g, carry):
        rows = rows2(g)
        s_x2 = sine(center(rows, 256))
        for a1 in range(2):
            x3 = sine(center(2 * rows + a1, 512))
            x4 = [sine(center(4 * rows + 2 * a1 + b1, 1024)) for b1 in range(2)]
            for t2 in range(2):
                s_y2, y3, own, last = y_tabs[t2]
                ta = 2 * t2 + a1
                change3[g * 4 + ta] = (x3 * y3 - s_x2 * s_y2) * third
                for a2 in range(2):
                    for b1 in range(2):
                        at = (g * 4 + ta) * 4 + a2 * 2 + b1
                        product = x4[b1] * last[a2]
                        change4[at] = (product - x3 * own[a2]) * third
                        speed4[at] = (2.0 + product) * third
        return carry

    lax.fori_loop(0, groups, target_tables, 0)

    def put(ref, at, cycles):
        s, c = sincos(cycles)
        ref[at] = c
        ref[at + 1] = s

    def phases_three(i, carry):
        g = i >> log2(parents)
        parent = i & (parents - 1)
        m3 = parent >> log2(py)
        n3 = parent & (py - 1)
        for c in range(4):
            box = (2 * m3 + c // 2) * ny + 2 * n3 + c % 2
            for ta in range(4):
                cycles = change3[g * 4 + ta] * amp2[box] + lin2[2 * box + ta % 2]
                put(cs3, ((i * 4 + c) * 4 + ta) * 2, cycles)
        return carry

    lax.fori_loop(0, groups * parents, phases_three, 0)

    def phases_four(i, carry):
        last = i & (boxes - 1)
        gta = i >> log2(boxes)
        g = gta >> 2
        t2 = (gta >> 1) & 1
        a1 = gta & 1
        m4 = last >> log2(fy)
        n4 = last & (fy - 1)
        p1 = m4.astype(jnp.float32) + z1
        p2 = n4.astype(jnp.float32) + z2
        rows = rows2(g) * 4 + 2 * a1
        for tile in range(4):
            a2, b1 = tile // 2, tile % 2
            for c in range(4):
                box = (2 * m4 + c // 2) * py + 2 * n4 + c % 2
                cycles = change4[gta * 4 + tile] * amp3[box] + lin3[2 * box + b1]
                put(cs4, ((i * 4 + c) * 4 + tile) * 2, cycles)
            col = (4 * (cols2 + t2) + 2 * a2 + upper).astype(jnp.float32) + 0.5
            r4 = (rows + b1).astype(jnp.float32) + 0.5
            put(cs5, (i * 4 + tile) * 2, speed4[gta * 4 + tile] * amp4[last] + (r4 * p1 + col * p2))
        return carry

    lax.fori_loop(0, groups * 4 * boxes, phases_four, 0)


def phase_side(nx, ny, piece_x, piece_y):
    px, py, fx, fy, wide, groups = group_bits(nx, ny, piece_x, piece_y)
    parents, boxes = px * py, fx * fy
    items = groups * parents
    return pl.pallas_call(
        functools.partial(phase_kernel, nx, ny, piece_x, piece_y),
        out_specs=[pl.BlockSpec(memory_space=pltpu.VMEM)] * 3,
        out_shape=[jax.ShapeDtypeStruct((32 * items, 8, 128), jnp.float32), jax.ShapeDtypeStruct((32 * items, 8, 128), jnp.float32),
                   jax.ShapeDtypeStruct((8 * items, 8, 128), jnp.float32)],
        scratch_shapes=[
            tab(nx * ny), tab(2 * nx * ny), tab(parents), tab(2 * parents), tab(boxes),
            tab(groups * 4), tab(groups * 16), tab(groups * 16),
        ],
        name="phases",
        cost_estimate=pl.CostEstimate(flops=2 * 10**9, bytes_accessed=9 * 2**20, transcendentals=0),
    )()


def target_kernel(nx, ny, piece_x, piece_y, w_ref, mix_ref, cs3_hbm, cs4_hbm, cs5_hbm, out_hbm,
                  z3_ref, cs3, cs4, cs5, out_ref, in_sem, out_sem):
    px, py, fx, fy, wide, groups = group_bits(nx, ny, piece_x, piece_y)
    parents, boxes = px * py, fx * fy
    low_half = iotas()[0] < 64

    def coming(which, g):
        source, target = ((cs3_hbm, cs3), (cs4_hbm, cs4), (cs5_hbm, cs5))[which]
        part = source.shape[0] // groups
        rows = pl.ds(g * part, part)
        return pltpu.make_async_copy(source.at[rows], target.at[rows], in_sem.at[which, g])

    for which in range(3):
        for g in range(groups):
            coming(which, g).start()

    def await_next(per_group, parts):
        stepwise = per_group == UNROLL
        for which in parts:
            for g in range(1 if stepwise else groups):
                coming(which, g).wait()
        if not stepwise:
            return None

        def before(k):
            @pl.when(k + 1 < groups)
            def _():
                for which in parts:
                    coming(which, k + 1).wait()

        return before

    def arrived(box, g, part):
        if wide:
            at = (((g >> 1) * 2 + part) * 2 + (g & 1)) * 8
        else:
            at = (g * 2 + part) * 8
        return w_ref[box, pl.ds(pl.multiple_of(at, 8), 8), :]

    def produce_three(i):
        tiles = fresh(LOW[2])
        g = i >> log2(parents)
        parent = i & (parents - 1)
        m3 = parent >> log2(py)
        n3 = parent & (py - 1)
        for c in range(4):
            box = (2 * m3 + c // 2) * ny + 2 * n3 + c % 2
            reals = doubled(arrived(box, g, 0), low_half)
            imags = doubled(arrived(box, g, 1), low_half)
            for ta in range(4):
                at = ((i * 4 + c) * 4 + ta) * 2
                turn_back(reals[ta // 2], imags[ta // 2], cs3[at], cs3[at + 1], tiles, ta, c, LOW[2])
        return laid(tiles)

    def consume_three(i, y):
        z3_ref[pl.ds(pl.multiple_of(i * 64, 64), 64), :] = y

    staged(groups * parents, produce_three, consume_three, mix_ref, LOW[2], await_next(parents, (0,)))

    def decode(i):
        last = i & (boxes - 1)
        gta = i >> log2(boxes)
        return gta >> 2, gta & 3, last

    def produce_four(i):
        tiles = fresh(LOW[3])
        g, ta, last = decode(i)
        m4 = last >> log2(fy)
        n4 = last & (fy - 1)
        for c in range(4):
            box = (2 * m4 + c // 2) * py + 2 * n4 + c % 2
            source = pl.multiple_of(((g * parents + box) * 4 + ta) * 16, 16)
            reals = doubled(z3_ref[pl.ds(source, 8), :], low_half)
            imags = doubled(z3_ref[pl.ds(source + 8, 8), :], low_half)
            for tile in range(4):
                at = ((i * 4 + c) * 4 + tile) * 2
                turn_back(reals[tile // 2], imags[tile // 2], cs4[at], cs4[at + 1], tiles, tile, c, LOW[3])
        return laid(tiles)

    def consume_four(i, y):
        g, ta, last = decode(i)
        t2 = ta >> 1
        a1 = ta & 1
        gx = g >> 1 if wide else g
        for a2 in range(2):
            for b1 in range(2):
                tile = a2 * 2 + b1
                real = y[tile * 16:tile * 16 + 8]
                imag = y[tile * 16 + 8:tile * 16 + 16]
                c, s = cs5[(i * 4 + tile) * 2], cs5[(i * 4 + tile) * 2 + 1]
                ore = real * c - imag * s
                oim = real * s + imag * c
                pair = (
                    jnp.where(low_half, ore, pltpu.roll(oim, 64, 1)),
                    jnp.where(low_half, pltpu.roll(ore, 64, 1), oim),
                )
                for b2, value in enumerate(pair):
                    inner = (4 * t2 + 2 * a2 + b2) * boxes + last

                    def at(h):
                        line = (h * piece_x + gx) * 4 + 2 * a1 + b1
                        return line * (piece_y * 8 * boxes) + inner

                    if wide:
                        out_ref[pl.ds(at(g & 1), 8, stride=8 * boxes), :] = value
                    else:
                        for h in range(2):
                            out_ref[pl.ds(at(h), 4, stride=8 * boxes), :] = value[4 * h:4 * h + 4]

    early = wide and 4 * boxes == UNROLL
    size = 4 * piece_y * 8 * boxes if early else out_hbm.shape[0]

    def leaving(k):
        if early:
            k = (k & 1) * piece_x + (k >> 1)
        rows = pl.ds(pl.multiple_of(k * size, size), size)
        return pltpu.make_async_copy(out_ref.at[rows], out_hbm.at[rows], out_sem.at[k])

    staged(groups * 4 * boxes, produce_four, consume_four, mix_ref, LOW[3],
           await_next(4 * boxes, (1, 2)), (lambda k: leaving(k).start()) if early else None)
    if not early:
        leaving(0).start()
    for k in range(groups if early else 1):
        leaving(k).wait()


def target_side(arrived, mix, phases, nx, ny, piece_x, piece_y):
    parents, boxes = (nx // 2) * (ny // 2), (nx // 4) * (ny // 4)
    groups = piece_x * (2 if piece_y == 8 else 1)
    return pl.pallas_call(
        functools.partial(target_kernel, nx, ny, piece_x, piece_y),
        in_specs=[pl.BlockSpec(memory_space=pltpu.VMEM)] * 2 + [pl.BlockSpec(memory_space=pl.ANY)] * 3,
        out_specs=pl.BlockSpec(memory_space=pl.ANY),
        out_shape=jax.ShapeDtypeStruct((2 * 4 * piece_x * 2 * 4 * piece_y * boxes, 128), jnp.float32),
        scratch_shapes=[
            pltpu.VMEM((groups * parents * 64, 128), jnp.float32),
            *[pltpu.VMEM(p.shape, jnp.float32) for p in phases],
            pltpu.VMEM((2 * 4 * piece_x * 2 * 4 * piece_y * boxes, 128), jnp.float32),
            pltpu.SemaphoreType.DMA((3, groups)),
            pltpu.SemaphoreType.DMA((groups,)),
        ],
        name="target_levels",
        cost_estimate=pl.CostEstimate(flops=2 * 10**9, bytes_accessed=2 * 2**20, transcendentals=0),
    )(arrived, mix, *phases)


def to_targets(made, nx, ny, piece_x, piece_y):
    if (piece_x, piece_y) != (2, 8):
        made = made.reshape(4, 2, 4, 2, 2, 4, 2, 2, 128)
        lead = [0, 1] + ([3] if piece_x == 1 else []) + [2] + ([6] if piece_y == 4 else [])
        rest = ([3] if piece_x == 2 else []) + [4, 5] + ([6] if piece_y == 8 else []) + [7]
        made = made.transpose(lead + rest + [8])
    return made.reshape(nx * ny, -1, 128)


def on_device(weights):
    nx = lax.axis_size("sx")
    ny = lax.axis_size("sy")
    piece_x = 2 * weights.shape[0] // nx
    piece_y = 2 * weights.shape[1] // ny
    mix = jnp.asarray(mixing())
    made = to_targets(source_side(weights, mix), nx, ny, piece_x, piece_y)
    arrived = lax.all_to_all(made, ("sx", "sy"), split_axis=0, concat_axis=0, tiled=True)
    phases = phase_side(nx, ny, piece_x, piece_y)
    out = target_side(arrived, mix, phases, nx, ny, piece_x, piece_y)
    return out.reshape(2, 4 * piece_x, 2, 4 * piece_y, nx // 4, ny // 4, 128)


def solution(mesh):
    return jax.shard_map(
        on_device,
        mesh=mesh,
        in_specs=(P(None, None, "sx", "sy", None),),
        out_specs=P(None, "sx", None, "sy", None, None, None),
        check_vma=False,
    )
```

```python
import functools

import jax
import jax.numpy as jnp
import ml_dtypes
import numpy as np
from jax import lax
from jax.experimental import pallas as pl
from jax.experimental.pallas import tpu as pltpu
from jax.sharding import PartitionSpec as P

GRID = 4096
BOXES = 64

HALF_SIN = (4.442867279052734, -7.30741548538208, 3.5945212841033936, -0.7836661338806152)

UNROLL = 8

LOW = (True, True, True, True)

NODES = 0.5 - 0.5 * np.cos(np.pi * (2.0 * np.arange(8) + 1.0) / 16.0)


def mixing():
    def side(c):
        shifted = (c + NODES) / 2.0
        out = np.ones((8, 8))
        for i in range(8):
            for k in range(8):
                if k != i:
                    out[i] *= (shifted - NODES[k]) / (NODES[i] - NODES[k])
        return out

    rows = []
    for cx in range(2):
        for cy in range(2):
            rows.append(np.kron(np.eye(2), np.kron(side(cx), side(cy)).T))
    full = np.concatenate(rows, axis=0)
    high = full.astype(ml_dtypes.bfloat16)
    low = (full - high.astype(np.float64)).astype(ml_dtypes.bfloat16)
    return np.concatenate([high, low], axis=1)


def horner(coefs, z):
    total = coefs[-1] * z + coefs[-2]
    for c in coefs[-3::-1]:
        total = total * z + c
    return total


def sincos(cycles):
    f = cycles - jnp.round(cycles)
    h = f * horner(HALF_SIN, f * f)
    w = h * h
    d = 2.0 - w
    return h * d * lax.rsqrt(d), 1.0 - w


def sine(cycles):
    return sincos(cycles)[0]


def iotas():
    lane = lax.broadcasted_iota(jnp.int32, (8, 128), 1)
    row = lax.broadcasted_iota(jnp.int32, (8, 128), 0)
    return lane, row


def lane_nodes(lane):
    j1 = (lane >> 3) & 7
    j2 = lane & 7
    z1 = jnp.zeros((8, 128), jnp.float32)
    z2 = jnp.zeros((8, 128), jnp.float32)
    for j in range(8):
        z1 = jnp.where(j1 == j, float(NODES[j]), z1)
        z2 = jnp.where(j2 == j, float(NODES[j]), z2)
    return z1, z2


def center(index, total):
    return (index.astype(jnp.float32) + 0.5) * (1.0 / total)


def doubled(value, low_half):
    other = pltpu.roll(value, 64, 1)
    return jnp.where(low_half, value, other), jnp.where(low_half, other, value)


def turn_back(real, imag, c, s, tiles, tile, child, low):
    both = jnp.concatenate([real * c + imag * s, imag * c - real * s], axis=0)
    high = both.astype(jnp.bfloat16)
    tiles[tile][child] = high
    if low:
        tiles[4 + tile][child] = (both - high.astype(jnp.float32)).astype(jnp.bfloat16)


def fresh(low):
    return [[None] * 4 for _ in range(8 if low else 4)]


def laid(tiles):
    return jnp.concatenate([jnp.concatenate(row, axis=1) for row in tiles], axis=0)


def log2(n):
    return n.bit_length() - 1


def staged(count, produce, consume, mix_ref, low, before=None, after=None):
    def contracted(rows):
        y = jnp.dot(rows, mix_ref[...], preferred_element_type=jnp.float32)
        total = y[:64, :128] + y[:64, 128:]
        return total + y[64:, :128] if low else total

    def body(k, rows):
        if before is not None:
            before(k)
        for j in range(UNROLL):
            i = k * UNROLL + j
            y = contracted(rows)
            rows = produce(jnp.minimum(i + 1, count - 1))
            consume(i, y)
        if after is not None:
            after(k)
        return rows

    lax.fori_loop(0, count // UNROLL, body, produce(jnp.int32(0)))


def source_kernel(w_hbm, mix_hbm, out_hbm, amp0, amp1, q_tab, speed, shift_x, shift_y, change,
                  z1_ref, w_ref, mix_ref, out_ref, in_sem, mix_sem, out_sem):
    fetches = [
        pltpu.make_async_copy(w_hbm.at[:, a, :, b], w_ref.at[4 * a + b], in_sem.at[4 * a + b])
        for a in range(4)
        for b in range(4)
    ]
    fetches.append(pltpu.make_async_copy(mix_hbm, mix_ref, mix_sem))
    for fetch in fetches:
        fetch.start()
    lane, row = iotas()
    low_half = lane < 64
    upper = (lane >> 6) & 1
    pos_x = lax.axis_index("sx")
    pos_y = lax.axis_index("sy")
    third = 1.0 / 3.0

    z1, z2 = lane_nodes(lane)
    qx0 = [(4 * pos_x + m).astype(jnp.float32) + z1 for m in range(4)]
    qy0 = [(4 * pos_y + n).astype(jnp.float32) + z2 for n in range(4)]
    for m in range(4):
        for n in range(4):
            amp0[4 * m + n] = 64.0 * jnp.sqrt(qx0[m] * qx0[m] + qy0[n] * qy0[n])
    sign = jnp.where(low_half, -0.25, 0.25)
    for m in range(2):
        qx = (2 * pos_x + m).astype(jnp.float32) + z1
        for n in range(2):
            qy = (2 * pos_y + n).astype(jnp.float32) + z2
            amp1[2 * m + n] = 128.0 * jnp.sqrt(qx * qx + qy * qy)
            for t1 in range(2):
                q_tab[2 * (2 * m + n) + t1] = sign * qy + (0.25 * (2 * t1 - 1)) * qx

    hx = row >> 2
    hy = (row >> 1) & 1
    b_low = row & 1
    y_tabs = []
    for jb in range(4):
        column = hy * 8 + jb * 2 + b_low
        both = column * 2 + upper
        for n in range(4):
            v = (both.astype(jnp.float32) + 0.5) * 0.5 * qy0[n]
            shift_y[jb * 4 + n] = v - jnp.round(v)
        own = [sine(center(column * 2 + s2, 128)) for s2 in range(2)]
        child = [sine(center((column * 2 + s2) * 2 + upper, 256)) for s2 in range(2)]
        y_tabs.append((jnp.where(low_half, own[0], own[1]), own, child))

    def tables(i, carry):
        a_mid = i >> 1
        s1 = i & 1
        rows = (hx * 4 + a_mid) * 2 + s1
        s_x = sine(center(rows, 128))
        child_x = [sine(center(rows * 2 + t1, 256)) for t1 in range(2)]
        for m in range(4):
            v = (rows.astype(jnp.float32) + 0.5) * 0.5 * qx0[m]
            shift_x[i * 4 + m] = v - jnp.round(v)
        for jb in range(4):
            both, own, child = y_tabs[jb]
            at = (a_mid * 4 + jb) * 2 + s1
            speed[at] = (2.0 + s_x * both) * third
            for t1 in range(2):
                for s2 in range(2):
                    change[at * 4 + t1 * 2 + s2] = (child_x[t1] * child[s2] - s_x * own[s2]) * third
        return carry

    lax.fori_loop(0, 8, tables, 0)
    for fetch in fetches:
        fetch.wait()
    w_rows = w_ref.reshape(16 * 128, 128)

    def produce_one(i):
        tiles = fresh(LOW[0])
        ajb = i >> 1
        m_half = i & 1
        a_mid = ajb >> 2
        jb = ajb & 3
        for n_half in range(2):
            for cx in range(2):
                m = 2 * m_half + cx
                for cy in range(2):
                    n = 2 * n_half + cy
                    box = 4 * m + n
                    value = w_rows[pl.ds(ajb * 128 + box, 8, stride=16), :]
                    other = pltpu.roll(value, 64, 1)
                    real = jnp.where(low_half, value, other)
                    imag = jnp.where(low_half, other, value)
                    amp = amp0[box]
                    for s1 in range(2):
                        shift = shift_x[(a_mid * 2 + s1) * 4 + m] + shift_y[jb * 4 + n]
                        cycles = speed[ajb * 2 + s1] * amp + shift
                        s, c = sincos(cycles)
                        turn_back(real, imag, c, s, tiles, n_half * 2 + s1, 2 * cx + cy, LOW[0])
        return laid(tiles)

    def consume_one(i, y):
        z1_ref[pl.ds(pl.multiple_of(i * 64, 64), 64), :] = y

    staged(32, produce_one, consume_one, mix_ref, LOW[0])

    def produce_two(i):
        tiles = fresh(LOW[1])
        s1 = i & 1
        ajb = i >> 1
        for c in range(4):
            source = pl.multiple_of(((ajb * 4 + c) * 2 + s1) * 16, 16)
            reals = doubled(z1_ref[pl.ds(source, 8), :], low_half)
            imags = doubled(z1_ref[pl.ds(source + 8, 8), :], low_half)
            amp = amp1[c]
            for t1 in range(2):
                lin = q_tab[2 * c + t1]
                for s2 in range(2):
                    cycles = change[i * 4 + t1 * 2 + s2] * amp + lin
                    sin, cos = sincos(cycles)
                    turn_back(reals[s2], imags[s2], cos, sin, tiles, t1 * 2 + s2, c, LOW[1])
        return laid(tiles)

    def consume_two(i, y):
        s1 = i & 1
        ajb = i >> 1
        base = pl.multiple_of((((ajb >> 2) * 2 + s1) * 4 + (ajb & 3)) * 64, 64)
        for t1 in range(2):
            for s2 in range(2):
                tile = (t1 * 2 + s2) * 16
                for part in range(2):
                    at = base + (t1 * 32 + part * 16 + s2)
                    out_ref[pl.ds(at, 8, stride=2), :] = y[tile + 8 * part:tile + 8 * part + 8]

    def leaving(k):
        rows = pl.ds(pl.multiple_of(k * 512, 512), 512)
        return pltpu.make_async_copy(out_ref.at[rows], out_hbm.at[rows], out_sem.at[k])

    staged(32, produce_two, consume_two, mix_ref, LOW[1],
           after=lambda k: leaving(k).start())
    for k in range(4):
        leaving(k).wait()


def tab(n):
    return pltpu.VMEM((n, 8, 128), jnp.float32)


def source_side(weights, mix):
    pieces = weights.reshape(2, 4, 2, 4, 2, 16, 128)
    return pl.pallas_call(
        source_kernel,
        in_specs=[pl.BlockSpec(memory_space=pltpu.HBM)] * 2,
        out_specs=pl.BlockSpec(memory_space=pltpu.HBM),
        out_shape=jax.ShapeDtypeStruct((2048, 128), jnp.float32),
        scratch_shapes=[
            tab(16), tab(4), tab(8), tab(32), tab(32), tab(16), tab(128),
            pltpu.VMEM((2048, 128), jnp.float32),
            pltpu.VMEM((16, 2, 2, 2, 16, 128), jnp.float32),
            pltpu.VMEM((512, 256), jnp.bfloat16),
            pltpu.VMEM((2048, 128), jnp.float32),
            pltpu.SemaphoreType.DMA((16,)),
            pltpu.SemaphoreType.DMA,
            pltpu.SemaphoreType.DMA((4,)),
        ],
        name="source_levels",
        cost_estimate=pl.CostEstimate(flops=2 * 10**9, bytes_accessed=2 * 2**20, transcendentals=0),
    )(pieces, mix)


def group_bits(nx, ny, piece_x, piece_y):
    return nx // 2, ny // 2, nx // 4, ny // 4, piece_y == 8, piece_x * (2 if piece_y == 8 else 1)


def ranges(ref, items):
    return (ref.at[pl.ds(0, 32 * items)], ref.at[pl.ds(32 * items, 32 * items)],
            ref.at[pl.ds(64 * items, 8 * items)])


def phase_kernel(nx, ny, piece_x, piece_y, out_ref,
                 amp2, lin2, amp3, lin3, amp4, change3, change4, speed4):
    px, py, fx, fy, wide, groups = group_bits(nx, ny, piece_x, piece_y)
    parents, boxes = px * py, fx * fy
    items = groups * parents
    cs3, cs4, cs5 = ranges(out_ref, items)
    lane, row = iotas()
    low_half = lane < 64
    upper = (lane >> 6) & 1
    pos_x = lax.axis_index("sx")
    pos_y = lax.axis_index("sy")
    sign = jnp.where(low_half, -0.25, 0.25)
    third = 1.0 / 3.0
    z1, z2 = lane_nodes(lane)

    def box_tables(count_x, count_y, scale, amp, lin):
        qys = [float(n) + z2 for n in range(count_y)]

        def one(m, carry):
            qx = m.astype(jnp.float32) + z1
            for n, qy in enumerate(qys):
                box = m * count_y + n
                amp[box] = scale * jnp.sqrt(qx * qx + qy * qy)
                if lin is not None:
                    lin[2 * box] = sign * qy - 0.25 * qx
                    lin[2 * box + 1] = sign * qy + 0.25 * qx
            return carry

        lax.fori_loop(0, count_x, one, 0)

    box_tables(nx, ny, 256.0, amp2, lin2)
    box_tables(px, py, 512.0, amp3, lin3)
    box_tables(fx, fy, 1024.0, amp4, None)

    if wide:
        hy = row >> 2
        k = row & 3
    else:
        hy = (row >> 1) & 1
        k = row & 1
    cols2 = hy * 32 + pos_y * piece_y + 2 * k

    def rows2(g):
        if wide:
            return jnp.full((8, 128), (g & 1) * 16 + pos_x * piece_x + (g >> 1), jnp.int32)
        return (row >> 2) * 16 + pos_x * piece_x + g

    y_tabs = []
    for t2 in range(2):
        s_y2 = sine(center(cols2 + t2, 256))
        own = [sine(center(2 * (cols2 + t2) + a2, 512)) for a2 in range(2)]
        last = [sine(center(4 * (cols2 + t2) + 2 * a2 + upper, 1024)) for a2 in range(2)]
        y_tabs.append((s_y2, jnp.where(low_half, own[0], own[1]), own, last))

    def target_tables(g, carry):
        rows = rows2(g)
        s_x2 = sine(center(rows, 256))
        for a1 in range(2):
            x3 = sine(center(2 * rows + a1, 512))
            x4 = [sine(center(4 * rows + 2 * a1 + b1, 1024)) for b1 in range(2)]
            for t2 in range(2):
                s_y2, y3, own, last = y_tabs[t2]
                ta = 2 * t2 + a1
                change3[g * 4 + ta] = (x3 * y3 - s_x2 * s_y2) * third
                for a2 in range(2):
                    for b1 in range(2):
                        at = (g * 4 + ta) * 4 + a2 * 2 + b1
                        product = x4[b1] * last[a2]
                        change4[at] = (product - x3 * own[a2]) * third
                        speed4[at] = (2.0 + product) * third
        return carry

    lax.fori_loop(0, groups, target_tables, 0)

    def put(ref, at, cycles):
        s, c = sincos(cycles)
        ref[at] = c
        ref[at + 1] = s

    def phases_three(i, carry):
        g = i >> log2(parents)
        parent = i & (parents - 1)
        m3 = parent >> log2(py)
        n3 = parent & (py - 1)
        for c in range(4):
            box = (2 * m3 + c // 2) * ny + 2 * n3 + c % 2
            for ta in range(4):
                cycles = change3[g * 4 + ta] * amp2[box] + lin2[2 * box + ta % 2]
                put(cs3, ((i * 4 + c) * 4 + ta) * 2, cycles)
        return carry

    lax.fori_loop(0, groups * parents, phases_three, 0)

    def phases_four(i, carry):
        last = i & (boxes - 1)
        gta = i >> log2(boxes)
        g = gta >> 2
        t2 = (gta >> 1) & 1
        a1 = gta & 1
        m4 = last >> log2(fy)
        n4 = last & (fy - 1)
        p1 = m4.astype(jnp.float32) + z1
        p2 = n4.astype(jnp.float32) + z2
        rows = rows2(g) * 4 + 2 * a1
        for tile in range(4):
            a2, b1 = tile // 2, tile % 2
            for c in range(4):
                box = (2 * m4 + c // 2) * py + 2 * n4 + c % 2
                cycles = change4[gta * 4 + tile] * amp3[box] + lin3[2 * box + b1]
                put(cs4, ((i * 4 + c) * 4 + tile) * 2, cycles)
            col = (4 * (cols2 + t2) + 2 * a2 + upper).astype(jnp.float32) + 0.5
            r4 = (rows + b1).astype(jnp.float32) + 0.5
            put(cs5, (i * 4 + tile) * 2, speed4[gta * 4 + tile] * amp4[last] + (r4 * p1 + col * p2))
        return carry

    lax.fori_loop(0, groups * 4 * boxes, phases_four, 0)


def phase_side(nx, ny, piece_x, piece_y):
    px, py, fx, fy, wide, groups = group_bits(nx, ny, piece_x, piece_y)
    parents, boxes = px * py, fx * fy
    items = groups * parents
    return pl.pallas_call(
        functools.partial(phase_kernel, nx, ny, piece_x, piece_y),
        out_specs=pl.BlockSpec(memory_space=pltpu.VMEM),
        out_shape=jax.ShapeDtypeStruct((72 * items, 8, 128), jnp.float32),
        scratch_shapes=[
            tab(nx * ny), tab(2 * nx * ny), tab(parents), tab(2 * parents), tab(boxes),
            tab(groups * 4), tab(groups * 16), tab(groups * 16),
        ],
        name="phases",
        cost_estimate=pl.CostEstimate(flops=2 * 10**9, bytes_accessed=9 * 2**20, transcendentals=0),
    )()


def target_kernel(nx, ny, piece_x, piece_y, w_ref, mix_ref, cs_hbm, out_hbm,
                  z3_ref, cs_ref, out_ref, in_sem, out_sem):
    px, py, fx, fy, wide, groups = group_bits(nx, ny, piece_x, piece_y)
    parents, boxes = px * py, fx * fy
    low_half = iotas()[0] < 64

    comes = ranges(cs_hbm, groups * parents)
    cs3, cs4, cs5 = kept = ranges(cs_ref, groups * parents)

    def coming(which, g):
        source, target = comes[which], kept[which]
        part = source.shape[0] // groups
        rows = pl.ds(g * part, part)
        return pltpu.make_async_copy(source.at[rows], target.at[rows], in_sem.at[which, g])

    for which in range(3):
        for g in range(groups):
            coming(which, g).start()

    def await_next(per_group, parts):
        stepwise = per_group == UNROLL
        for which in parts:
            for g in range(1 if stepwise else groups):
                coming(which, g).wait()
        if not stepwise:
            return None

        def before(k):
            @pl.when(k + 1 < groups)
            def _():
                for which in parts:
                    coming(which, k + 1).wait()

        return before

    def arrived(box, g, part):
        if wide:
            at = (((g >> 1) * 2 + part) * 2 + (g & 1)) * 8
        else:
            at = (g * 2 + part) * 8
        return w_ref[box, pl.ds(pl.multiple_of(at, 8), 8), :]

    def produce_three(i):
        tiles = fresh(LOW[2])
        g = i >> log2(parents)
        parent = i & (parents - 1)
        m3 = parent >> log2(py)
        n3 = parent & (py - 1)
        for c in range(4):
            box = (2 * m3 + c // 2) * ny + 2 * n3 + c % 2
            reals = doubled(arrived(box, g, 0), low_half)
            imags = doubled(arrived(box, g, 1), low_half)
            for ta in range(4):
                at = ((i * 4 + c) * 4 + ta) * 2
                turn_back(reals[ta // 2], imags[ta // 2], cs3[at], cs3[at + 1], tiles, ta, c, LOW[2])
        return laid(tiles)

    def consume_three(i, y):
        z3_ref[pl.ds(pl.multiple_of(i * 64, 64), 64), :] = y

    staged(groups * parents, produce_three, consume_three, mix_ref, LOW[2], await_next(parents, (0,)))

    def decode(i):
        last = i & (boxes - 1)
        gta = i >> log2(boxes)
        return gta >> 2, gta & 3, last

    def produce_four(i):
        tiles = fresh(LOW[3])
        g, ta, last = decode(i)
        m4 = last >> log2(fy)
        n4 = last & (fy - 1)
        for c in range(4):
            box = (2 * m4 + c // 2) * py + 2 * n4 + c % 2
            source = pl.multiple_of(((g * parents + box) * 4 + ta) * 16, 16)
            reals = doubled(z3_ref[pl.ds(source, 8), :], low_half)
            imags = doubled(z3_ref[pl.ds(source + 8, 8), :], low_half)
            for tile in range(4):
                at = ((i * 4 + c) * 4 + tile) * 2
                turn_back(reals[tile // 2], imags[tile // 2], cs4[at], cs4[at + 1], tiles, tile, c, LOW[3])
        return laid(tiles)

    def consume_four(i, y):
        g, ta, last = decode(i)
        t2 = ta >> 1
        a1 = ta & 1
        gx = g >> 1 if wide else g
        for a2 in range(2):
            for b1 in range(2):
                tile = a2 * 2 + b1
                real = y[tile * 16:tile * 16 + 8]
                imag = y[tile * 16 + 8:tile * 16 + 16]
                c, s = cs5[(i * 4 + tile) * 2], cs5[(i * 4 + tile) * 2 + 1]
                ore = real * c - imag * s
                oim = real * s + imag * c
                pair = (
                    jnp.where(low_half, ore, pltpu.roll(oim, 64, 1)),
                    jnp.where(low_half, pltpu.roll(ore, 64, 1), oim),
                )
                for b2, value in enumerate(pair):
                    inner = (4 * t2 + 2 * a2 + b2) * boxes + last

                    def at(h):
                        line = (h * piece_x + gx) * 4 + 2 * a1 + b1
                        return line * (piece_y * 8 * boxes) + inner

                    if wide:
                        out_ref[pl.ds(at(g & 1), 8, stride=8 * boxes), :] = value
                    else:
                        for h in range(2):
                            out_ref[pl.ds(at(h), 4, stride=8 * boxes), :] = value[4 * h:4 * h + 4]

    early = wide and 4 * boxes == UNROLL
    size = 4 * piece_y * 8 * boxes if early else out_hbm.shape[0]

    def leaving(k):
        if early:
            k = (k & 1) * piece_x + (k >> 1)
        rows = pl.ds(pl.multiple_of(k * size, size), size)
        return pltpu.make_async_copy(out_ref.at[rows], out_hbm.at[rows], out_sem.at[k])

    staged(groups * 4 * boxes, produce_four, consume_four, mix_ref, LOW[3],
           await_next(4 * boxes, (1, 2)), (lambda k: leaving(k).start()) if early else None)
    if not early:
        leaving(0).start()
    for k in range(groups if early else 1):
        leaving(k).wait()


def target_side(arrived, mix, phases, nx, ny, piece_x, piece_y):
    parents, boxes = (nx // 2) * (ny // 2), (nx // 4) * (ny // 4)
    groups = piece_x * (2 if piece_y == 8 else 1)
    return pl.pallas_call(
        functools.partial(target_kernel, nx, ny, piece_x, piece_y),
        in_specs=[pl.BlockSpec(memory_space=pltpu.VMEM)] * 2 + [pl.BlockSpec(memory_space=pltpu.HBM)],
        out_specs=pl.BlockSpec(memory_space=pltpu.HBM),
        out_shape=jax.ShapeDtypeStruct((2 * 4 * piece_x * 2 * 4 * piece_y * boxes, 128), jnp.float32),
        scratch_shapes=[
            pltpu.VMEM((groups * parents * 64, 128), jnp.float32),
            pltpu.VMEM(phases.shape, jnp.float32),
            pltpu.VMEM((2 * 4 * piece_x * 2 * 4 * piece_y * boxes, 128), jnp.float32),
            pltpu.SemaphoreType.DMA((3, groups)),
            pltpu.SemaphoreType.DMA((groups,)),
        ],
        compiler_params=pltpu.CompilerParams(vmem_limit_bytes=48 * 2**20),
        name="target_levels",
        cost_estimate=pl.CostEstimate(flops=2 * 10**9, bytes_accessed=2 * 2**20, transcendentals=0),
    )(arrived, mix, phases)


def to_targets(made, nx, ny, piece_x, piece_y):
    if (piece_x, piece_y) != (2, 8):
        made = made.reshape(4, 2, 4, 2, 2, 4, 2, 2, 128)
        lead = [0, 1] + ([3] if piece_x == 1 else []) + [2] + ([6] if piece_y == 4 else [])
        rest = ([3] if piece_x == 2 else []) + [4, 5] + ([6] if piece_y == 8 else []) + [7]
        made = made.transpose(lead + rest + [8])
    return made.reshape(nx * ny, -1, 128)


def on_device(weights):
    nx = lax.axis_size("sx")
    ny = lax.axis_size("sy")
    piece_x = 2 * weights.shape[0] // nx
    piece_y = 2 * weights.shape[1] // ny
    mix = jnp.asarray(mixing())
    made = to_targets(source_side(weights, mix), nx, ny, piece_x, piece_y)
    arrived = lax.all_to_all(made, ("sx", "sy"), split_axis=0, concat_axis=0, tiled=True)
    phases = phase_side(nx, ny, piece_x, piece_y)
    out = target_side(arrived, mix, phases, nx, ny, piece_x, piece_y)
    return out.reshape(2, 4 * piece_x, 2, 4 * piece_y, nx // 4, ny // 4, 128)


def solution(mesh):
    return jax.shard_map(
        on_device,
        mesh=mesh,
        in_specs=(P(None, None, "sx", "sy", None),),
        out_specs=P(None, "sx", None, "sy", None, None, None),
        check_vma=False,
    )
```

```python
import functools

import jax
import jax.numpy as jnp
import ml_dtypes
import numpy as np
from jax import lax
from jax.experimental import pallas as pl
from jax.experimental.pallas import tpu as pltpu
from jax.sharding import PartitionSpec as P

GRID = 4096
BOXES = 64

HALF_SIN = (4.442867279052734, -7.30741548538208, 3.5945212841033936, -0.7836661338806152)

EARLY = 256

UNROLL = (16, 16, 8, 16)

LOW = (True, True, True, True)

NODES = 0.5 - 0.5 * np.cos(np.pi * (2.0 * np.arange(8) + 1.0) / 16.0)


def mixing():
    def side(c):
        shifted = (c + NODES) / 2.0
        out = np.ones((8, 8))
        for i in range(8):
            for k in range(8):
                if k != i:
                    out[i] *= (shifted - NODES[k]) / (NODES[i] - NODES[k])
        return out

    rows = []
    for cx in range(2):
        for cy in range(2):
            rows.append(np.kron(np.eye(2), np.kron(side(cx), side(cy)).T))
    full = np.concatenate(rows, axis=0)
    high = full.astype(ml_dtypes.bfloat16)
    low = (full - high.astype(np.float64)).astype(ml_dtypes.bfloat16)
    return np.concatenate([high, low], axis=1)


def horner(coefs, z):
    total = coefs[-1] * z + coefs[-2]
    for c in coefs[-3::-1]:
        total = total * z + c
    return total


def sincos(cycles):
    f = cycles - jnp.round(cycles)
    h = f * horner(HALF_SIN, f * f)
    w = h * h
    d = 2.0 - w
    return h * d * lax.rsqrt(d), 1.0 - w


def sine(cycles):
    return sincos(cycles)[0]


def iotas():
    lane = lax.broadcasted_iota(jnp.int32, (8, 128), 1)
    row = lax.broadcasted_iota(jnp.int32, (8, 128), 0)
    return lane, row


def lane_nodes(lane):
    j1 = (lane >> 3) & 7
    j2 = lane & 7
    z1 = jnp.zeros((8, 128), jnp.float32)
    z2 = jnp.zeros((8, 128), jnp.float32)
    for j in range(8):
        z1 = jnp.where(j1 == j, float(NODES[j]), z1)
        z2 = jnp.where(j2 == j, float(NODES[j]), z2)
    return z1, z2


def center(index, total):
    return (index.astype(jnp.float32) + 0.5) * (1.0 / total)


def doubled(value, low_half):
    other = pltpu.roll(value, 64, 1)
    return jnp.where(low_half, value, other), jnp.where(low_half, other, value)


def turn_back(real, imag, c, s, tiles, tile, child, low):
    both = jnp.concatenate([real * c + imag * s, imag * c - real * s], axis=0)
    high = both.astype(jnp.bfloat16)
    tiles[tile][child] = high
    if low:
        tiles[4 + tile][child] = (both - high.astype(jnp.float32)).astype(jnp.bfloat16)


def fresh(low):
    return [[None] * 4 for _ in range(8 if low else 4)]


def laid(tiles):
    return jnp.concatenate([jnp.concatenate(row, axis=1) for row in tiles], axis=0)


def log2(n):
    return n.bit_length() - 1


def staged(count, produce, consume, mix_ref, low, unroll, before=None, after=None):
    def contracted(rows):
        y = jnp.dot(rows, mix_ref[...], preferred_element_type=jnp.float32)
        total = y[:64, :128] + y[:64, 128:]
        return total + y[64:, :128] if low else total

    def body(k, rows):
        if before is not None:
            before(k)
        for j in range(unroll):
            i = k * unroll + j
            y = contracted(rows)
            rows = produce(jnp.minimum(i + 1, count - 1))
            consume(i, y)
        if after is not None:
            after(k)
        return rows

    lax.fori_loop(0, count // unroll, body, produce(jnp.int32(0)))


def source_kernel(w_hbm, mix_hbm, out_hbm, amp0, amp1, q_tab, speed, shift_x, shift_y, change,
                  z1_ref, w_ref, mix_ref, out_ref, in_sem, mix_sem, out_sem):
    fetches = [
        pltpu.make_async_copy(w_hbm.at[:, a, :, b], w_ref.at[4 * a + b], in_sem.at[4 * a + b])
        for a in range(4)
        for b in range(4)
    ]
    fetches.append(pltpu.make_async_copy(mix_hbm, mix_ref, mix_sem))
    for fetch in fetches:
        fetch.start()
    lane, row = iotas()
    low_half = lane < 64
    upper = (lane >> 6) & 1
    pos_x = lax.axis_index("sx")
    pos_y = lax.axis_index("sy")
    third = 1.0 / 3.0

    z1, z2 = lane_nodes(lane)
    qx0 = [(4 * pos_x + m).astype(jnp.float32) + z1 for m in range(4)]
    qy0 = [(4 * pos_y + n).astype(jnp.float32) + z2 for n in range(4)]
    for m in range(4):
        for n in range(4):
            amp0[4 * m + n] = 64.0 * jnp.sqrt(qx0[m] * qx0[m] + qy0[n] * qy0[n])
    sign = jnp.where(low_half, -0.25, 0.25)
    for m in range(2):
        qx = (2 * pos_x + m).astype(jnp.float32) + z1
        for n in range(2):
            qy = (2 * pos_y + n).astype(jnp.float32) + z2
            amp1[2 * m + n] = 128.0 * jnp.sqrt(qx * qx + qy * qy)
            for t1 in range(2):
                q_tab[2 * (2 * m + n) + t1] = sign * qy + (0.25 * (2 * t1 - 1)) * qx

    hx = row >> 2
    hy = (row >> 1) & 1
    b_low = row & 1
    y_tabs = []
    for jb in range(4):
        column = hy * 8 + jb * 2 + b_low
        both = column * 2 + upper
        for n in range(4):
            v = (both.astype(jnp.float32) + 0.5) * 0.5 * qy0[n]
            shift_y[jb * 4 + n] = v - jnp.round(v)
        own = [sine(center(column * 2 + s2, 128)) for s2 in range(2)]
        child = [sine(center((column * 2 + s2) * 2 + upper, 256)) for s2 in range(2)]
        y_tabs.append((jnp.where(low_half, own[0], own[1]), own, child))

    def tables(i, carry):
        a_mid = i >> 1
        s1 = i & 1
        rows = (hx * 4 + a_mid) * 2 + s1
        s_x = sine(center(rows, 128))
        child_x = [sine(center(rows * 2 + t1, 256)) for t1 in range(2)]
        for m in range(4):
            v = (rows.astype(jnp.float32) + 0.5) * 0.5 * qx0[m]
            shift_x[i * 4 + m] = v - jnp.round(v)
        for jb in range(4):
            both, own, child = y_tabs[jb]
            at = (a_mid * 4 + jb) * 2 + s1
            speed[at] = (2.0 + s_x * both) * third
            for t1 in range(2):
                for s2 in range(2):
                    change[at * 4 + t1 * 2 + s2] = (child_x[t1] * child[s2] - s_x * own[s2]) * third
        return carry

    lax.fori_loop(0, 8, tables, 0)
    for fetch in fetches:
        fetch.wait()
    w_rows = w_ref.reshape(16 * 128, 128)

    def produce_one(i):
        tiles = fresh(LOW[0])
        ajb = i >> 1
        m_half = i & 1
        a_mid = ajb >> 2
        jb = ajb & 3
        for n_half in range(2):
            for cx in range(2):
                m = 2 * m_half + cx
                for cy in range(2):
                    n = 2 * n_half + cy
                    box = 4 * m + n
                    value = w_rows[pl.ds(ajb * 128 + box, 8, stride=16), :]
                    other = pltpu.roll(value, 64, 1)
                    real = jnp.where(low_half, value, other)
                    imag = jnp.where(low_half, other, value)
                    amp = amp0[box]
                    for s1 in range(2):
                        shift = shift_x[(a_mid * 2 + s1) * 4 + m] + shift_y[jb * 4 + n]
                        cycles = speed[ajb * 2 + s1] * amp + shift
                        s, c = sincos(cycles)
                        turn_back(real, imag, c, s, tiles, n_half * 2 + s1, 2 * cx + cy, LOW[0])
        return laid(tiles)

    def consume_one(i, y):
        z1_ref[pl.ds(pl.multiple_of(i * 64, 64), 64), :] = y

    staged(32, produce_one, consume_one, mix_ref, LOW[0], UNROLL[0])

    def produce_two(i):
        tiles = fresh(LOW[1])
        s1 = i & 1
        ajb = i >> 1
        for c in range(4):
            source = pl.multiple_of(((ajb * 4 + c) * 2 + s1) * 16, 16)
            reals = doubled(z1_ref[pl.ds(source, 8), :], low_half)
            imags = doubled(z1_ref[pl.ds(source + 8, 8), :], low_half)
            amp = amp1[c]
            for t1 in range(2):
                lin = q_tab[2 * c + t1]
                for s2 in range(2):
                    cycles = change[i * 4 + t1 * 2 + s2] * amp + lin
                    sin, cos = sincos(cycles)
                    turn_back(reals[s2], imags[s2], cos, sin, tiles, t1 * 2 + s2, c, LOW[1])
        return laid(tiles)

    def consume_two(i, y):
        s1 = i & 1
        ajb = i >> 1
        base = pl.multiple_of((((ajb >> 2) * 2 + s1) * 4 + (ajb & 3)) * 64, 64)
        for t1 in range(2):
            for s2 in range(2):
                tile = (t1 * 2 + s2) * 16
                for part in range(2):
                    at = base + (t1 * 32 + part * 16 + s2)
                    out_ref[pl.ds(at, 8, stride=2), :] = y[tile + 8 * part:tile + 8 * part + 8]

    def leaving(k):
        size = 64 * UNROLL[1]
        rows = pl.ds(pl.multiple_of(k * size, size), size)
        return pltpu.make_async_copy(out_ref.at[rows], out_hbm.at[rows], out_sem.at[k])

    staged(32, produce_two, consume_two, mix_ref, LOW[1], UNROLL[1],
           after=lambda k: leaving(k).start())
    for k in range(32 // UNROLL[1]):
        leaving(k).wait()


def tab(n):
    return pltpu.VMEM((n, 8, 128), jnp.float32)


def source_side(weights, mix):
    pieces = weights.reshape(2, 4, 2, 4, 2, 16, 128)
    return pl.pallas_call(
        source_kernel,
        in_specs=[pl.BlockSpec(memory_space=pltpu.HBM)] * 2,
        out_specs=pl.BlockSpec(memory_space=pltpu.HBM),
        out_shape=jax.ShapeDtypeStruct((2048, 128), jnp.float32),
        scratch_shapes=[
            tab(16), tab(4), tab(8), tab(32), tab(32), tab(16), tab(128),
            pltpu.VMEM((2048, 128), jnp.float32),
            pltpu.VMEM((16, 2, 2, 2, 16, 128), jnp.float32),
            pltpu.VMEM((512, 256), jnp.bfloat16),
            pltpu.VMEM((2048, 128), jnp.float32),
            pltpu.SemaphoreType.DMA((16,)),
            pltpu.SemaphoreType.DMA,
            pltpu.SemaphoreType.DMA((4,)),
        ],
        name="source_levels",
        cost_estimate=pl.CostEstimate(flops=2 * 10**9, bytes_accessed=2 * 2**20, transcendentals=0),
    )(pieces, mix)


def group_bits(nx, ny, piece_x, piece_y):
    return nx // 2, ny // 2, nx // 4, ny // 4, piece_y == 8, piece_x * (2 if piece_y == 8 else 1)


def ranges(ref, items):
    return (ref.at[pl.ds(0, 32 * items)], ref.at[pl.ds(32 * items, 32 * items)],
            ref.at[pl.ds(64 * items, 8 * items)])


def phase_kernel(nx, ny, piece_x, piece_y, out_ref, early_ref,
                 amp2, lin2, amp3, lin3, amp4, change3, change4, speed4):
    px, py, fx, fy, wide, groups = group_bits(nx, ny, piece_x, piece_y)
    parents, boxes = px * py, fx * fy
    items = groups * parents
    cs3, cs4, cs5 = ranges(out_ref, items)
    lane, row = iotas()
    low_half = lane < 64
    upper = (lane >> 6) & 1
    pos_x = lax.axis_index("sx")
    pos_y = lax.axis_index("sy")
    sign = jnp.where(low_half, -0.25, 0.25)
    third = 1.0 / 3.0
    z1, z2 = lane_nodes(lane)

    def box_tables(count_x, count_y, scale, amp, lin):
        qys = [float(n) + z2 for n in range(count_y)]

        def one(m, carry):
            qx = m.astype(jnp.float32) + z1
            for n, qy in enumerate(qys):
                box = m * count_y + n
                amp[box] = scale * jnp.sqrt(qx * qx + qy * qy)
                if lin is not None:
                    lin[2 * box] = sign * qy - 0.25 * qx
                    lin[2 * box + 1] = sign * qy + 0.25 * qx
            return carry

        lax.fori_loop(0, count_x, one, 0)

    box_tables(nx, ny, 256.0, amp2, lin2)
    box_tables(px, py, 512.0, amp3, lin3)
    box_tables(fx, fy, 1024.0, amp4, None)

    if wide:
        hy = row >> 2
        k = row & 3
    else:
        hy = (row >> 1) & 1
        k = row & 1
    cols2 = hy * 32 + pos_y * piece_y + 2 * k

    def rows2(g):
        if wide:
            return jnp.full((8, 128), (g & 1) * 16 + pos_x * piece_x + (g >> 1), jnp.int32)
        return (row >> 2) * 16 + pos_x * piece_x + g

    y_tabs = []
    for t2 in range(2):
        s_y2 = sine(center(cols2 + t2, 256))
        own = [sine(center(2 * (cols2 + t2) + a2, 512)) for a2 in range(2)]
        last = [sine(center(4 * (cols2 + t2) + 2 * a2 + upper, 1024)) for a2 in range(2)]
        y_tabs.append((s_y2, jnp.where(low_half, own[0], own[1]), own, last))

    def target_tables(g, carry):
        rows = rows2(g)
        s_x2 = sine(center(rows, 256))
        for a1 in range(2):
            x3 = sine(center(2 * rows + a1, 512))
            x4 = [sine(center(4 * rows + 2 * a1 + b1, 1024)) for b1 in range(2)]
            for t2 in range(2):
                s_y2, y3, own, last = y_tabs[t2]
                ta = 2 * t2 + a1
                change3[g * 4 + ta] = (x3 * y3 - s_x2 * s_y2) * third
                for a2 in range(2):
                    for b1 in range(2):
                        at = (g * 4 + ta) * 4 + a2 * 2 + b1
                        product = x4[b1] * last[a2]
                        change4[at] = (product - x3 * own[a2]) * third
                        speed4[at] = (2.0 + product) * third
        return carry

    lax.fori_loop(0, groups, target_tables, 0)

    def put(ref, at, cycles):
        s, c = sincos(cycles)
        ref[at] = c
        ref[at + 1] = s

    def phases_three(i, carry):
        g = i >> log2(parents)
        parent = i & (parents - 1)
        m3 = parent >> log2(py)
        n3 = parent & (py - 1)
        for c in range(4):
            box = (2 * m3 + c // 2) * ny + 2 * n3 + c % 2
            for ta in range(4):
                cycles = change3[g * 4 + ta] * amp2[box] + lin2[2 * box + ta % 2]
                put(cs3, ((i * 4 + c) * 4 + ta) * 2, cycles)
        return carry

    lax.fori_loop(0, groups * parents, phases_three, 0)

    def early(i, carry):
        early_ref[pl.ds(i * 8, 8)] = cs3[pl.ds(i * 8, 8)]
        return carry

    lax.fori_loop(0, early_ref.shape[0] // 8, early, 0)

    def phases_four(i, carry):
        last = i & (boxes - 1)
        gta = i >> log2(boxes)
        g = gta >> 2
        t2 = (gta >> 1) & 1
        a1 = gta & 1
        m4 = last >> log2(fy)
        n4 = last & (fy - 1)
        p1 = m4.astype(jnp.float32) + z1
        p2 = n4.astype(jnp.float32) + z2
        rows = rows2(g) * 4 + 2 * a1
        for tile in range(4):
            a2, b1 = tile // 2, tile % 2
            for c in range(4):
                box = (2 * m4 + c // 2) * py + 2 * n4 + c % 2
                cycles = change4[gta * 4 + tile] * amp3[box] + lin3[2 * box + b1]
                put(cs4, ((i * 4 + c) * 4 + tile) * 2, cycles)
            col = (4 * (cols2 + t2) + 2 * a2 + upper).astype(jnp.float32) + 0.5
            r4 = (rows + b1).astype(jnp.float32) + 0.5
            put(cs5, (i * 4 + tile) * 2, speed4[gta * 4 + tile] * amp4[last] + (r4 * p1 + col * p2))
        return carry

    lax.fori_loop(0, groups * 4 * boxes, phases_four, 0)


def phase_side(nx, ny, piece_x, piece_y):
    px, py, fx, fy, wide, groups = group_bits(nx, ny, piece_x, piece_y)
    parents, boxes = px * py, fx * fy
    items = groups * parents
    return pl.pallas_call(
        functools.partial(phase_kernel, nx, ny, piece_x, piece_y),
        out_specs=[pl.BlockSpec(memory_space=pltpu.VMEM)] * 2,
        out_shape=[jax.ShapeDtypeStruct((72 * items, 8, 128), jnp.float32),
                   pltpu.VMEM((EARLY, 8, 128), jnp.float32)],
        scratch_shapes=[
            tab(nx * ny), tab(2 * nx * ny), tab(parents), tab(2 * parents), tab(boxes),
            tab(groups * 4), tab(groups * 16), tab(groups * 16),
        ],
        name="phases",
        cost_estimate=pl.CostEstimate(flops=2 * 10**9, bytes_accessed=9 * 2**20, transcendentals=0),
    )()


def target_kernel(nx, ny, piece_x, piece_y, w_ref, mix_ref, early_ref, cs_hbm, out_hbm,
                  z3_ref, cs_ref, out_ref, in_sem, out_sem):
    px, py, fx, fy, wide, groups = group_bits(nx, ny, piece_x, piece_y)
    parents, boxes = px * py, fx * fy
    low_half = iotas()[0] < 64

    comes = ranges(cs_hbm, groups * parents)
    cs3, cs4, cs5 = kept = ranges(cs_ref, groups * parents)

    def coming(which, g):
        source, target = comes[which], kept[which]
        part = source.shape[0] // groups
        rows = pl.ds(g * part, part)
        return pltpu.make_async_copy(source.at[rows], target.at[rows], in_sem.at[which, g])

    for g in range(1, groups):
        coming(0, g).start()
    for g in range(groups):
        coming(1, g).start()
        coming(2, g).start()
    head = 32 * parents
    if head > EARLY:
        rest = pl.ds(EARLY, head - EARLY)
        filling = pltpu.make_async_copy(comes[0].at[rest], cs3.at[rest], in_sem.at[0, 0])
        filling.start()

    def early(i, carry):
        cs3[pl.ds(i * 8, 8)] = early_ref[pl.ds(i * 8, 8)]
        return carry

    lax.fori_loop(0, EARLY // 8, early, 0)
    if head > EARLY:
        filling.wait()

    def await_next(per_group, unroll, parts):
        stepwise = unroll % per_group == 0
        for which in parts:
            for g in range(1 if stepwise else groups):
                if (which, g) != (0, 0):
                    coming(which, g).wait()
        if not stepwise:
            return None
        each = unroll // per_group

        def before(k):
            for n in range(1, each + 1):

                @pl.when(k * each + n < groups)
                def _():
                    for which in parts:
                        coming(which, k * each + n).wait()

        return before

    def arrived(box, g, part):
        if wide:
            at = (((g >> 1) * 2 + part) * 2 + (g & 1)) * 8
        else:
            at = (g * 2 + part) * 8
        return w_ref[box, pl.ds(pl.multiple_of(at, 8), 8), :]

    def produce_three(i):
        tiles = fresh(LOW[2])
        g = i >> log2(parents)
        parent = i & (parents - 1)
        m3 = parent >> log2(py)
        n3 = parent & (py - 1)
        for c in range(4):
            box = (2 * m3 + c // 2) * ny + 2 * n3 + c % 2
            reals = doubled(arrived(box, g, 0), low_half)
            imags = doubled(arrived(box, g, 1), low_half)
            for ta in range(4):
                at = ((i * 4 + c) * 4 + ta) * 2
                turn_back(reals[ta // 2], imags[ta // 2], cs3[at], cs3[at + 1], tiles, ta, c, LOW[2])
        return laid(tiles)

    def consume_three(i, y):
        z3_ref[pl.ds(pl.multiple_of(i * 64, 64), 64), :] = y

    staged(groups * parents, produce_three, consume_three, mix_ref, LOW[2], UNROLL[2],
           await_next(parents, UNROLL[2], (0,)))

    def decode(i):
        last = i & (boxes - 1)
        gta = i >> log2(boxes)
        return gta >> 2, gta & 3, last

    def produce_four(i):
        tiles = fresh(LOW[3])
        g, ta, last = decode(i)
        m4 = last >> log2(fy)
        n4 = last & (fy - 1)
        for c in range(4):
            box = (2 * m4 + c // 2) * py + 2 * n4 + c % 2
            source = pl.multiple_of(((g * parents + box) * 4 + ta) * 16, 16)
            reals = doubled(z3_ref[pl.ds(source, 8), :], low_half)
            imags = doubled(z3_ref[pl.ds(source + 8, 8), :], low_half)
            for tile in range(4):
                at = ((i * 4 + c) * 4 + tile) * 2
                turn_back(reals[tile // 2], imags[tile // 2], cs4[at], cs4[at + 1], tiles, tile, c, LOW[3])
        return laid(tiles)

    def consume_four(i, y):
        g, ta, last = decode(i)
        t2 = ta >> 1
        a1 = ta & 1
        gx = g >> 1 if wide else g
        for a2 in range(2):
            for b1 in range(2):
                tile = a2 * 2 + b1
                real = y[tile * 16:tile * 16 + 8]
                imag = y[tile * 16 + 8:tile * 16 + 16]
                c, s = cs5[(i * 4 + tile) * 2], cs5[(i * 4 + tile) * 2 + 1]
                ore = real * c - imag * s
                oim = real * s + imag * c
                pair = (
                    jnp.where(low_half, ore, pltpu.roll(oim, 64, 1)),
                    jnp.where(low_half, pltpu.roll(ore, 64, 1), oim),
                )
                for b2, value in enumerate(pair):
                    inner = (4 * t2 + 2 * a2 + b2) * boxes + last

                    def at(h):
                        line = (h * piece_x + gx) * 4 + 2 * a1 + b1
                        return line * (piece_y * 8 * boxes) + inner

                    if wide:
                        out_ref[pl.ds(at(g & 1), 8, stride=8 * boxes), :] = value
                    else:
                        for h in range(2):
                            out_ref[pl.ds(at(h), 4, stride=8 * boxes), :] = value[4 * h:4 * h + 4]

    each = UNROLL[3] // (4 * boxes)
    early = wide and UNROLL[3] % (4 * boxes) == 0
    size = 4 * piece_y * 8 * boxes if early else out_hbm.shape[0]

    def leaving(k):
        if early:
            k = (k & 1) * piece_x + (k >> 1)
        rows = pl.ds(pl.multiple_of(k * size, size), size)
        return pltpu.make_async_copy(out_ref.at[rows], out_hbm.at[rows], out_sem.at[k])

    def leave_trip(k):
        for n in range(each):
            leaving(k * each + n).start()

    staged(groups * 4 * boxes, produce_four, consume_four, mix_ref, LOW[3], UNROLL[3],
           await_next(4 * boxes, UNROLL[3], (1, 2)), leave_trip if early else None)
    if not early:
        leaving(0).start()
    for k in range(groups if early else 1):
        leaving(k).wait()


def target_side(arrived, mix, phases, nx, ny, piece_x, piece_y):
    parents, boxes = (nx // 2) * (ny // 2), (nx // 4) * (ny // 4)
    groups = piece_x * (2 if piece_y == 8 else 1)
    return pl.pallas_call(
        functools.partial(target_kernel, nx, ny, piece_x, piece_y),
        in_specs=[pl.BlockSpec(memory_space=pltpu.VMEM)] * 3 + [pl.BlockSpec(memory_space=pltpu.HBM)],
        out_specs=pl.BlockSpec(memory_space=pltpu.HBM),
        out_shape=jax.ShapeDtypeStruct((2 * 4 * piece_x * 2 * 4 * piece_y * boxes, 128), jnp.float32),
        scratch_shapes=[
            pltpu.VMEM((groups * parents * 64, 128), jnp.float32),
            pltpu.VMEM(phases[0].shape, jnp.float32),
            pltpu.VMEM((2 * 4 * piece_x * 2 * 4 * piece_y * boxes, 128), jnp.float32),
            pltpu.SemaphoreType.DMA((3, groups)),
            pltpu.SemaphoreType.DMA((groups,)),
        ],
        compiler_params=pltpu.CompilerParams(vmem_limit_bytes=48 * 2**20),
        name="target_levels",
        cost_estimate=pl.CostEstimate(flops=2 * 10**9, bytes_accessed=2 * 2**20, transcendentals=0),
    )(arrived, mix, phases[1], phases[0])


def to_targets(made, nx, ny, piece_x, piece_y):
    if (piece_x, piece_y) != (2, 8):
        made = made.reshape(4, 2, 4, 2, 2, 4, 2, 2, 128)
        lead = [0, 1] + ([3] if piece_x == 1 else []) + [2] + ([6] if piece_y == 4 else [])
        rest = ([3] if piece_x == 2 else []) + [4, 5] + ([6] if piece_y == 8 else []) + [7]
        made = made.transpose(lead + rest + [8])
    return made.reshape(nx * ny, -1, 128)


def on_device(weights):
    nx = lax.axis_size("sx")
    ny = lax.axis_size("sy")
    piece_x = 2 * weights.shape[0] // nx
    piece_y = 2 * weights.shape[1] // ny
    mix = jnp.asarray(mixing())
    made = to_targets(source_side(weights, mix), nx, ny, piece_x, piece_y)
    arrived = lax.all_to_all(made, ("sx", "sy"), split_axis=0, concat_axis=0, tiled=True)
    phases = phase_side(nx, ny, piece_x, piece_y)
    out = target_side(arrived, mix, phases, nx, ny, piece_x, piece_y)
    return out.reshape(2, 4 * piece_x, 2, 4 * piece_y, nx // 4, ny // 4, 128)


def solution(mesh):
    return jax.shard_map(
        on_device,
        mesh=mesh,
        in_specs=(P(None, None, "sx", "sy", None),),
        out_specs=P(None, "sx", None, "sy", None, None, None),
        check_vma=False,
    )
```

```python
import functools

import jax
import jax.numpy as jnp
import ml_dtypes
import numpy as np
from jax import lax
from jax.experimental import pallas as pl
from jax.experimental.pallas import tpu as pltpu
from jax.sharding import PartitionSpec as P

GRID = 4096
BOXES = 64

HALF_SIN = (4.442867279052734, -7.30741548538208, 3.5945212841033936, -0.7836661338806152)

EARLY = 256

UNROLL = (16, 16, 8, 16)

LOW = (True, True, True, True)

NODES = 0.5 - 0.5 * np.cos(np.pi * (2.0 * np.arange(8) + 1.0) / 16.0)


def mixing():
    def side(c):
        shifted = (c + NODES) / 2.0
        out = np.ones((8, 8))
        for i in range(8):
            for k in range(8):
                if k != i:
                    out[i] *= (shifted - NODES[k]) / (NODES[i] - NODES[k])
        return out

    rows = []
    for cx in range(2):
        for cy in range(2):
            rows.append(np.kron(np.eye(2), np.kron(side(cx), side(cy)).T))
    full = np.concatenate(rows, axis=0)
    high = full.astype(ml_dtypes.bfloat16)
    low = (full - high.astype(np.float64)).astype(ml_dtypes.bfloat16)
    return np.concatenate([high, low], axis=1)


def horner(coefs, z):
    total = coefs[-1] * z + coefs[-2]
    for c in coefs[-3::-1]:
        total = total * z + c
    return total


def sincos(cycles):
    f = cycles - jnp.round(cycles)
    h = f * horner(HALF_SIN, f * f)
    w = h * h
    d = 2.0 - w
    return h * d * lax.rsqrt(d), 1.0 - w


def sine(cycles):
    return sincos(cycles)[0]


def iotas():
    lane = lax.broadcasted_iota(jnp.int32, (8, 128), 1)
    row = lax.broadcasted_iota(jnp.int32, (8, 128), 0)
    return lane, row


def lane_nodes(lane):
    j1 = (lane >> 3) & 7
    j2 = lane & 7
    z1 = jnp.zeros((8, 128), jnp.float32)
    z2 = jnp.zeros((8, 128), jnp.float32)
    for j in range(8):
        z1 = jnp.where(j1 == j, float(NODES[j]), z1)
        z2 = jnp.where(j2 == j, float(NODES[j]), z2)
    return z1, z2


def center(index, total):
    return (index.astype(jnp.float32) + 0.5) * (1.0 / total)


def doubled(value, low_half):
    other = pltpu.roll(value, 64, 1)
    return jnp.where(low_half, value, other), jnp.where(low_half, other, value)


def turn_back(real, imag, c, s, tiles, tile, child, low):
    both = jnp.concatenate([real * c + imag * s, imag * c - real * s], axis=0)
    high = both.astype(jnp.bfloat16)
    tiles[tile][child] = high
    if low:
        tiles[4 + tile][child] = (both - high.astype(jnp.float32)).astype(jnp.bfloat16)


def fresh(low):
    return [[None] * 4 for _ in range(8 if low else 4)]


def laid(tiles):
    return jnp.concatenate([jnp.concatenate(row, axis=1) for row in tiles], axis=0)


def log2(n):
    return n.bit_length() - 1


def staged(count, produce, consume, mix_ref, low, unroll, before=None, after=None):
    def contracted(rows):
        y = jnp.dot(rows, mix_ref[...], preferred_element_type=jnp.float32)
        total = y[:64, :128] + y[:64, 128:]
        return total + y[64:, :128] if low else total

    def body(k, rows):
        if before is not None:
            before(k)
        for j in range(unroll):
            i = k * unroll + j
            y = contracted(rows)
            rows = produce(jnp.minimum(i + 1, count - 1))
            consume(i, y)
        if after is not None:
            after(k)
        return rows

    lax.fori_loop(0, count // unroll, body, produce(jnp.int32(0)))


def source_kernel(w_hbm, mix_hbm, out_hbm, amp0, amp1, q_tab, speed, shift_x, shift_y, change,
                  z1_ref, w_ref, mix_ref, out_ref, in_sem, mix_sem, out_sem):
    fetches = [
        pltpu.make_async_copy(w_hbm.at[:, a, :, b], w_ref.at[4 * a + b], in_sem.at[4 * a + b])
        for a in range(4)
        for b in range(4)
    ]
    fetches.append(pltpu.make_async_copy(mix_hbm, mix_ref, mix_sem))
    for fetch in fetches:
        fetch.start()
    lane, row = iotas()
    low_half = lane < 64
    upper = (lane >> 6) & 1
    pos_x = lax.axis_index("sx")
    pos_y = lax.axis_index("sy")
    third = 1.0 / 3.0

    z1, z2 = lane_nodes(lane)
    qx0 = [(4 * pos_x + m).astype(jnp.float32) + z1 for m in range(4)]
    qy0 = [(4 * pos_y + n).astype(jnp.float32) + z2 for n in range(4)]
    for m in range(4):
        for n in range(4):
            amp0[4 * m + n] = 64.0 * jnp.sqrt(qx0[m] * qx0[m] + qy0[n] * qy0[n])
    sign = jnp.where(low_half, -0.25, 0.25)
    for m in range(2):
        qx = (2 * pos_x + m).astype(jnp.float32) + z1
        for n in range(2):
            qy = (2 * pos_y + n).astype(jnp.float32) + z2
            amp1[2 * m + n] = 128.0 * jnp.sqrt(qx * qx + qy * qy)
            for t1 in range(2):
                q_tab[2 * (2 * m + n) + t1] = sign * qy + (0.25 * (2 * t1 - 1)) * qx

    hx = row >> 2
    hy = (row >> 1) & 1
    b_low = row & 1
    y_tabs = []
    for jb in range(4):
        column = hy * 8 + jb * 2 + b_low
        both = column * 2 + upper
        for n in range(4):
            v = (both.astype(jnp.float32) + 0.5) * 0.5 * qy0[n]
            shift_y[jb * 4 + n] = v - jnp.round(v)
        own = [sine(center(column * 2 + s2, 128)) for s2 in range(2)]
        child = [sine(center((column * 2 + s2) * 2 + upper, 256)) for s2 in range(2)]
        y_tabs.append((jnp.where(low_half, own[0], own[1]), own, child))

    def tables(i, carry):
        a_mid = i >> 1
        s1 = i & 1
        rows = (hx * 4 + a_mid) * 2 + s1
        s_x = sine(center(rows, 128))
        child_x = [sine(center(rows * 2 + t1, 256)) for t1 in range(2)]
        for m in range(4):
            v = (rows.astype(jnp.float32) + 0.5) * 0.5 * qx0[m]
            shift_x[i * 4 + m] = v - jnp.round(v)
        for jb in range(4):
            both, own, child = y_tabs[jb]
            at = (a_mid * 4 + jb) * 2 + s1
            speed[at] = (2.0 + s_x * both) * third
            for t1 in range(2):
                for s2 in range(2):
                    change[at * 4 + t1 * 2 + s2] = (child_x[t1] * child[s2] - s_x * own[s2]) * third
        return carry

    lax.fori_loop(0, 8, tables, 0)
    for fetch in fetches:
        fetch.wait()
    w_rows = w_ref.reshape(17 * 128, 128)

    def produce_one(i):
        tiles = fresh(LOW[0])
        ajb = i >> 1
        m_half = i & 1
        a_mid = ajb >> 2
        jb = ajb & 3
        for n_half in range(2):
            for cx in range(2):
                m = 2 * m_half + cx
                for cy in range(2):
                    n = 2 * n_half + cy
                    box = 4 * m + n
                    value = w_rows[pl.ds(ajb * 128 + box, 8, stride=16), :]
                    other = pltpu.roll(value, 64, 1)
                    real = jnp.where(low_half, value, other)
                    imag = jnp.where(low_half, other, value)
                    amp = amp0[box]
                    for s1 in range(2):
                        shift = shift_x[(a_mid * 2 + s1) * 4 + m] + shift_y[jb * 4 + n]
                        cycles = speed[ajb * 2 + s1] * amp + shift
                        s, c = sincos(cycles)
                        turn_back(real, imag, c, s, tiles, n_half * 2 + s1, 2 * cx + cy, LOW[0])
        return laid(tiles)

    def consume_one(i, y):
        z1_ref[pl.ds(pl.multiple_of(i * 64, 64), 64), :] = y

    staged(32, produce_one, consume_one, mix_ref, LOW[0], UNROLL[0])

    def produce_two(i):
        tiles = fresh(LOW[1])
        s1 = i & 1
        ajb = i >> 1
        for c in range(4):
            source = pl.multiple_of(((ajb * 4 + c) * 2 + s1) * 16, 16)
            reals = doubled(z1_ref[pl.ds(source, 8), :], low_half)
            imags = doubled(z1_ref[pl.ds(source + 8, 8), :], low_half)
            amp = amp1[c]
            for t1 in range(2):
                lin = q_tab[2 * c + t1]
                for s2 in range(2):
                    cycles = change[i * 4 + t1 * 2 + s2] * amp + lin
                    sin, cos = sincos(cycles)
                    turn_back(reals[s2], imags[s2], cos, sin, tiles, t1 * 2 + s2, c, LOW[1])
        return laid(tiles)

    def consume_two(i, y):
        s1 = i & 1
        ajb = i >> 1
        base = pl.multiple_of((((ajb >> 2) * 2 + s1) * 4 + (ajb & 3)) * 64, 64)
        for t1 in range(2):
            for s2 in range(2):
                tile = (t1 * 2 + s2) * 16
                for part in range(2):
                    at = base + (t1 * 32 + part * 16 + s2)
                    out_ref[pl.ds(at, 8, stride=2), :] = y[tile + 8 * part:tile + 8 * part + 8]

    def leaving(k):
        size = 64 * UNROLL[1]
        rows = pl.ds(pl.multiple_of(k * size, size), size)
        return pltpu.make_async_copy(out_ref.at[rows], out_hbm.at[rows], out_sem.at[k])

    staged(32, produce_two, consume_two, mix_ref, LOW[1], UNROLL[1],
           after=lambda k: leaving(k).start())
    for k in range(32 // UNROLL[1]):
        leaving(k).wait()


def tab(n):
    return pltpu.VMEM((n, 8, 128), jnp.float32)


def source_side(weights, mix):
    pieces = weights.reshape(2, 4, 2, 4, 2, 16, 128)
    return pl.pallas_call(
        source_kernel,
        in_specs=[pl.BlockSpec(memory_space=pltpu.HBM)] * 2,
        out_specs=pl.BlockSpec(memory_space=pltpu.HBM),
        out_shape=jax.ShapeDtypeStruct((2048, 128), jnp.float32),
        scratch_shapes=[
            tab(16), tab(4), tab(8), tab(32), tab(32), tab(16), tab(128),
            pltpu.VMEM((2048, 128), jnp.float32),
            pltpu.VMEM((17, 2, 2, 2, 16, 128), jnp.float32),
            pltpu.VMEM((512, 256), jnp.bfloat16),
            pltpu.VMEM((2064, 128), jnp.float32),
            pltpu.SemaphoreType.DMA((16,)),
            pltpu.SemaphoreType.DMA,
            pltpu.SemaphoreType.DMA((4,)),
        ],
        name="source_levels",
        cost_estimate=pl.CostEstimate(flops=2 * 10**9, bytes_accessed=2 * 2**20, transcendentals=0),
    )(pieces, mix)


def group_bits(nx, ny, piece_x, piece_y):
    return nx // 2, ny // 2, nx // 4, ny // 4, piece_y == 8, piece_x * (2 if piece_y == 8 else 1)


def ranges(ref, items):
    return ref.at[pl.ds(0, 32 * items)], ref.at[pl.ds(32 * items, 32 * items)]


def phase_kernel(nx, ny, piece_x, piece_y, out_ref, early_ref, cs5,
                 amp2, lin2, amp3, lin3, amp4, change3, change4, speed4):
    px, py, fx, fy, wide, groups = group_bits(nx, ny, piece_x, piece_y)
    parents, boxes = px * py, fx * fy
    items = groups * parents
    cs3, cs4 = ranges(out_ref, items)
    lane, row = iotas()
    low_half = lane < 64
    upper = (lane >> 6) & 1
    pos_x = lax.axis_index("sx")
    pos_y = lax.axis_index("sy")
    sign = jnp.where(low_half, -0.25, 0.25)
    third = 1.0 / 3.0
    z1, z2 = lane_nodes(lane)

    def box_tables(count_x, count_y, scale, amp, lin):
        qys = [float(n) + z2 for n in range(count_y)]

        def one(m, carry):
            qx = m.astype(jnp.float32) + z1
            for n, qy in enumerate(qys):
                box = m * count_y + n
                amp[box] = scale * jnp.sqrt(qx * qx + qy * qy)
                if lin is not None:
                    lin[2 * box] = sign * qy - 0.25 * qx
                    lin[2 * box + 1] = sign * qy + 0.25 * qx
            return carry

        lax.fori_loop(0, count_x, one, 0)

    box_tables(nx, ny, 256.0, amp2, lin2)
    box_tables(px, py, 512.0, amp3, lin3)
    box_tables(fx, fy, 1024.0, amp4, None)

    if wide:
        hy = row >> 2
        k = row & 3
    else:
        hy = (row >> 1) & 1
        k = row & 1
    cols2 = hy * 32 + pos_y * piece_y + 2 * k

    def rows2(g):
        if wide:
            return jnp.full((8, 128), (g & 1) * 16 + pos_x * piece_x + (g >> 1), jnp.int32)
        return (row >> 2) * 16 + pos_x * piece_x + g

    y_tabs = []
    for t2 in range(2):
        s_y2 = sine(center(cols2 + t2, 256))
        own = [sine(center(2 * (cols2 + t2) + a2, 512)) for a2 in range(2)]
        last = [sine(center(4 * (cols2 + t2) + 2 * a2 + upper, 1024)) for a2 in range(2)]
        y_tabs.append((s_y2, jnp.where(low_half, own[0], own[1]), own, last))

    def target_tables(g, carry):
        rows = rows2(g)
        s_x2 = sine(center(rows, 256))
        for a1 in range(2):
            x3 = sine(center(2 * rows + a1, 512))
            x4 = [sine(center(4 * rows + 2 * a1 + b1, 1024)) for b1 in range(2)]
            for t2 in range(2):
                s_y2, y3, own, last = y_tabs[t2]
                ta = 2 * t2 + a1
                change3[g * 4 + ta] = (x3 * y3 - s_x2 * s_y2) * third
                for a2 in range(2):
                    for b1 in range(2):
                        at = (g * 4 + ta) * 4 + a2 * 2 + b1
                        product = x4[b1] * last[a2]
                        change4[at] = (product - x3 * own[a2]) * third
                        speed4[at] = (2.0 + product) * third
        return carry

    lax.fori_loop(0, groups, target_tables, 0)

    def put(ref, at, cycles):
        s, c = sincos(cycles)
        ref[at] = c
        ref[at + 1] = s

    def phases_three(i, carry):
        g = i >> log2(parents)
        parent = i & (parents - 1)
        m3 = parent >> log2(py)
        n3 = parent & (py - 1)
        for c in range(4):
            box = (2 * m3 + c // 2) * ny + 2 * n3 + c % 2
            for ta in range(4):
                cycles = change3[g * 4 + ta] * amp2[box] + lin2[2 * box + ta % 2]
                put(cs3, ((i * 4 + c) * 4 + ta) * 2, cycles)
        return carry

    lax.fori_loop(0, groups * parents, phases_three, 0)

    def early(i, carry):
        early_ref[pl.ds(i * 8, 8)] = cs3[pl.ds(i * 8, 8)]
        return carry

    lax.fori_loop(0, early_ref.shape[0] // 8, early, 0)

    def phases_four(i, carry):
        last = i & (boxes - 1)
        gta = i >> log2(boxes)
        g = gta >> 2
        t2 = (gta >> 1) & 1
        a1 = gta & 1
        m4 = last >> log2(fy)
        n4 = last & (fy - 1)
        p1 = m4.astype(jnp.float32) + z1
        p2 = n4.astype(jnp.float32) + z2
        rows = rows2(g) * 4 + 2 * a1
        for tile in range(4):
            a2, b1 = tile // 2, tile % 2
            for c in range(4):
                box = (2 * m4 + c // 2) * py + 2 * n4 + c % 2
                cycles = change4[gta * 4 + tile] * amp3[box] + lin3[2 * box + b1]
                put(cs4, ((i * 4 + c) * 4 + tile) * 2, cycles)
            col = (4 * (cols2 + t2) + 2 * a2 + upper).astype(jnp.float32) + 0.5
            r4 = (rows + b1).astype(jnp.float32) + 0.5
            put(cs5, (i * 4 + tile) * 2, speed4[gta * 4 + tile] * amp4[last] + (r4 * p1 + col * p2))
        return carry

    lax.fori_loop(0, groups * 4 * boxes, phases_four, 0)


def phase_side(nx, ny, piece_x, piece_y):
    px, py, fx, fy, wide, groups = group_bits(nx, ny, piece_x, piece_y)
    parents, boxes = px * py, fx * fy
    items = groups * parents
    return pl.pallas_call(
        functools.partial(phase_kernel, nx, ny, piece_x, piece_y),
        out_specs=[pl.BlockSpec(memory_space=pltpu.VMEM)] * 3,
        out_shape=[jax.ShapeDtypeStruct((64 * items, 8, 128), jnp.float32),
                   pltpu.VMEM((EARLY, 8, 128), jnp.float32),
                   pltpu.VMEM((8 * items, 8, 128), jnp.float32)],
        scratch_shapes=[
            tab(nx * ny), tab(2 * nx * ny), tab(parents), tab(2 * parents), tab(boxes),
            tab(groups * 4), tab(groups * 16), tab(groups * 16),
        ],
        name="phases",
        cost_estimate=pl.CostEstimate(flops=2 * 10**9, bytes_accessed=9 * 2**20, transcendentals=0),
    )()


def target_kernel(nx, ny, piece_x, piece_y, w_ref, mix_ref, early_ref, cs5, cs_hbm, out_hbm,
                  z3_ref, cs_ref, out_ref, in_sem, out_sem):
    px, py, fx, fy, wide, groups = group_bits(nx, ny, piece_x, piece_y)
    parents, boxes = px * py, fx * fy
    low_half = iotas()[0] < 64

    comes = ranges(cs_hbm, groups * parents)
    cs3, cs4 = kept = ranges(cs_ref, groups * parents)

    def coming(which, g):
        source, target = comes[which], kept[which]
        part = source.shape[0] // groups
        rows = pl.ds(g * part, part)
        return pltpu.make_async_copy(source.at[rows], target.at[rows], in_sem.at[which, g])

    for g in range(1, groups):
        coming(0, g).start()
    for g in range(groups):
        coming(1, g).start()
    head = 32 * parents
    if head > EARLY:
        rest = pl.ds(EARLY, head - EARLY)
        filling = pltpu.make_async_copy(comes[0].at[rest], cs3.at[rest], in_sem.at[0, 0])
        filling.start()

    def early(i, carry):
        cs3[pl.ds(i * 8, 8)] = early_ref[pl.ds(i * 8, 8)]
        return carry

    lax.fori_loop(0, EARLY // 8, early, 0)
    if head > EARLY:
        filling.wait()

    def await_next(per_group, unroll, parts):
        stepwise = unroll % per_group == 0
        for which in parts:
            for g in range(1 if stepwise else groups):
                if (which, g) != (0, 0):
                    coming(which, g).wait()
        if not stepwise:
            return None
        each = unroll // per_group

        def before(k):
            for n in range(1, each + 1):

                @pl.when(k * each + n < groups)
                def _():
                    for which in parts:
                        coming(which, k * each + n).wait()

        return before

    def arrived(box, g, part):
        if wide:
            at = (((g >> 1) * 2 + part) * 2 + (g & 1)) * 8
        else:
            at = (g * 2 + part) * 8
        return w_ref[box, pl.ds(pl.multiple_of(at, 8), 8), :]

    def produce_three(i):
        tiles = fresh(LOW[2])
        g = i >> log2(parents)
        parent = i & (parents - 1)
        m3 = parent >> log2(py)
        n3 = parent & (py - 1)
        for c in range(4):
            box = (2 * m3 + c // 2) * ny + 2 * n3 + c % 2
            reals = doubled(arrived(box, g, 0), low_half)
            imags = doubled(arrived(box, g, 1), low_half)
            for ta in range(4):
                at = ((i * 4 + c) * 4 + ta) * 2
                turn_back(reals[ta // 2], imags[ta // 2], cs3[at], cs3[at + 1], tiles, ta, c, LOW[2])
        return laid(tiles)

    def consume_three(i, y):
        z3_ref[pl.ds(pl.multiple_of(i * 64, 64), 64), :] = y

    staged(groups * parents, produce_three, consume_three, mix_ref, LOW[2], UNROLL[2],
           await_next(parents, UNROLL[2], (0,)))

    def decode(i):
        last = i & (boxes - 1)
        gta = i >> log2(boxes)
        return gta >> 2, gta & 3, last

    def produce_four(i):
        tiles = fresh(LOW[3])
        g, ta, last = decode(i)
        m4 = last >> log2(fy)
        n4 = last & (fy - 1)
        for c in range(4):
            box = (2 * m4 + c // 2) * py + 2 * n4 + c % 2
            source = pl.multiple_of(((g * parents + box) * 4 + ta) * 16, 16)
            reals = doubled(z3_ref[pl.ds(source, 8), :], low_half)
            imags = doubled(z3_ref[pl.ds(source + 8, 8), :], low_half)
            for tile in range(4):
                at = ((i * 4 + c) * 4 + tile) * 2
                turn_back(reals[tile // 2], imags[tile // 2], cs4[at], cs4[at + 1], tiles, tile, c, LOW[3])
        return laid(tiles)

    def consume_four(i, y):
        g, ta, last = decode(i)
        t2 = ta >> 1
        a1 = ta & 1
        gx = g >> 1 if wide else g
        for a2 in range(2):
            for b1 in range(2):
                tile = a2 * 2 + b1
                real = y[tile * 16:tile * 16 + 8]
                imag = y[tile * 16 + 8:tile * 16 + 16]
                c, s = cs5[(i * 4 + tile) * 2], cs5[(i * 4 + tile) * 2 + 1]
                ore = real * c - imag * s
                oim = real * s + imag * c
                pair = (
                    jnp.where(low_half, ore, pltpu.roll(oim, 64, 1)),
                    jnp.where(low_half, pltpu.roll(ore, 64, 1), oim),
                )
                for b2, value in enumerate(pair):
                    inner = (4 * t2 + 2 * a2 + b2) * boxes + last

                    def at(h):
                        line = (h * piece_x + gx) * 4 + 2 * a1 + b1
                        return line * (piece_y * 8 * boxes) + inner

                    if wide:
                        out_ref[pl.ds(at(g & 1), 8, stride=8 * boxes), :] = value
                    else:
                        for h in range(2):
                            out_ref[pl.ds(at(h), 4, stride=8 * boxes), :] = value[4 * h:4 * h + 4]

    each = UNROLL[3] // (4 * boxes)
    early = wide and UNROLL[3] % (4 * boxes) == 0
    size = 4 * piece_y * 8 * boxes if early else out_hbm.shape[0]

    def leaving(k):
        if early:
            k = (k & 1) * piece_x + (k >> 1)
        rows = pl.ds(pl.multiple_of(k * size, size), size)
        return pltpu.make_async_copy(out_ref.at[rows], out_hbm.at[rows], out_sem.at[k])

    def leave_trip(k):
        for n in range(each):
            leaving(k * each + n).start()

    staged(groups * 4 * boxes, produce_four, consume_four, mix_ref, LOW[3], UNROLL[3],
           await_next(4 * boxes, UNROLL[3], (1,)), leave_trip if early else None)
    if not early:
        leaving(0).start()
    for k in range(groups if early else 1):
        leaving(k).wait()


def target_side(arrived, mix, phases, nx, ny, piece_x, piece_y):
    parents, boxes = (nx // 2) * (ny // 2), (nx // 4) * (ny // 4)
    groups = piece_x * (2 if piece_y == 8 else 1)
    return pl.pallas_call(
        functools.partial(target_kernel, nx, ny, piece_x, piece_y),
        in_specs=[pl.BlockSpec(memory_space=pltpu.VMEM)] * 4 + [pl.BlockSpec(memory_space=pltpu.HBM)],
        out_specs=pl.BlockSpec(memory_space=pltpu.HBM),
        out_shape=jax.ShapeDtypeStruct((2 * 4 * piece_x * 2 * 4 * piece_y * boxes, 128), jnp.float32),
        scratch_shapes=[
            pltpu.VMEM((groups * parents * 64, 128), jnp.float32),
            pltpu.VMEM(phases[0].shape, jnp.float32),
            pltpu.VMEM(((64 * piece_x * piece_y + 64) * boxes, 128), jnp.float32),
            pltpu.SemaphoreType.DMA((2, groups)),
            pltpu.SemaphoreType.DMA((groups,)),
        ],
        compiler_params=pltpu.CompilerParams(vmem_limit_bytes=48 * 2**20),
        name="target_levels",
        cost_estimate=pl.CostEstimate(flops=2 * 10**9, bytes_accessed=2 * 2**20, transcendentals=0),
    )(arrived, mix, phases[1], phases[2], phases[0])


def to_targets(made, nx, ny, piece_x, piece_y):
    if (piece_x, piece_y) != (2, 8):
        made = made.reshape(4, 2, 4, 2, 2, 4, 2, 2, 128)
        lead = [0, 1] + ([3] if piece_x == 1 else []) + [2] + ([6] if piece_y == 4 else [])
        rest = ([3] if piece_x == 2 else []) + [4, 5] + ([6] if piece_y == 8 else []) + [7]
        made = made.transpose(lead + rest + [8])
    return made.reshape(nx * ny, -1, 128)


def on_device(weights):
    nx = lax.axis_size("sx")
    ny = lax.axis_size("sy")
    piece_x = 2 * weights.shape[0] // nx
    piece_y = 2 * weights.shape[1] // ny
    mix = jnp.asarray(mixing())
    made = to_targets(source_side(weights, mix), nx, ny, piece_x, piece_y)
    arrived = lax.all_to_all(made, ("sx", "sy"), split_axis=0, concat_axis=0, tiled=True)
    phases = phase_side(nx, ny, piece_x, piece_y)
    out = target_side(arrived, mix, phases, nx, ny, piece_x, piece_y)
    return out.reshape(2, 4 * piece_x, 2, 4 * piece_y, nx // 4, ny // 4, 128)


def solution(mesh):
    return jax.shard_map(
        on_device,
        mesh=mesh,
        in_specs=(P(None, None, "sx", "sy", None),),
        out_specs=P(None, "sx", None, "sy", None, None, None),
        check_vma=False,
    )
```

```python
import functools

import jax
import jax.numpy as jnp
import ml_dtypes
import numpy as np
from jax import lax
from jax.experimental import pallas as pl
from jax.experimental.pallas import tpu as pltpu
from jax.sharding import PartitionSpec as P

GRID = 4096
BOXES = 64

HALF_SIN = (4.442867279052734, -7.30741548538208, 3.5945212841033936, -0.7836661338806152)

EARLY = 256

UNROLL = (32, 16, 8, 16)

LOW = (True, True, True, True)

NODES = 0.5 - 0.5 * np.cos(np.pi * (2.0 * np.arange(8) + 1.0) / 16.0)


def mixing():
    def side(c):
        shifted = (c + NODES) / 2.0
        out = np.ones((8, 8))
        for i in range(8):
            for k in range(8):
                if k != i:
                    out[i] *= (shifted - NODES[k]) / (NODES[i] - NODES[k])
        return out

    rows = []
    for cx in range(2):
        for cy in range(2):
            rows.append(np.kron(np.eye(2), np.kron(side(cx), side(cy)).T))
    full = np.concatenate(rows, axis=0)
    high = full.astype(ml_dtypes.bfloat16)
    low = (full - high.astype(np.float64)).astype(ml_dtypes.bfloat16)
    return np.concatenate([high, low], axis=1)


def horner(coefs, z):
    total = coefs[-1] * z + coefs[-2]
    for c in coefs[-3::-1]:
        total = total * z + c
    return total


def sincos(cycles):
    f = cycles - jnp.round(cycles)
    h = f * horner(HALF_SIN, f * f)
    w = h * h
    d = 2.0 - w
    return h * d * lax.rsqrt(d), 1.0 - w


def sine(cycles):
    return sincos(cycles)[0]


def iotas():
    lane = lax.broadcasted_iota(jnp.int32, (8, 128), 1)
    row = lax.broadcasted_iota(jnp.int32, (8, 128), 0)
    return lane, row


def lane_nodes(lane):
    j1 = (lane >> 3) & 7
    j2 = lane & 7
    z1 = jnp.zeros((8, 128), jnp.float32)
    z2 = jnp.zeros((8, 128), jnp.float32)
    for j in range(8):
        z1 = jnp.where(j1 == j, float(NODES[j]), z1)
        z2 = jnp.where(j2 == j, float(NODES[j]), z2)
    return z1, z2


def center(index, total):
    return (index.astype(jnp.float32) + 0.5) * (1.0 / total)


def doubled(value, low_half):
    other = pltpu.roll(value, 64, 1)
    return jnp.where(low_half, value, other), jnp.where(low_half, other, value)


def turn_back(real, imag, c, s, tiles, tile, child, low):
    both = jnp.concatenate([real * c + imag * s, imag * c - real * s], axis=0)
    high = both.astype(jnp.bfloat16)
    tiles[tile][child] = high
    if low:
        tiles[4 + tile][child] = (both - high.astype(jnp.float32)).astype(jnp.bfloat16)


def fresh(low):
    return [[None] * 4 for _ in range(8 if low else 4)]


def laid(tiles):
    return jnp.concatenate([jnp.concatenate(row, axis=1) for row in tiles], axis=0)


def log2(n):
    return n.bit_length() - 1


def staged(count, produce, consume, mix_ref, low, unroll, before=None, after=None, every=8):
    def contracted(rows):
        y = jnp.dot(rows, mix_ref[...], preferred_element_type=jnp.float32)
        total = y[:64, :128] + y[:64, 128:]
        return total + y[64:, :128] if low else total

    def body(k, rows):
        if before is not None:
            before(k)
        for j in range(unroll):
            i = k * unroll + j
            y = contracted(rows)
            if unroll < count or j + 1 < count:
                rows = produce(jnp.minimum(i + 1, count - 1))
            consume(i, y)
            if after is not None and (j + 1) % every == 0:
                after(k * (unroll // every) + j // every)
        return rows

    if unroll == count:
        body(jnp.int32(0), produce(jnp.int32(0)))
    else:
        lax.fori_loop(0, count // unroll, body, produce(jnp.int32(0)))


def source_kernel(w_hbm, mix_hbm, out_hbm, amp0, amp1, q_tab, speed, shift_x, shift_y, change,
                  z1_ref, w_ref, mix_ref, out_ref, in_sem, mix_sem, out_sem):
    fetches = [
        pltpu.make_async_copy(w_hbm.at[:, a, :, b], w_ref.at[4 * a + b], in_sem.at[4 * a + b])
        for a in range(4)
        for b in range(4)
    ]
    fetches.append(pltpu.make_async_copy(mix_hbm, mix_ref, mix_sem))
    for fetch in fetches:
        fetch.start()
    lane, row = iotas()
    low_half = lane < 64
    upper = (lane >> 6) & 1
    pos_x = lax.axis_index("sx")
    pos_y = lax.axis_index("sy")
    third = 1.0 / 3.0

    z1, z2 = lane_nodes(lane)
    qx0 = [(4 * pos_x + m).astype(jnp.float32) + z1 for m in range(4)]
    qy0 = [(4 * pos_y + n).astype(jnp.float32) + z2 for n in range(4)]
    for m in range(4):
        for n in range(4):
            amp0[4 * m + n] = 64.0 * jnp.sqrt(qx0[m] * qx0[m] + qy0[n] * qy0[n])
    sign = jnp.where(low_half, -0.25, 0.25)
    for m in range(2):
        qx = (2 * pos_x + m).astype(jnp.float32) + z1
        for n in range(2):
            qy = (2 * pos_y + n).astype(jnp.float32) + z2
            amp1[2 * m + n] = 128.0 * jnp.sqrt(qx * qx + qy * qy)
            for t1 in range(2):
                q_tab[2 * (2 * m + n) + t1] = sign * qy + (0.25 * (2 * t1 - 1)) * qx

    hx = row >> 2
    hy = (row >> 1) & 1
    b_low = row & 1
    y_tabs = []
    for jb in range(4):
        column = hy * 8 + jb * 2 + b_low
        both = column * 2 + upper
        for n in range(4):
            v = (both.astype(jnp.float32) + 0.5) * 0.5 * qy0[n]
            shift_y[jb * 4 + n] = v - jnp.round(v)
        own = [sine(center(column * 2 + s2, 128)) for s2 in range(2)]
        child = [sine(center((column * 2 + s2) * 2 + upper, 256)) for s2 in range(2)]
        y_tabs.append((jnp.where(low_half, own[0], own[1]), own, child))

    def tables(i, carry):
        a_mid = i >> 1
        s1 = i & 1
        rows = (hx * 4 + a_mid) * 2 + s1
        s_x = sine(center(rows, 128))
        child_x = [sine(center(rows * 2 + t1, 256)) for t1 in range(2)]
        for m in range(4):
            v = (rows.astype(jnp.float32) + 0.5) * 0.5 * qx0[m]
            shift_x[i * 4 + m] = v - jnp.round(v)
        for jb in range(4):
            both, own, child = y_tabs[jb]
            at = (a_mid * 4 + jb) * 2 + s1
            speed[at] = (2.0 + s_x * both) * third
            for t1 in range(2):
                for s2 in range(2):
                    change[at * 4 + t1 * 2 + s2] = (child_x[t1] * child[s2] - s_x * own[s2]) * third
        return carry

    lax.fori_loop(0, 8, tables, 0)
    for fetch in fetches:
        fetch.wait()
    w_rows = w_ref.reshape(17 * 128, 128)

    def produce_one(i):
        tiles = fresh(LOW[0])
        ajb = i >> 1
        m_half = i & 1
        a_mid = ajb >> 2
        jb = ajb & 3
        for n_half in range(2):
            for cx in range(2):
                m = 2 * m_half + cx
                for cy in range(2):
                    n = 2 * n_half + cy
                    box = 4 * m + n
                    value = w_rows[pl.ds(ajb * 128 + box, 8, stride=16), :]
                    other = pltpu.roll(value, 64, 1)
                    real = jnp.where(low_half, value, other)
                    imag = jnp.where(low_half, other, value)
                    amp = amp0[box]
                    for s1 in range(2):
                        shift = shift_x[(a_mid * 2 + s1) * 4 + m] + shift_y[jb * 4 + n]
                        cycles = speed[ajb * 2 + s1] * amp + shift
                        s, c = sincos(cycles)
                        turn_back(real, imag, c, s, tiles, n_half * 2 + s1, 2 * cx + cy, LOW[0])
        return laid(tiles)

    def consume_one(i, y):
        z1_ref[pl.ds(pl.multiple_of(i * 64, 64), 64), :] = y

    staged(32, produce_one, consume_one, mix_ref, LOW[0], UNROLL[0])

    def produce_two(i):
        tiles = fresh(LOW[1])
        s1 = i & 1
        ajb = i >> 1
        for c in range(4):
            source = pl.multiple_of(((ajb * 4 + c) * 2 + s1) * 16, 16)
            reals = doubled(z1_ref[pl.ds(source, 8), :], low_half)
            imags = doubled(z1_ref[pl.ds(source + 8, 8), :], low_half)
            amp = amp1[c]
            for t1 in range(2):
                lin = q_tab[2 * c + t1]
                for s2 in range(2):
                    cycles = change[i * 4 + t1 * 2 + s2] * amp + lin
                    sin, cos = sincos(cycles)
                    turn_back(reals[s2], imags[s2], cos, sin, tiles, t1 * 2 + s2, c, LOW[1])
        return laid(tiles)

    def consume_two(i, y):
        s1 = i & 1
        ajb = i >> 1
        base = pl.multiple_of((((ajb >> 2) * 2 + s1) * 4 + (ajb & 3)) * 64, 64)
        for t1 in range(2):
            for s2 in range(2):
                tile = (t1 * 2 + s2) * 16
                for part in range(2):
                    at = base + (t1 * 32 + part * 16 + s2)
                    out_ref[pl.ds(at, 8, stride=2), :] = y[tile + 8 * part:tile + 8 * part + 8]

    def leaving(k):
        rows = pl.ds(pl.multiple_of(k * 512, 512), 512)
        return pltpu.make_async_copy(out_ref.at[rows], out_hbm.at[rows], out_sem.at[k])

    staged(32, produce_two, consume_two, mix_ref, LOW[1], UNROLL[1],
           after=lambda k: leaving(k).start())
    for k in range(4):
        leaving(k).wait()


def tab(n):
    return pltpu.VMEM((n, 8, 128), jnp.float32)


def source_side(weights, mix):
    pieces = weights.reshape(2, 4, 2, 4, 2, 16, 128)
    return pl.pallas_call(
        source_kernel,
        in_specs=[pl.BlockSpec(memory_space=pltpu.HBM)] * 2,
        out_specs=pl.BlockSpec(memory_space=pltpu.HBM),
        out_shape=jax.ShapeDtypeStruct((2048, 128), jnp.float32),
        scratch_shapes=[
            tab(16), tab(4), tab(8), tab(32), tab(32), tab(16), tab(128),
            pltpu.VMEM((2048, 128), jnp.float32),
            pltpu.VMEM((17, 2, 2, 2, 16, 128), jnp.float32),
            pltpu.VMEM((512, 256), jnp.bfloat16),
            pltpu.VMEM((2064, 128), jnp.float32),
            pltpu.SemaphoreType.DMA((16,)),
            pltpu.SemaphoreType.DMA,
            pltpu.SemaphoreType.DMA((4,)),
        ],
        name="source_levels",
        cost_estimate=pl.CostEstimate(flops=2 * 10**9, bytes_accessed=2 * 2**20, transcendentals=0),
    )(pieces, mix)


def group_bits(nx, ny, piece_x, piece_y):
    return nx // 2, ny // 2, nx // 4, ny // 4, piece_y == 8, piece_x * (2 if piece_y == 8 else 1)


def ranges(ref, items):
    return ref.at[pl.ds(0, 32 * items)], ref.at[pl.ds(32 * items, 32 * items)]


def phase_kernel(nx, ny, piece_x, piece_y, out_ref, early_ref, cs5,
                 amp2, lin2, amp3, lin3, amp4, change3, change4, speed4):
    px, py, fx, fy, wide, groups = group_bits(nx, ny, piece_x, piece_y)
    parents, boxes = px * py, fx * fy
    items = groups * parents
    cs3, cs4 = ranges(out_ref, items)
    lane, row = iotas()
    low_half = lane < 64
    upper = (lane >> 6) & 1
    pos_x = lax.axis_index("sx")
    pos_y = lax.axis_index("sy")
    sign = jnp.where(low_half, -0.25, 0.25)
    third = 1.0 / 3.0
    z1, z2 = lane_nodes(lane)

    def box_tables(count_x, count_y, scale, amp, lin):
        qys = [float(n) + z2 for n in range(count_y)]

        def one(m, carry):
            qx = m.astype(jnp.float32) + z1
            for n, qy in enumerate(qys):
                box = m * count_y + n
                amp[box] = scale * jnp.sqrt(qx * qx + qy * qy)
                if lin is not None:
                    lin[2 * box] = sign * qy - 0.25 * qx
                    lin[2 * box + 1] = sign * qy + 0.25 * qx
            return carry

        lax.fori_loop(0, count_x, one, 0)

    box_tables(nx, ny, 256.0, amp2, lin2)
    box_tables(px, py, 512.0, amp3, lin3)
    box_tables(fx, fy, 1024.0, amp4, None)

    if wide:
        hy = row >> 2
        k = row & 3
    else:
        hy = (row >> 1) & 1
        k = row & 1
    cols2 = hy * 32 + pos_y * piece_y + 2 * k

    def rows2(g):
        if wide:
            return jnp.full((8, 128), (g & 1) * 16 + pos_x * piece_x + (g >> 1), jnp.int32)
        return (row >> 2) * 16 + pos_x * piece_x + g

    y_tabs = []
    for t2 in range(2):
        s_y2 = sine(center(cols2 + t2, 256))
        own = [sine(center(2 * (cols2 + t2) + a2, 512)) for a2 in range(2)]
        last = [sine(center(4 * (cols2 + t2) + 2 * a2 + upper, 1024)) for a2 in range(2)]
        y_tabs.append((s_y2, jnp.where(low_half, own[0], own[1]), own, last))

    def target_tables(g, carry):
        rows = rows2(g)
        s_x2 = sine(center(rows, 256))
        for a1 in range(2):
            x3 = sine(center(2 * rows + a1, 512))
            x4 = [sine(center(4 * rows + 2 * a1 + b1, 1024)) for b1 in range(2)]
            for t2 in range(2):
                s_y2, y3, own, last = y_tabs[t2]
                ta = 2 * t2 + a1
                change3[g * 4 + ta] = (x3 * y3 - s_x2 * s_y2) * third
                for a2 in range(2):
                    for b1 in range(2):
                        at = (g * 4 + ta) * 4 + a2 * 2 + b1
                        product = x4[b1] * last[a2]
                        change4[at] = (product - x3 * own[a2]) * third
                        speed4[at] = (2.0 + product) * third
        return carry

    lax.fori_loop(0, groups, target_tables, 0)

    def put(ref, at, cycles):
        s, c = sincos(cycles)
        ref[at] = c
        ref[at + 1] = s

    def phases_three(i, carry):
        g = i >> log2(parents)
        parent = i & (parents - 1)
        m3 = parent >> log2(py)
        n3 = parent & (py - 1)
        for c in range(4):
            box = (2 * m3 + c // 2) * ny + 2 * n3 + c % 2
            for ta in range(4):
                cycles = change3[g * 4 + ta] * amp2[box] + lin2[2 * box + ta % 2]
                put(cs3, ((i * 4 + c) * 4 + ta) * 2, cycles)
        return carry

    lax.fori_loop(0, groups * parents, phases_three, 0)

    def early(i, carry):
        early_ref[pl.ds(i * 8, 8)] = cs3[pl.ds(i * 8, 8)]
        return carry

    lax.fori_loop(0, early_ref.shape[0] // 8, early, 0)

    def phases_four(i, carry):
        last = i & (boxes - 1)
        gta = i >> log2(boxes)
        g = gta >> 2
        t2 = (gta >> 1) & 1
        a1 = gta & 1
        m4 = last >> log2(fy)
        n4 = last & (fy - 1)
        p1 = m4.astype(jnp.float32) + z1
        p2 = n4.astype(jnp.float32) + z2
        rows = rows2(g) * 4 + 2 * a1
        for tile in range(4):
            a2, b1 = tile // 2, tile % 2
            for c in range(4):
                box = (2 * m4 + c // 2) * py + 2 * n4 + c % 2
                cycles = change4[gta * 4 + tile] * amp3[box] + lin3[2 * box + b1]
                put(cs4, ((i * 4 + c) * 4 + tile) * 2, cycles)
            col = (4 * (cols2 + t2) + 2 * a2 + upper).astype(jnp.float32) + 0.5
            r4 = (rows + b1).astype(jnp.float32) + 0.5
            put(cs5, (i * 4 + tile) * 2, speed4[gta * 4 + tile] * amp4[last] + (r4 * p1 + col * p2))
        return carry

    lax.fori_loop(0, groups * 4 * boxes, phases_four, 0)


def phase_side(nx, ny, piece_x, piece_y):
    px, py, fx, fy, wide, groups = group_bits(nx, ny, piece_x, piece_y)
    parents, boxes = px * py, fx * fy
    items = groups * parents
    return pl.pallas_call(
        functools.partial(phase_kernel, nx, ny, piece_x, piece_y),
        out_specs=[pl.BlockSpec(memory_space=pltpu.VMEM)] * 3,
        out_shape=[jax.ShapeDtypeStruct((64 * items, 8, 128), jnp.float32),
                   pltpu.VMEM((EARLY, 8, 128), jnp.float32),
                   pltpu.VMEM((8 * items, 8, 128), jnp.float32)],
        scratch_shapes=[
            tab(nx * ny), tab(2 * nx * ny), tab(parents), tab(2 * parents), tab(boxes),
            tab(groups * 4), tab(groups * 16), tab(groups * 16),
        ],
        name="phases",
        cost_estimate=pl.CostEstimate(flops=2 * 10**9, bytes_accessed=9 * 2**20, transcendentals=0),
    )()


def target_kernel(nx, ny, piece_x, piece_y, w_ref, mix_ref, early_ref, cs5, cs_hbm, out_hbm,
                  z3_ref, cs_ref, out_ref, in_sem, out_sem):
    px, py, fx, fy, wide, groups = group_bits(nx, ny, piece_x, piece_y)
    parents, boxes = px * py, fx * fy
    low_half = iotas()[0] < 64

    comes = ranges(cs_hbm, groups * parents)
    cs3, cs4 = kept = ranges(cs_ref, groups * parents)

    def coming(which, g):
        source, target = comes[which], kept[which]
        part = source.shape[0] // groups
        rows = pl.ds(g * part, part)
        return pltpu.make_async_copy(source.at[rows], target.at[rows], in_sem.at[which, g])

    for g in range(1, groups):
        coming(0, g).start()
    for g in range(groups):
        coming(1, g).start()
    head = 32 * parents
    if head > EARLY:
        rest = pl.ds(EARLY, head - EARLY)
        filling = pltpu.make_async_copy(comes[0].at[rest], cs3.at[rest], in_sem.at[0, 0])
        filling.start()

    def early(i, carry):
        cs3[pl.ds(i * 8, 8)] = early_ref[pl.ds(i * 8, 8)]
        return carry

    lax.fori_loop(0, EARLY // 8, early, 0)
    if head > EARLY:
        filling.wait()

    def await_next(per_group, unroll, parts):
        stepwise = unroll % per_group == 0
        for which in parts:
            for g in range(1 if stepwise else groups):
                if (which, g) != (0, 0):
                    coming(which, g).wait()
        if not stepwise:
            return None
        each = unroll // per_group

        def before(k):
            for n in range(1, each + 1):

                @pl.when(k * each + n < groups)
                def _():
                    for which in parts:
                        coming(which, k * each + n).wait()

        return before

    def arrived(box, g, part):
        if wide:
            at = (((g >> 1) * 2 + part) * 2 + (g & 1)) * 8
        else:
            at = (g * 2 + part) * 8
        return w_ref[box, pl.ds(pl.multiple_of(at, 8), 8), :]

    def produce_three(i):
        tiles = fresh(LOW[2])
        g = i >> log2(parents)
        parent = i & (parents - 1)
        m3 = parent >> log2(py)
        n3 = parent & (py - 1)
        for c in range(4):
            box = (2 * m3 + c // 2) * ny + 2 * n3 + c % 2
            reals = doubled(arrived(box, g, 0), low_half)
            imags = doubled(arrived(box, g, 1), low_half)
            for ta in range(4):
                at = ((i * 4 + c) * 4 + ta) * 2
                turn_back(reals[ta // 2], imags[ta // 2], cs3[at], cs3[at + 1], tiles, ta, c, LOW[2])
        return laid(tiles)

    def consume_three(i, y):
        z3_ref[pl.ds(pl.multiple_of(i * 64, 64), 64), :] = y

    staged(groups * parents, produce_three, consume_three, mix_ref, LOW[2], UNROLL[2],
           await_next(parents, UNROLL[2], (0,)))

    def decode(i):
        last = i & (boxes - 1)
        gta = i >> log2(boxes)
        return gta >> 2, gta & 3, last

    def produce_four(i):
        tiles = fresh(LOW[3])
        g, ta, last = decode(i)
        m4 = last >> log2(fy)
        n4 = last & (fy - 1)
        for c in range(4):
            box = (2 * m4 + c // 2) * py + 2 * n4 + c % 2
            source = pl.multiple_of(((g * parents + box) * 4 + ta) * 16, 16)
            reals = doubled(z3_ref[pl.ds(source, 8), :], low_half)
            imags = doubled(z3_ref[pl.ds(source + 8, 8), :], low_half)
            for tile in range(4):
                at = ((i * 4 + c) * 4 + tile) * 2
                turn_back(reals[tile // 2], imags[tile // 2], cs4[at], cs4[at + 1], tiles, tile, c, LOW[3])
        return laid(tiles)

    def consume_four(i, y):
        g, ta, last = decode(i)
        t2 = ta >> 1
        a1 = ta & 1
        gx = g >> 1 if wide else g
        for a2 in range(2):
            for b1 in range(2):
                tile = a2 * 2 + b1
                real = y[tile * 16:tile * 16 + 8]
                imag = y[tile * 16 + 8:tile * 16 + 16]
                c, s = cs5[(i * 4 + tile) * 2], cs5[(i * 4 + tile) * 2 + 1]
                ore = real * c - imag * s
                oim = real * s + imag * c
                pair = (
                    jnp.where(low_half, ore, pltpu.roll(oim, 64, 1)),
                    jnp.where(low_half, pltpu.roll(ore, 64, 1), oim),
                )
                for b2, value in enumerate(pair):
                    inner = (4 * t2 + 2 * a2 + b2) * boxes + last

                    def at(h):
                        line = (h * piece_x + gx) * 4 + 2 * a1 + b1
                        return line * (piece_y * 8 * boxes) + inner

                    if wide:
                        out_ref[pl.ds(at(g & 1), 8, stride=8 * boxes), :] = value
                    else:
                        for h in range(2):
                            out_ref[pl.ds(at(h), 4, stride=8 * boxes), :] = value[4 * h:4 * h + 4]

    early = wide and 4 * boxes == 8
    size = 4 * piece_y * 8 * boxes if early else out_hbm.shape[0]

    def leaving(k):
        if early:
            k = (k & 1) * piece_x + (k >> 1)
        rows = pl.ds(pl.multiple_of(k * size, size), size)
        return pltpu.make_async_copy(out_ref.at[rows], out_hbm.at[rows], out_sem.at[k])

    staged(groups * 4 * boxes, produce_four, consume_four, mix_ref, LOW[3], UNROLL[3],
           await_next(4 * boxes, UNROLL[3], (1,)), (lambda k: leaving(k).start()) if early else None)
    if not early:
        leaving(0).start()
    for k in range(groups if early else 1):
        leaving(k).wait()


def target_side(arrived, mix, phases, nx, ny, piece_x, piece_y):
    parents, boxes = (nx // 2) * (ny // 2), (nx // 4) * (ny // 4)
    groups = piece_x * (2 if piece_y == 8 else 1)
    return pl.pallas_call(
        functools.partial(target_kernel, nx, ny, piece_x, piece_y),
        in_specs=[pl.BlockSpec(memory_space=pltpu.VMEM)] * 4 + [pl.BlockSpec(memory_space=pltpu.HBM)],
        out_specs=pl.BlockSpec(memory_space=pltpu.HBM),
        out_shape=jax.ShapeDtypeStruct((2 * 4 * piece_x * 2 * 4 * piece_y * boxes, 128), jnp.float32),
        scratch_shapes=[
            pltpu.VMEM((groups * parents * 64, 128), jnp.float32),
            pltpu.VMEM(phases[0].shape, jnp.float32),
            pltpu.VMEM(((64 * piece_x * piece_y + 64) * boxes, 128), jnp.float32),
            pltpu.SemaphoreType.DMA((2, groups)),
            pltpu.SemaphoreType.DMA((groups,)),
        ],
        compiler_params=pltpu.CompilerParams(vmem_limit_bytes=48 * 2**20),
        name="target_levels",
        cost_estimate=pl.CostEstimate(flops=2 * 10**9, bytes_accessed=2 * 2**20, transcendentals=0),
    )(arrived, mix, phases[1], phases[2], phases[0])


def to_targets(made, nx, ny, piece_x, piece_y):
    if (piece_x, piece_y) != (2, 8):
        made = made.reshape(4, 2, 4, 2, 2, 4, 2, 2, 128)
        lead = [0, 1] + ([3] if piece_x == 1 else []) + [2] + ([6] if piece_y == 4 else [])
        rest = ([3] if piece_x == 2 else []) + [4, 5] + ([6] if piece_y == 8 else []) + [7]
        made = made.transpose(lead + rest + [8])
    return made.reshape(nx * ny, -1, 128)


def on_device(weights):
    nx = lax.axis_size("sx")
    ny = lax.axis_size("sy")
    piece_x = 2 * weights.shape[0] // nx
    piece_y = 2 * weights.shape[1] // ny
    mix = jnp.asarray(mixing())
    made = to_targets(source_side(weights, mix), nx, ny, piece_x, piece_y)
    arrived = lax.all_to_all(made, ("sx", "sy"), split_axis=0, concat_axis=0, tiled=True)
    phases = phase_side(nx, ny, piece_x, piece_y)
    out = target_side(arrived, mix, phases, nx, ny, piece_x, piece_y)
    return out.reshape(2, 4 * piece_x, 2, 4 * piece_y, nx // 4, ny // 4, 128)


def solution(mesh):
    return jax.shard_map(
        on_device,
        mesh=mesh,
        in_specs=(P(None, None, "sx", "sy", None),),
        out_specs=P(None, "sx", None, "sy", None, None, None),
        check_vma=False,
    )
```

```python
import functools

import jax
import jax.numpy as jnp
import ml_dtypes
import numpy as np
from jax import lax
from jax.experimental import pallas as pl
from jax.experimental.pallas import tpu as pltpu
from jax.sharding import PartitionSpec as P

GRID = 4096
BOXES = 64

HALF_SIN = (4.442867279052734, -7.30741548538208, 3.5945212841033936, -0.7836661338806152)

EARLY = 256

UNROLL = (32, 32, 8, 16)

LOW = (True, True, True, True)

NODES = 0.5 - 0.5 * np.cos(np.pi * (2.0 * np.arange(8) + 1.0) / 16.0)


def mixing():
    def side(c):
        shifted = (c + NODES) / 2.0
        out = np.ones((8, 8))
        for i in range(8):
            for k in range(8):
                if k != i:
                    out[i] *= (shifted - NODES[k]) / (NODES[i] - NODES[k])
        return out

    rows = []
    for cx in range(2):
        for cy in range(2):
            rows.append(np.kron(np.eye(2), np.kron(side(cx), side(cy)).T))
    full = np.concatenate(rows, axis=0)
    high = full.astype(ml_dtypes.bfloat16)
    low = (full - high.astype(np.float64)).astype(ml_dtypes.bfloat16)
    return np.concatenate([high, low], axis=1)


def horner(coefs, z):
    total = coefs[-1] * z + coefs[-2]
    for c in coefs[-3::-1]:
        total = total * z + c
    return total


def sincos(cycles):
    f = cycles - jnp.round(cycles)
    h = f * horner(HALF_SIN, f * f)
    w = h * h
    d = 2.0 - w
    return h * d * lax.rsqrt(d), 1.0 - w


def sine(cycles):
    return sincos(cycles)[0]


def iotas():
    lane = lax.broadcasted_iota(jnp.int32, (8, 128), 1)
    row = lax.broadcasted_iota(jnp.int32, (8, 128), 0)
    return lane, row


def lane_nodes(lane):
    j1 = (lane >> 3) & 7
    j2 = lane & 7
    z1 = jnp.zeros((8, 128), jnp.float32)
    z2 = jnp.zeros((8, 128), jnp.float32)
    for j in range(8):
        z1 = jnp.where(j1 == j, float(NODES[j]), z1)
        z2 = jnp.where(j2 == j, float(NODES[j]), z2)
    return z1, z2


def center(index, total):
    return (index.astype(jnp.float32) + 0.5) * (1.0 / total)


def doubled(value, low_half):
    other = pltpu.roll(value, 64, 1)
    return jnp.where(low_half, value, other), jnp.where(low_half, other, value)


def turn_back(real, imag, c, s, tiles, tile, child, low):
    both = jnp.concatenate([real * c + imag * s, imag * c - real * s], axis=0)
    high = both.astype(jnp.bfloat16)
    tiles[tile][child] = high
    if low:
        tiles[4 + tile][child] = (both - high.astype(jnp.float32)).astype(jnp.bfloat16)


def fresh(low):
    return [[None] * 4 for _ in range(8 if low else 4)]


def laid(tiles):
    return jnp.concatenate([jnp.concatenate(row, axis=1) for row in tiles], axis=0)


def log2(n):
    return n.bit_length() - 1


def staged(count, produce, consume, mix_ref, low, unroll, before=None, after=None, every=8):
    def contracted(rows):
        y = jnp.dot(rows, mix_ref[...], preferred_element_type=jnp.float32)
        total = y[:64, :128] + y[:64, 128:]
        return total + y[64:, :128] if low else total

    def body(k, rows):
        if before is not None:
            before(k)
        for j in range(unroll):
            i = k * unroll + j
            y = contracted(rows)
            if unroll < count or j + 1 < count:
                rows = produce(jnp.minimum(i + 1, count - 1))
            consume(i, y)
            if after is not None and (j + 1) % every == 0:
                after(k * (unroll // every) + j // every)
        return rows

    if unroll == count:
        body(jnp.int32(0), produce(jnp.int32(0)))
    else:
        lax.fori_loop(0, count // unroll, body, produce(jnp.int32(0)))


def source_kernel(w_hbm, mix_hbm, out_hbm, amp0, amp1, q_tab, speed, shift_x, shift_y, change,
                  z1_ref, w_ref, mix_ref, out_ref, in_sem, mix_sem, out_sem):
    fetches = [
        pltpu.make_async_copy(w_hbm.at[:, a, :, b], w_ref.at[4 * a + b], in_sem.at[4 * a + b])
        for a in range(4)
        for b in range(4)
    ]
    fetches.append(pltpu.make_async_copy(mix_hbm, mix_ref, mix_sem))
    for fetch in fetches:
        fetch.start()
    lane, row = iotas()
    low_half = lane < 64
    upper = (lane >> 6) & 1
    pos_x = lax.axis_index("sx")
    pos_y = lax.axis_index("sy")
    third = 1.0 / 3.0

    z1, z2 = lane_nodes(lane)
    qx0 = [(4 * pos_x + m).astype(jnp.float32) + z1 for m in range(4)]
    qy0 = [(4 * pos_y + n).astype(jnp.float32) + z2 for n in range(4)]
    for m in range(4):
        for n in range(4):
            amp0[4 * m + n] = 64.0 * jnp.sqrt(qx0[m] * qx0[m] + qy0[n] * qy0[n])
    sign = jnp.where(low_half, -0.25, 0.25)
    for m in range(2):
        qx = (2 * pos_x + m).astype(jnp.float32) + z1
        for n in range(2):
            qy = (2 * pos_y + n).astype(jnp.float32) + z2
            amp1[2 * m + n] = 128.0 * jnp.sqrt(qx * qx + qy * qy)
            for t1 in range(2):
                q_tab[2 * (2 * m + n) + t1] = sign * qy + (0.25 * (2 * t1 - 1)) * qx

    hx = row >> 2
    hy = (row >> 1) & 1
    b_low = row & 1
    y_tabs = []
    for jb in range(4):
        column = hy * 8 + jb * 2 + b_low
        both = column * 2 + upper
        for n in range(4):
            v = (both.astype(jnp.float32) + 0.5) * 0.5 * qy0[n]
            shift_y[jb * 4 + n] = v - jnp.round(v)
        own = [sine(center(column * 2 + s2, 128)) for s2 in range(2)]
        child = [sine(center((column * 2 + s2) * 2 + upper, 256)) for s2 in range(2)]
        y_tabs.append((jnp.where(low_half, own[0], own[1]), own, child))

    def tables(i, carry):
        a_mid = i >> 1
        s1 = i & 1
        rows = (hx * 4 + a_mid) * 2 + s1
        s_x = sine(center(rows, 128))
        child_x = [sine(center(rows * 2 + t1, 256)) for t1 in range(2)]
        for m in range(4):
            v = (rows.astype(jnp.float32) + 0.5) * 0.5 * qx0[m]
            shift_x[i * 4 + m] = v - jnp.round(v)
        for jb in range(4):
            both, own, child = y_tabs[jb]
            at = (a_mid * 4 + jb) * 2 + s1
            speed[at] = (2.0 + s_x * both) * third
            for t1 in range(2):
                for s2 in range(2):
                    change[at * 4 + t1 * 2 + s2] = (child_x[t1] * child[s2] - s_x * own[s2]) * third
        return carry

    lax.fori_loop(0, 8, tables, 0)
    for fetch in fetches:
        fetch.wait()
    w_rows = w_ref.reshape(17 * 128, 128)

    def produce_one(i):
        tiles = fresh(LOW[0])
        ajb = i >> 1
        m_half = i & 1
        a_mid = ajb >> 2
        jb = ajb & 3
        for n_half in range(2):
            for cx in range(2):
                m = 2 * m_half + cx
                for cy in range(2):
                    n = 2 * n_half + cy
                    box = 4 * m + n
                    value = w_rows[pl.ds(ajb * 128 + box, 8, stride=16), :]
                    other = pltpu.roll(value, 64, 1)
                    real = jnp.where(low_half, value, other)
                    imag = jnp.where(low_half, other, value)
                    amp = amp0[box]
                    for s1 in range(2):
                        shift = shift_x[(a_mid * 2 + s1) * 4 + m] + shift_y[jb * 4 + n]
                        cycles = speed[ajb * 2 + s1] * amp + shift
                        s, c = sincos(cycles)
                        turn_back(real, imag, c, s, tiles, n_half * 2 + s1, 2 * cx + cy, LOW[0])
        return laid(tiles)

    def consume_one(i, y):
        z1_ref[pl.ds(pl.multiple_of(i * 64, 64), 64), :] = y

    staged(32, produce_one, consume_one, mix_ref, LOW[0], UNROLL[0])

    def produce_two(i):
        tiles = fresh(LOW[1])
        s1 = i & 1
        ajb = i >> 1
        for c in range(4):
            source = pl.multiple_of(((ajb * 4 + c) * 2 + s1) * 16, 16)
            reals = doubled(z1_ref[pl.ds(source, 8), :], low_half)
            imags = doubled(z1_ref[pl.ds(source + 8, 8), :], low_half)
            amp = amp1[c]
            for t1 in range(2):
                lin = q_tab[2 * c + t1]
                for s2 in range(2):
                    cycles = change[i * 4 + t1 * 2 + s2] * amp + lin
                    sin, cos = sincos(cycles)
                    turn_back(reals[s2], imags[s2], cos, sin, tiles, t1 * 2 + s2, c, LOW[1])
        return laid(tiles)

    def consume_two(i, y):
        s1 = i & 1
        ajb = i >> 1
        base = pl.multiple_of((((ajb >> 2) * 2 + s1) * 4 + (ajb & 3)) * 64, 64)
        for t1 in range(2):
            for s2 in range(2):
                tile = (t1 * 2 + s2) * 16
                for part in range(2):
                    at = base + (t1 * 32 + part * 16 + s2)
                    out_ref[pl.ds(at, 8, stride=2), :] = y[tile + 8 * part:tile + 8 * part + 8]

    def leaving(k):
        rows = pl.ds(pl.multiple_of(k * 512, 512), 512)
        return pltpu.make_async_copy(out_ref.at[rows], out_hbm.at[rows], out_sem.at[k])

    staged(32, produce_two, consume_two, mix_ref, LOW[1], UNROLL[1],
           after=lambda k: leaving(k).start())
    for k in range(4):
        leaving(k).wait()


def tab(n):
    return pltpu.VMEM((n, 8, 128), jnp.float32)


def source_side(weights, mix):
    pieces = weights.reshape(2, 4, 2, 4, 2, 16, 128)
    return pl.pallas_call(
        source_kernel,
        in_specs=[pl.BlockSpec(memory_space=pltpu.HBM)] * 2,
        out_specs=pl.BlockSpec(memory_space=pltpu.HBM),
        out_shape=jax.ShapeDtypeStruct((2048, 128), jnp.float32),
        scratch_shapes=[
            tab(16), tab(4), tab(8), tab(32), tab(32), tab(16), tab(128),
            pltpu.VMEM((2048, 128), jnp.float32),
            pltpu.VMEM((17, 2, 2, 2, 16, 128), jnp.float32),
            pltpu.VMEM((512, 256), jnp.bfloat16),
            pltpu.VMEM((2064, 128), jnp.float32),
            pltpu.SemaphoreType.DMA((16,)),
            pltpu.SemaphoreType.DMA,
            pltpu.SemaphoreType.DMA((4,)),
        ],
        name="source_levels",
        cost_estimate=pl.CostEstimate(flops=2 * 10**9, bytes_accessed=2 * 2**20, transcendentals=0),
    )(pieces, mix)


def group_bits(nx, ny, piece_x, piece_y):
    return nx // 2, ny // 2, nx // 4, ny // 4, piece_y == 8, piece_x * (2 if piece_y == 8 else 1)


def ranges(ref, items):
    return ref.at[pl.ds(0, 32 * items)], ref.at[pl.ds(32 * items, 32 * items)]


def phase_kernel(nx, ny, piece_x, piece_y, out_ref, early_ref, cs5,
                 amp2, lin2, amp3, lin3, amp4, change3, change4, speed4):
    px, py, fx, fy, wide, groups = group_bits(nx, ny, piece_x, piece_y)
    parents, boxes = px * py, fx * fy
    items = groups * parents
    cs3, cs4 = ranges(out_ref, items)
    lane, row = iotas()
    low_half = lane < 64
    upper = (lane >> 6) & 1
    pos_x = lax.axis_index("sx")
    pos_y = lax.axis_index("sy")
    sign = jnp.where(low_half, -0.25, 0.25)
    third = 1.0 / 3.0
    z1, z2 = lane_nodes(lane)

    def box_tables(count_x, count_y, scale, amp, lin):
        qys = [float(n) + z2 for n in range(count_y)]

        def one(m, carry):
            qx = m.astype(jnp.float32) + z1
            for n, qy in enumerate(qys):
                box = m * count_y + n
                amp[box] = scale * jnp.sqrt(qx * qx + qy * qy)
                if lin is not None:
                    lin[2 * box] = sign * qy - 0.25 * qx
                    lin[2 * box + 1] = sign * qy + 0.25 * qx
            return carry

        lax.fori_loop(0, count_x, one, 0)

    box_tables(nx, ny, 256.0, amp2, lin2)
    box_tables(px, py, 512.0, amp3, lin3)
    box_tables(fx, fy, 1024.0, amp4, None)

    if wide:
        hy = row >> 2
        k = row & 3
    else:
        hy = (row >> 1) & 1
        k = row & 1
    cols2 = hy * 32 + pos_y * piece_y + 2 * k

    def rows2(g):
        if wide:
            return jnp.full((8, 128), (g & 1) * 16 + pos_x * piece_x + (g >> 1), jnp.int32)
        return (row >> 2) * 16 + pos_x * piece_x + g

    y_tabs = []
    for t2 in range(2):
        s_y2 = sine(center(cols2 + t2, 256))
        own = [sine(center(2 * (cols2 + t2) + a2, 512)) for a2 in range(2)]
        last = [sine(center(4 * (cols2 + t2) + 2 * a2 + upper, 1024)) for a2 in range(2)]
        y_tabs.append((s_y2, jnp.where(low_half, own[0], own[1]), own, last))

    def target_tables(g, carry):
        rows = rows2(g)
        s_x2 = sine(center(rows, 256))
        for a1 in range(2):
            x3 = sine(center(2 * rows + a1, 512))
            x4 = [sine(center(4 * rows + 2 * a1 + b1, 1024)) for b1 in range(2)]
            for t2 in range(2):
                s_y2, y3, own, last = y_tabs[t2]
                ta = 2 * t2 + a1
                change3[g * 4 + ta] = (x3 * y3 - s_x2 * s_y2) * third
                for a2 in range(2):
                    for b1 in range(2):
                        at = (g * 4 + ta) * 4 + a2 * 2 + b1
                        product = x4[b1] * last[a2]
                        change4[at] = (product - x3 * own[a2]) * third
                        speed4[at] = (2.0 + product) * third
        return carry

    lax.fori_loop(0, groups, target_tables, 0)

    def put(ref, at, cycles):
        s, c = sincos(cycles)
        ref[at] = c
        ref[at + 1] = s

    def phases_three(i, carry):
        g = i >> log2(parents)
        parent = i & (parents - 1)
        m3 = parent >> log2(py)
        n3 = parent & (py - 1)
        for c in range(4):
            box = (2 * m3 + c // 2) * ny + 2 * n3 + c % 2
            for ta in range(4):
                cycles = change3[g * 4 + ta] * amp2[box] + lin2[2 * box + ta % 2]
                put(cs3, ((i * 4 + c) * 4 + ta) * 2, cycles)
        return carry

    lax.fori_loop(0, groups * parents, phases_three, 0)

    def early(i, carry):
        early_ref[pl.ds(i * 8, 8)] = cs3[pl.ds(i * 8, 8)]
        return carry

    lax.fori_loop(0, early_ref.shape[0] // 8, early, 0)

    def phases_four(i, carry):
        last = i & (boxes - 1)
        gta = i >> log2(boxes)
        g = gta >> 2
        t2 = (gta >> 1) & 1
        a1 = gta & 1
        m4 = last >> log2(fy)
        n4 = last & (fy - 1)
        p1 = m4.astype(jnp.float32) + z1
        p2 = n4.astype(jnp.float32) + z2
        rows = rows2(g) * 4 + 2 * a1
        for tile in range(4):
            a2, b1 = tile // 2, tile % 2
            for c in range(4):
                box = (2 * m4 + c // 2) * py + 2 * n4 + c % 2
                cycles = change4[gta * 4 + tile] * amp3[box] + lin3[2 * box + b1]
                put(cs4, ((i * 4 + c) * 4 + tile) * 2, cycles)
            col = (4 * (cols2 + t2) + 2 * a2 + upper).astype(jnp.float32) + 0.5
            r4 = (rows + b1).astype(jnp.float32) + 0.5
            put(cs5, (i * 4 + tile) * 2, speed4[gta * 4 + tile] * amp4[last] + (r4 * p1 + col * p2))
        return carry

    lax.fori_loop(0, groups * 4 * boxes, phases_four, 0)


def phase_side(nx, ny, piece_x, piece_y):
    px, py, fx, fy, wide, groups = group_bits(nx, ny, piece_x, piece_y)
    parents, boxes = px * py, fx * fy
    items = groups * parents
    return pl.pallas_call(
        functools.partial(phase_kernel, nx, ny, piece_x, piece_y),
        out_specs=[pl.BlockSpec(memory_space=pltpu.VMEM)] * 3,
        out_shape=[jax.ShapeDtypeStruct((64 * items, 8, 128), jnp.float32),
                   pltpu.VMEM((EARLY, 8, 128), jnp.float32),
                   pltpu.VMEM((8 * items, 8, 128), jnp.float32)],
        scratch_shapes=[
            tab(nx * ny), tab(2 * nx * ny), tab(parents), tab(2 * parents), tab(boxes),
            tab(groups * 4), tab(groups * 16), tab(groups * 16),
        ],
        name="phases",
        cost_estimate=pl.CostEstimate(flops=2 * 10**9, bytes_accessed=9 * 2**20, transcendentals=0),
    )()


def target_kernel(nx, ny, piece_x, piece_y, w_ref, mix_ref, early_ref, cs5, cs_hbm, out_hbm,
                  z3_ref, cs_ref, out_ref, in_sem, out_sem):
    px, py, fx, fy, wide, groups = group_bits(nx, ny, piece_x, piece_y)
    parents, boxes = px * py, fx * fy
    low_half = iotas()[0] < 64

    comes = ranges(cs_hbm, groups * parents)
    cs3, cs4 = kept = ranges(cs_ref, groups * parents)

    def coming(which, g):
        source, target = comes[which], kept[which]
        part = source.shape[0] // groups
        rows = pl.ds(g * part, part)
        return pltpu.make_async_copy(source.at[rows], target.at[rows], in_sem.at[which, g])

    for g in range(1, groups):
        coming(0, g).start()
    for g in range(groups):
        coming(1, g).start()
    head = 32 * parents
    if head > EARLY:
        rest = pl.ds(EARLY, head - EARLY)
        filling = pltpu.make_async_copy(comes[0].at[rest], cs3.at[rest], in_sem.at[0, 0])
        filling.start()

    def early(i, carry):
        cs3[pl.ds(i * 8, 8)] = early_ref[pl.ds(i * 8, 8)]
        return carry

    lax.fori_loop(0, EARLY // 8, early, 0)
    if head > EARLY:
        filling.wait()

    def await_next(per_group, unroll, parts):
        stepwise = unroll % per_group == 0
        for which in parts:
            for g in range(1 if stepwise else groups):
                if (which, g) != (0, 0):
                    coming(which, g).wait()
        if not stepwise:
            return None
        each = unroll // per_group

        def before(k):
            for n in range(1, each + 1):

                @pl.when(k * each + n < groups)
                def _():
                    for which in parts:
                        coming(which, k * each + n).wait()

        return before

    def arrived(box, g, part):
        if wide:
            at = (((g >> 1) * 2 + part) * 2 + (g & 1)) * 8
        else:
            at = (g * 2 + part) * 8
        return w_ref[box, pl.ds(pl.multiple_of(at, 8), 8), :]

    def produce_three(i):
        tiles = fresh(LOW[2])
        g = i >> log2(parents)
        parent = i & (parents - 1)
        m3 = parent >> log2(py)
        n3 = parent & (py - 1)
        for c in range(4):
            box = (2 * m3 + c // 2) * ny + 2 * n3 + c % 2
            reals = doubled(arrived(box, g, 0), low_half)
            imags = doubled(arrived(box, g, 1), low_half)
            for ta in range(4):
                at = ((i * 4 + c) * 4 + ta) * 2
                turn_back(reals[ta // 2], imags[ta // 2], cs3[at], cs3[at + 1], tiles, ta, c, LOW[2])
        return laid(tiles)

    def consume_three(i, y):
        z3_ref[pl.ds(pl.multiple_of(i * 64, 64), 64), :] = y

    staged(groups * parents, produce_three, consume_three, mix_ref, LOW[2], UNROLL[2],
           await_next(parents, UNROLL[2], (0,)))

    def decode(i):
        last = i & (boxes - 1)
        gta = i >> log2(boxes)
        return gta >> 2, gta & 3, last

    def produce_four(i):
        tiles = fresh(LOW[3])
        g, ta, last = decode(i)
        m4 = last >> log2(fy)
        n4 = last & (fy - 1)
        for c in range(4):
            box = (2 * m4 + c // 2) * py + 2 * n4 + c % 2
            source = pl.multiple_of(((g * parents + box) * 4 + ta) * 16, 16)
            reals = doubled(z3_ref[pl.ds(source, 8), :], low_half)
            imags = doubled(z3_ref[pl.ds(source + 8, 8), :], low_half)
            for tile in range(4):
                at = ((i * 4 + c) * 4 + tile) * 2
                turn_back(reals[tile // 2], imags[tile // 2], cs4[at], cs4[at + 1], tiles, tile, c, LOW[3])
        return laid(tiles)

    def consume_four(i, y):
        g, ta, last = decode(i)
        t2 = ta >> 1
        a1 = ta & 1
        gx = g >> 1 if wide else g
        for a2 in range(2):
            for b1 in range(2):
                tile = a2 * 2 + b1
                real = y[tile * 16:tile * 16 + 8]
                imag = y[tile * 16 + 8:tile * 16 + 16]
                c, s = cs5[(i * 4 + tile) * 2], cs5[(i * 4 + tile) * 2 + 1]
                ore = real * c - imag * s
                oim = real * s + imag * c
                pair = (
                    jnp.where(low_half, ore, pltpu.roll(oim, 64, 1)),
                    jnp.where(low_half, pltpu.roll(ore, 64, 1), oim),
                )
                for b2, value in enumerate(pair):
                    inner = (4 * t2 + 2 * a2 + b2) * boxes + last

                    def at(h):
                        line = (h * piece_x + gx) * 4 + 2 * a1 + b1
                        return line * (piece_y * 8 * boxes) + inner

                    if wide:
                        out_ref[pl.ds(at(g & 1), 8, stride=8 * boxes), :] = value
                    else:
                        for h in range(2):
                            out_ref[pl.ds(at(h), 4, stride=8 * boxes), :] = value[4 * h:4 * h + 4]

    early = wide and 4 * boxes == 8
    size = 4 * piece_y * 8 * boxes if early else out_hbm.shape[0]

    def leaving(k):
        if early:
            k = (k & 1) * piece_x + (k >> 1)
        rows = pl.ds(pl.multiple_of(k * size, size), size)
        return pltpu.make_async_copy(out_ref.at[rows], out_hbm.at[rows], out_sem.at[k])

    staged(groups * 4 * boxes, produce_four, consume_four, mix_ref, LOW[3], UNROLL[3],
           await_next(4 * boxes, UNROLL[3], (1,)), (lambda k: leaving(k).start()) if early else None)
    if not early:
        leaving(0).start()
    for k in range(groups if early else 1):
        leaving(k).wait()


def target_side(arrived, mix, phases, nx, ny, piece_x, piece_y):
    parents, boxes = (nx // 2) * (ny // 2), (nx // 4) * (ny // 4)
    groups = piece_x * (2 if piece_y == 8 else 1)
    return pl.pallas_call(
        functools.partial(target_kernel, nx, ny, piece_x, piece_y),
        in_specs=[pl.BlockSpec(memory_space=pltpu.VMEM)] * 4 + [pl.BlockSpec(memory_space=pltpu.HBM)],
        out_specs=pl.BlockSpec(memory_space=pltpu.HBM),
        out_shape=jax.ShapeDtypeStruct((2 * 4 * piece_x * 2 * 4 * piece_y * boxes, 128), jnp.float32),
        scratch_shapes=[
            pltpu.VMEM((groups * parents * 64, 128), jnp.float32),
            pltpu.VMEM(phases[0].shape, jnp.float32),
            pltpu.VMEM(((64 * piece_x * piece_y + 64) * boxes, 128), jnp.float32),
            pltpu.SemaphoreType.DMA((2, groups)),
            pltpu.SemaphoreType.DMA((groups,)),
        ],
        compiler_params=pltpu.CompilerParams(vmem_limit_bytes=48 * 2**20),
        name="target_levels",
        cost_estimate=pl.CostEstimate(flops=2 * 10**9, bytes_accessed=2 * 2**20, transcendentals=0),
    )(arrived, mix, phases[1], phases[2], phases[0])


def to_targets(made, nx, ny, piece_x, piece_y):
    if (piece_x, piece_y) != (2, 8):
        made = made.reshape(4, 2, 4, 2, 2, 4, 2, 2, 128)
        lead = [0, 1] + ([3] if piece_x == 1 else []) + [2] + ([6] if piece_y == 4 else [])
        rest = ([3] if piece_x == 2 else []) + [4, 5] + ([6] if piece_y == 8 else []) + [7]
        made = made.transpose(lead + rest + [8])
    return made.reshape(nx * ny, -1, 128)


def on_device(weights):
    nx = lax.axis_size("sx")
    ny = lax.axis_size("sy")
    piece_x = 2 * weights.shape[0] // nx
    piece_y = 2 * weights.shape[1] // ny
    mix = jnp.asarray(mixing())
    made = to_targets(source_side(weights, mix), nx, ny, piece_x, piece_y)
    arrived = lax.all_to_all(made, ("sx", "sy"), split_axis=0, concat_axis=0, tiled=True)
    phases = phase_side(nx, ny, piece_x, piece_y)
    out = target_side(arrived, mix, phases, nx, ny, piece_x, piece_y)
    return out.reshape(2, 4 * piece_x, 2, 4 * piece_y, nx // 4, ny // 4, 128)


def solution(mesh):
    return jax.shard_map(
        on_device,
        mesh=mesh,
        in_specs=(P(None, None, "sx", "sy", None),),
        out_specs=P(None, "sx", None, "sy", None, None, None),
        check_vma=False,
    )
```
